32 devices in a mesh: dp: 8 (over z, x), tensor: 4 (over y, core).
Axes of the slice: x: 2, y: 2, z: 4, core: 2. Of those that a mesh axis runs over, the one named last changes fastest.
Arguments:
- hidden_in: bfloat16 [16384, 768], P(('dp', 'tensor')), may hold values from -6 to 6
- seq_lengths: int32 [32], P('dp'), may hold values from 128 to 512, as said below
- w_query: bfloat16 [768, 768], P('dp', 'tensor'), may hold values from -0.3125 to 0.3125
- b_query: float32 [768], replicated, may hold values from -3 to 3
- w_key: bfloat16 [768, 768], P('dp', 'tensor'), may hold values from -0.3125 to 0.3125
- w_value: bfloat16 [768, 768], P('dp', 'tensor'), may hold values from -0.21875 to 0.21875
- b_value: float32 [768], replicated, may hold values from -2 to 2
- w_out: bfloat16 [768, 768], P('dp', 'tensor'), may hold values from -1.25 to 1.25
- b_out: float32 [768], replicated, may hold values from -2 to 2
- norm1_gain: float32 [768], replicated, may hold values from 0.5 to 1.5
- norm1_bias: float32 [768], replicated, may hold values from -2 to 2
- w_inner: bfloat16 [768, 3072], P('dp', 'tensor'), may hold values from -0.21875 to 0.21875
- b_inner: float32 [3072], replicated, may hold values from -3 to 3
- w_outer: bfloat16 [768, 3072], P('dp', 'tensor'), may hold values from -0.109375 to 0.109375
- b_outer: float32 [768], replicated, may hold values from -2 to 2
- norm2_gain: float32 [768], replicated, may hold values from 0.5 to 1.5
- norm2_bias: float32 [768], replicated, may hold values from -2 to 2
- out_grad: bfloat16 [16384, 768], P(('dp', 'tensor')), may hold values from -6 to 6
Outputs:
- layer_out: bfloat16 [16384, 768], P(('dp', 'tensor'))
- grad_in: float32 [16384, 768], P(('dp', 'tensor'))
- grad_w_query: float32 [768, 768], P('dp', 'tensor')
- grad_b_query: float32 [768], replicated
- grad_w_key: float32 [768, 768], P('dp', 'tensor')
- grad_w_value: float32 [768, 768], P('dp', 'tensor')
- grad_b_value: float32 [768], replicated
- grad_w_out: float32 [768, 768], P('dp', 'tensor')
- grad_b_out: float32 [768], replicated
- grad_norm1_gain: float32 [768], replicated
- grad_norm1_bias: float32 [768], replicated
- grad_w_inner: float32 [768, 3072], P('dp', 'tensor')
- grad_b_inner: float32 [3072], replicated
- grad_w_outer: float32 [768, 3072], P('dp', 'tensor')
- grad_b_outer: float32 [768], replicated
- grad_norm2_gain: float32 [768], replicated
- grad_norm2_bias: float32 [768], replicated
The draws below stay inside these ranges and needn't reach their ends.
Inputs may be any that keep to these rules, and one draw needn't show every extreme that they name: `seq_lengths`: every sequence has at least 128 valid slots, and one has exactly that many; one sequence is full in every draw.
All inputs are finite; a program needn't handle non-finite values.
Results may differ from the reference program's by a relative error of at most 0.019.
The reference program's roundings to bfloat16 on the way count: a program that leaves them out, or rounds other values in their place, can miss the bound.
Values may be sent and summed in bfloat16 or wider, within the bound.
A program may use at most 128 MiB of HBM per device.

```python
import jax
import jax.numpy as jnp
from jax import lax

D = 768
HEADS = 12
FF = 3072
SEQ = 512
HEAD_DIM = 64
ROWS_BLOCK = 512
SEQUENCES = 32
TOKENS = 16384


def draw_seq_lengths(key, part):
    first_key, second_key = jax.random.split(key)
    lengths = jax.random.randint(first_key, (SEQUENCES,), SEQ // 4, SEQ + 1)
    order = jax.random.permutation(second_key, SEQUENCES)
    lengths = lengths.at[order[0]].set(SEQ)
    lengths = lengths.at[order[1]].set(SEQ // 4)
    return lengths.astype(jnp.int32)


def with_spikes(entries, rng, source, target, blocks, factor):
    def block_of(position):
        return (jnp.arange(entries.shape[position]) // (entries.shape[position] // blocks)).reshape((-1,) + (1,) * (entries.ndim - 1 - position))

    first = jax.random.permutation(rng, blocks)[block_of(target)]
    far = (block_of(target) + blocks // 2) % blocks
    return jnp.where((block_of(source) == first) | (block_of(source) == far), factor * entries, entries)


def levels(stream_key, dims, shards, low, high):
    loudness = 1.0
    for dim, blocks in shards:
        draws = jax.random.uniform(jax.random.fold_in(jax.random.fold_in(stream_key, 6), dim), (blocks,), jnp.float32, low / len(shards), high / len(shards))
        loudness = loudness * jnp.repeat(jnp.exp(draws), dims[dim] // blocks).reshape((-1,) + (1,) * (len(dims) - 1 - dim))
    return loudness


def gaussian(own_key, dims, scale, reach, pieces=(), kind=jnp.bfloat16):
    level = levels(own_key, dims, pieces, -0.22, 0.18) if pieces else 1.0
    drawn = jax.random.normal(own_key, dims, jnp.float32) * scale * level
    return jnp.minimum(jnp.maximum(drawn, -reach), reach).astype(kind)


def noise_with(key, extent, width, bound, cuts, heavy, kind=jnp.bfloat16):
    drawn = width * jax.random.normal(key, extent, jnp.float32)
    if cuts:
        drawn = drawn * levels(key, extent, cuts, -0.22, 0.18)
    return jnp.clip(with_spikes(drawn, jax.random.fold_in(key, 3), *heavy), -bound, bound).astype(kind)


def setup_inputs(seed: int = 0) -> dict:
    arg_keys = jax.random.split(jax.random.key(seed), 19)
    hidden_in = noise_with(arg_keys[0], (TOKENS, D), 1.0, 6.0, ((0, 32),), (0, 1, 32, 2.75))
    seq_lengths = draw_seq_lengths(jax.random.fold_in(arg_keys[18], 71), 0)
    w_query = gaussian(arg_keys[2], (D, D), (D // 2) ** -0.5, 0.3125, ((0, 8), (1, 4)))
    b_query = gaussian(arg_keys[3], (D,), 0.5, 3.0, (), jnp.float32)
    w_key = gaussian(arg_keys[4], (D, D), (D // 2) ** -0.5, 0.3125, ((0, 8), (1, 4)))
    w_value = gaussian(arg_keys[5], (D, D), D ** -0.5, 0.21875, ((0, 8), (1, 4)))
    b_value = gaussian(arg_keys[6], (D,), 0.3, 2.0, (), jnp.float32)
    w_out = gaussian(arg_keys[7], (D, D), (D // 32) ** -0.5, 1.25, ((0, 8), (1, 4)))
    b_out = gaussian(arg_keys[8], (D,), 0.3, 2.0, (), jnp.float32)
    norm1_gain = jnp.clip(1.0 + 0.1 * jax.random.normal(arg_keys[9], (D,), jnp.float32), 0.5, 1.5)
    norm1_bias = gaussian(arg_keys[10], (D,), 0.3, 2.0, (), jnp.float32)
    w_inner = gaussian(arg_keys[11], (D, FF), D ** -0.5, 0.21875, ((0, 8), (1, 4)))
    b_inner = gaussian(arg_keys[12], (FF,), 0.5, 3.0, (), jnp.float32)
    w_outer = gaussian(arg_keys[13], (D, FF), FF ** -0.5, 0.109375, ((0, 8), (1, 4)))
    b_outer = gaussian(arg_keys[14], (D,), 0.3, 2.0, (), jnp.float32)
    norm2_gain = jnp.clip(1.0 + 0.1 * jax.random.normal(arg_keys[15], (D,), jnp.float32), 0.5, 1.5)
    norm2_bias = gaussian(arg_keys[16], (D,), 0.3, 2.0, (), jnp.float32)
    out_grad = noise_with(arg_keys[17], (TOKENS, D), 1.0, 6.0, ((0, 32),), (0, 1, 32, 2.75))
    return {"hidden_in": hidden_in, "seq_lengths": seq_lengths, "w_query": w_query, "b_query": b_query, "w_key": w_key, "w_value": w_value, "b_value": b_value, "w_out": w_out, "b_out": b_out, "norm1_gain": norm1_gain, "norm1_bias": norm1_bias, "w_inner": w_inner, "b_inner": b_inner, "w_outer": w_outer, "b_outer": b_outer, "norm2_gain": norm2_gain, "norm2_bias": norm2_bias, "out_grad": out_grad}


@jax.custom_vjp
def low(v):
    return lax.optimization_barrier(v.astype(jnp.bfloat16)).astype(jnp.float32)

@jax.custom_vjp
def low_back(v):
    return v

def low_keep(v):
    return (low(v), None)

def low_pass(kept, grad):
    return (grad,)

def back_keep(v):
    return (v, None)

def back_low(kept, grad):
    return (low(grad),)
low.defvjp(low_keep, low_pass)
low_back.defvjp(back_keep, back_low)
NEG_FILL = -1000000000.0
NORM_EPS = 1e-12

def exact_dot(first_op, second_op):
    return jnp.dot(first_op, second_op, precision=lax.Precision.HIGHEST, preferred_element_type=jnp.float32)

def exact_last(first_op, second_op):
    return lax.dot_general(first_op, second_op, (((1,), (1,)), ((), ())), precision=lax.Precision.HIGHEST, preferred_element_type=jnp.float32)

def layer_norm(residual, norm_gain, norm_bias):
    centre = residual - lax.optimization_barrier(jnp.mean(residual, axis=-1, keepdims=True))
    spread = lax.optimization_barrier(jnp.mean(centre * centre, axis=-1, keepdims=True))
    return centre * lax.rsqrt(spread + NORM_EPS) * norm_gain + norm_bias

def sequence_layer(seq_rows, length, weights):
    w_query, b_query, w_key, w_value, b_value, w_out, b_out, gain_one, bias_one, w_inner, b_inner, w_outer, b_outer, gain_two, bias_two = weights
    places = jnp.arange(SEQ, dtype=jnp.int32)
    valid = places < length
    queries = low(low_back(exact_dot(seq_rows, w_query) + b_query))
    key_rows = low(low_back(exact_dot(seq_rows, w_key)))
    values = low(low_back(exact_dot(seq_rows, w_value) + b_value))

    def heads_of(matrix):
        return matrix.reshape(SEQ, HEADS, HEAD_DIM).transpose(1, 0, 2)
    query_heads = heads_of(queries)
    key_head_tensor = heads_of(key_rows)
    value_head_tensor = heads_of(values)
    blocks = query_heads.reshape(HEADS, SEQ // ROWS_BLOCK, ROWS_BLOCK, HEAD_DIM).transpose(1, 0, 2, 3)
    score_scale = HEAD_DIM ** (-0.5)

    @jax.checkpoint
    def one_block(query_portion):
        scores = jnp.einsum('hqd,hkd->hqk', query_portion, key_head_tensor, precision=lax.Precision.HIGHEST) * score_scale
        scores = low_back(scores)
        scores = jnp.where(valid[None, None, :], scores, NEG_FILL)
        row_max = lax.optimization_barrier(jnp.max(scores, axis=-1, keepdims=True))
        exponent = jnp.exp(scores - row_max)
        row_total = lax.optimization_barrier(jnp.sum(exponent, axis=-1, keepdims=True))
        softmax = low(exponent / row_total)
        return jnp.einsum('hqk,hkd->hqd', softmax, value_head_tensor, precision=lax.Precision.HIGHEST)
    mixture = lax.map(one_block, blocks)
    mixture = mixture.transpose(0, 2, 1, 3).reshape(SEQ, D)
    mixture = low(low_back(mixture))
    attn_out = low_back(exact_last(mixture, w_out) + b_out)
    first_norm = layer_norm(seq_rows + attn_out, gain_one, bias_one)
    pre_act = low_back(exact_dot(low(first_norm), w_inner) + b_inner)
    act_low = low(jax.nn.gelu(pre_act, approximate=False))
    ffn_out = low_back(exact_last(act_low, w_outer) + b_outer)
    second = layer_norm(first_norm + ffn_out, gain_two, bias_two)
    return second * valid[:, None].astype(jnp.float32)

def reference(hidden_in, seq_lengths, w_query, b_query, w_key, w_value, b_value, w_out, b_out, norm1_gain, norm1_bias, w_inner, b_inner, w_outer, b_outer, norm2_gain, norm2_bias, out_grad):
    weights = tuple((item.astype(jnp.float32) for item in (w_query, b_query, w_key, w_value, b_value, w_out, b_out, norm1_gain, norm1_bias, w_inner, b_inner, w_outer, b_outer, norm2_gain, norm2_bias)))
    inputs = hidden_in.astype(jnp.float32)

    def forward(inputs, weights):
        seq_all = inputs.reshape(SEQUENCES, SEQ, D)

        def one_step(running, seq_item):
            return (running, sequence_layer(seq_item[0], seq_item[1], weights))
        _, outputs = lax.scan(one_step, jnp.zeros((), jnp.float32), (seq_all, seq_lengths))
        return outputs.reshape(TOKENS, D)
    result, backward = jax.vjp(forward, inputs, weights)
    input_grad, weight_grads = backward(out_grad.astype(jnp.float32))
    return (result.astype(jnp.bfloat16), input_grad, weight_grads[0], weight_grads[1], weight_grads[2], weight_grads[3], weight_grads[4], weight_grads[5], weight_grads[6], weight_grads[7], weight_grads[8], weight_grads[9], weight_grads[10], weight_grads[11], weight_grads[12], weight_grads[13], weight_grads[14])
```

```python
import functools

import jax
import jax.numpy as jnp
from jax import lax
from jax.experimental import pallas as pl
from jax.experimental.pallas import tpu as pltpu
from jax.sharding import PartitionSpec as P

HEAD_DIM = 64


NEG_FILL = -1000000000.0
NORM_EPS = 1e-12


def layer_norm(residual, norm_gain, norm_bias):
    centre = residual - jnp.mean(residual, axis=-1, keepdims=True)
    spread = jnp.mean(centre * centre, axis=-1, keepdims=True)
    return centre * lax.rsqrt(spread + NORM_EPS) * norm_gain + norm_bias


def exact_gelu(values):
    return jax.nn.gelu(values, approximate=False)


def contract_last(first_op, second_op):
    return lax.dot_general(
        first_op, second_op, (((1,), (1,)), ((), ())), preferred_element_type=jnp.float32
    )


def contract_first(first_op, second_op):
    return lax.dot_general(
        first_op, second_op, (((0,), (0,)), ((), ())), preferred_element_type=jnp.float32
    )


def split_blocks(heads_arr, block_rows):
    batches, length, head_size = heads_arr.shape
    return heads_arr.reshape(batches, length // block_rows, block_rows, head_size).transpose(
        1, 0, 2, 3
    )


def join_blocks(block_array):
    block_count, batches, block_rows, head_size = block_array.shape
    return block_array.transpose(1, 0, 2, 3).reshape(batches, block_count * block_rows, head_size)


def block_scores(query_portion, key_head_tensor, key_valid, score_scale):
    scores = (
        jnp.einsum(
            "eix,evx->eiv", query_portion, key_head_tensor, preferred_element_type=jnp.float32
        )
        * score_scale
    )
    return jnp.where(key_valid[:, None, :], scores, NEG_FILL)


def attend(query_heads, key_head_tensor, value_head_tensor, key_valid, block_rows, score_scale):

    def one_block(query_portion):
        scores = block_scores(query_portion, key_head_tensor, key_valid, score_scale)
        row_max = jnp.max(scores, axis=-1, keepdims=True)
        exponent = jnp.exp(scores - row_max)
        row_total = jnp.sum(exponent, axis=-1, keepdims=True)
        softmax_reduced = (exponent / row_total).astype(jnp.bfloat16)
        mixture = jnp.einsum(
            "fwj,fjt->fwt", softmax_reduced, value_head_tensor, preferred_element_type=jnp.float32
        )
        return (mixture.astype(jnp.bfloat16), row_max, row_total)

    mixture, row_max, row_total = lax.map(one_block, split_blocks(query_heads, block_rows))
    return (join_blocks(mixture), row_max, row_total)


def attend_back(
    query_heads,
    key_head_tensor,
    value_head_tensor,
    grad_heads,
    row_max,
    row_total,
    key_valid,
    block_rows,
    score_scale,
):

    def one_block(running, block_in):
        key_grad, value_grad = running
        query_portion, gradient_portion, max_part, total_part = block_in
        scores = block_scores(query_portion, key_head_tensor, key_valid, score_scale)
        softmax = jnp.exp(scores - max_part) / total_part
        softmax_reduced = softmax.astype(jnp.bfloat16)
        soft_grad = jnp.einsum(
            "eix,evx->eiv", gradient_portion, value_head_tensor, preferred_element_type=jnp.float32
        )
        centre = jnp.sum(softmax * soft_grad, axis=-1, keepdims=True)
        score_gradient = (softmax * (soft_grad - centre)).astype(jnp.bfloat16)
        query_grad = (
            jnp.einsum(
                "fwj,fjt->fwt", score_gradient, key_head_tensor, preferred_element_type=jnp.float32
            )
            * score_scale
        )
        key_grad = (
            key_grad
            + jnp.einsum(
                "oxl,oxn->oln", score_gradient, query_portion, preferred_element_type=jnp.float32
            )
            * score_scale
        )
        value_grad = value_grad + jnp.einsum(
            "oxl,oxn->oln", softmax_reduced, gradient_portion, preferred_element_type=jnp.float32
        )
        return ((key_grad, value_grad), query_grad)

    zero_grads = jnp.zeros(key_head_tensor.shape, jnp.float32)
    block_inputs = (
        split_blocks(query_heads, block_rows),
        split_blocks(grad_heads, block_rows),
        row_max,
        row_total,
    )
    (key_grad, value_grad), query_grad = lax.scan(one_block, (zero_grads, zero_grads), block_inputs)
    return (join_blocks(query_grad), key_grad, value_grad)


def per_device(
    hidden_in,
    seq_lengths,
    w_query,
    b_query,
    w_key,
    w_value,
    b_value,
    w_out,
    b_out,
    norm1_gain,
    norm1_bias,
    w_inner,
    b_inner,
    w_outer,
    b_outer,
    norm2_gain,
    norm2_bias,
    out_grad,
):
    tensor_size = lax.axis_size("tensor")
    tensor_place = lax.axis_index("tensor")
    local_rows, feature_width = hidden_in.shape
    group_rows = local_rows * tensor_size
    seq_count = seq_lengths.shape[0]
    seq_len = group_rows // seq_count
    head_cols = w_query.shape[1]
    inner_cols = w_inner.shape[1]
    heads_here = head_cols // HEAD_DIM
    block_rows = min(512, seq_len)
    score_scale = HEAD_DIM ** (-0.5)
    local_start = tensor_place * local_rows
    row_index = lax.iota(jnp.int32, group_rows)
    seq_match = (row_index[:, None] // seq_len == lax.iota(jnp.int32, seq_count)[None, :]).astype(
        jnp.int32
    )
    row_limit = jnp.sum(seq_match * seq_lengths[None, :], axis=1)
    row_valid = row_index % seq_len < row_limit
    local_mask = lax.dynamic_slice_in_dim(row_valid, local_start, local_rows).astype(jnp.float32)[
        :, None
    ]
    key_valid = jnp.repeat(row_valid.reshape(seq_count, seq_len), heads_here, axis=0)

    def heads_of(matrix):
        shaped = matrix.reshape(seq_count, seq_len, heads_here, HEAD_DIM).transpose(0, 2, 1, 3)
        return shaped.reshape(seq_count * heads_here, seq_len, HEAD_DIM)

    def rows_of(matrix):
        shaped = matrix.reshape(seq_count, heads_here, seq_len, HEAD_DIM).transpose(0, 2, 1, 3)
        return shaped.reshape(group_rows, head_cols)

    full_query, full_key, full_value, full_out, full_inner, full_outer = (
        lax.all_gather(w_query, "dp", axis=0, tiled=True),
        lax.all_gather(w_key, "dp", axis=0, tiled=True),
        lax.all_gather(w_value, "dp", axis=0, tiled=True),
        lax.all_gather(w_out, "dp", axis=0, tiled=True),
        lax.all_gather(w_inner, "dp", axis=0, tiled=True),
        lax.all_gather(w_outer, "dp", axis=0, tiled=True),
    )
    joint_weight = jnp.concatenate((full_query, full_key, full_value), axis=1)
    query_bias = lax.dynamic_slice_in_dim(b_query, tensor_place * head_cols, head_cols)
    value_bias = lax.dynamic_slice_in_dim(b_value, tensor_place * head_cols, head_cols)
    inner_bias = lax.dynamic_slice_in_dim(b_inner, tensor_place * inner_cols, inner_cols)
    joint_bias = jnp.concatenate((query_bias, jnp.zeros((head_cols,), jnp.float32), value_bias))
    whole_in = lax.all_gather(hidden_in, "tensor", axis=0, tiled=True)
    joint_rows = (
        jnp.dot(whole_in, joint_weight, preferred_element_type=jnp.float32) + joint_bias
    ).astype(jnp.bfloat16)
    query_heads = heads_of(joint_rows[:, :head_cols])
    key_head_tensor = heads_of(joint_rows[:, head_cols : 2 * head_cols])
    value_head_tensor = heads_of(joint_rows[:, 2 * head_cols :])
    mixture_heads, row_max, row_total = attend(
        query_heads, key_head_tensor, value_head_tensor, key_valid, block_rows, score_scale
    )
    mixture = rows_of(mixture_heads)
    summed_out = lax.psum_scatter(
        contract_last(mixture, full_out).astype(jnp.bfloat16),
        "tensor",
        scatter_dimension=0,
        tiled=True,
    ).astype(jnp.float32)
    first_sum = hidden_in.astype(jnp.float32) + (summed_out + b_out)
    first_norm = layer_norm(first_sum, norm1_gain, norm1_bias)
    mid_whole = lax.all_gather(first_norm.astype(jnp.bfloat16), "tensor", axis=0, tiled=True)
    pre_act = jnp.dot(mid_whole, full_inner, preferred_element_type=jnp.float32) + inner_bias
    act_low = exact_gelu(pre_act).astype(jnp.bfloat16)
    second_sum = first_norm + (
        lax.psum_scatter(
            contract_last(act_low, full_outer).astype(jnp.bfloat16),
            "tensor",
            scatter_dimension=0,
            tiled=True,
        ).astype(jnp.float32)
        + b_outer
    )
    normed, norm2_back = jax.vjp(layer_norm, second_sum, norm2_gain, norm2_bias)
    layer_out = (normed * local_mask).astype(jnp.bfloat16)
    out_cot = out_grad.astype(jnp.float32) * local_mask
    dsecond, gain2_part, bias2_part = norm2_back(out_cot)
    dffn_low = dsecond.astype(jnp.bfloat16)
    outer_bias_part = jnp.sum(dffn_low, axis=0, dtype=jnp.float32)
    dffn_whole = lax.all_gather(dffn_low, "tensor", axis=0, tiled=True)
    grad_outer = contract_first(dffn_whole, act_low)
    dact = jnp.dot(dffn_whole, full_outer, preferred_element_type=jnp.float32)
    _, gelu_back = jax.vjp(exact_gelu, pre_act)
    dpre_low = gelu_back(dact)[0].astype(jnp.bfloat16)
    inner_bias_part = jnp.sum(dpre_low, axis=0, dtype=jnp.float32)
    grad_inner = contract_first(mid_whole, dpre_low)
    dfirst_norm = dsecond + lax.psum_scatter(
        contract_last(dpre_low, full_inner).astype(jnp.bfloat16),
        "tensor",
        scatter_dimension=0,
        tiled=True,
    ).astype(jnp.float32)
    _, norm1_back = jax.vjp(layer_norm, first_sum, norm1_gain, norm1_bias)
    dfirst, gain1_part, bias1_part = norm1_back(dfirst_norm)
    dattn_low = dfirst.astype(jnp.bfloat16)
    out_bias_part = jnp.sum(dattn_low, axis=0, dtype=jnp.float32)
    dattn_whole = lax.all_gather(dattn_low, "tensor", axis=0, tiled=True)
    grad_out_w = contract_first(dattn_whole, mixture)
    dmixture = jnp.dot(dattn_whole, full_out, preferred_element_type=jnp.float32).astype(
        jnp.bfloat16
    )
    dquery_heads, dkey_heads, dvalue_heads = attend_back(
        query_heads,
        key_head_tensor,
        value_head_tensor,
        heads_of(dmixture),
        row_max,
        row_total,
        key_valid,
        block_rows,
        score_scale,
    )
    djoint = jnp.concatenate(
        (rows_of(dquery_heads), rows_of(dkey_heads), rows_of(dvalue_heads)), axis=1
    ).astype(jnp.bfloat16)
    joint_bias_part = jnp.sum(djoint, axis=0, dtype=jnp.float32)
    grad_joint = contract_first(whole_in, djoint)
    grad_in = dfirst + lax.psum_scatter(
        contract_last(djoint, joint_weight).astype(jnp.bfloat16),
        "tensor",
        scatter_dimension=0,
        tiled=True,
    ).astype(jnp.float32)
    grad_query = grad_joint[:, :head_cols]
    grad_key = grad_joint[:, head_cols : 2 * head_cols]
    grad_value = grad_joint[:, 2 * head_cols :]
    shard_grads = tuple(
        (
            lax.psum_scatter(grad_query, "dp", scatter_dimension=0, tiled=True),
            lax.psum_scatter(grad_key, "dp", scatter_dimension=0, tiled=True),
            lax.psum_scatter(grad_value, "dp", scatter_dimension=0, tiled=True),
            lax.psum_scatter(grad_out_w, "dp", scatter_dimension=0, tiled=True),
            lax.psum_scatter(grad_inner, "dp", scatter_dimension=0, tiled=True),
            lax.psum_scatter(grad_outer, "dp", scatter_dimension=0, tiled=True),
        )
    )

    def placed(vector, total_len):
        return lax.dynamic_update_slice_in_dim(
            jnp.zeros((total_len,), jnp.float32), vector, tensor_place * vector.shape[0], 0
        )

    query_bias_part = placed(joint_bias_part[:head_cols], feature_width)
    value_bias_part = placed(joint_bias_part[2 * head_cols :], feature_width)
    hidden_bias_part = placed(inner_bias_part, b_inner.shape[0])
    vector_sums = lax.psum(
        (
            query_bias_part,
            value_bias_part,
            out_bias_part,
            gain1_part,
            bias1_part,
            hidden_bias_part,
            outer_bias_part,
            gain2_part,
            bias2_part,
        ),
        ("dp", "tensor"),
    )
    return (
        layer_out,
        grad_in,
        shard_grads[0],
        vector_sums[0],
        shard_grads[1],
        shard_grads[2],
        vector_sums[1],
        shard_grads[3],
        vector_sums[2],
        vector_sums[3],
        vector_sums[4],
        shard_grads[4],
        vector_sums[5],
        shard_grads[5],
        vector_sums[6],
        vector_sums[7],
        vector_sums[8],
    )


Z_SIZE = 4
MESH_IDS = pl.DeviceIdType.MESH


def flip(place, bit):
    return place + bit - 2 * place * bit


class Place:
    def __init__(self):
        self.dp = lax.axis_index("dp")
        self.t = lax.axis_index("tensor")
        self.z = self.dp // 2
        self.x = self.dp % 2
        self.y = self.t // 2
        self.c = self.t % 2

    def chip(self, dz, da, db):
        c = self.c
        z = lax.rem(self.z - dz + Z_SIZE, Z_SIZE)
        x = flip(self.x, da * c + db * (1 - c))
        y = flip(self.y, da * (1 - c) + db * c)
        return z * 2 + x, y

    def device(self, dz=0, da=0, db=0, other=False):
        dp, y = self.chip(dz, da, db)
        core = 1 - self.c if other else self.c
        return {"dp": dp, "tensor": y * 2 + core}


def block_of(ref, m, dp, t, rows):
    return ref.at[m, t, pl.ds(pl.multiple_of(dp * rows, rows), rows), :]


def meet(me):
    barrier = pltpu.get_barrier_semaphore()
    peers = [me.device(dz=k) for k in range(1, Z_SIZE)]
    peers += [me.device(da=1), me.device(db=1), me.device(other=True)]
    for peer in peers:
        pl.semaphore_signal(barrier, inc=1, device_id=peer, device_id_type=MESH_IDS)
    pl.semaphore_wait(barrier, len(peers))


def remote(src, dst, send, recv, peer):
    return pltpu.make_async_remote_copy(
        src_ref=src, dst_ref=dst, send_sem=send, recv_sem=recv, device_id=peer, device_id_type=MESH_IDS
    )


def gather_kernel(p_ref, i_ref, o_ref, g_ref, send_sem, recv_sem, local_sem):
    me = Place()
    rows = p_ref.shape[0]
    c = me.c
    shards = (p_ref, i_ref, o_ref)

    def send(m, slot, src, chip, core, peer):
        dst = block_of(g_ref, m, chip[0], chip[1] * 2 + core, rows)
        remote(src, dst, send_sem.at[m, slot], recv_sem.at[m, slot], peer).start()

    def own(m, slot, peer):
        send(m, slot, shards[m], me.chip(0, 0, 0), c, peer)

    def forward(m, slot, dz, da, db, peer):
        chip = me.chip(dz, da, db)
        send(m, slot, block_of(g_ref, m, chip[0], chip[1] * 2 + c, rows), chip, c, peer)

    def arrived(m, slot):
        any_block = block_of(g_ref, m, 0, 0, rows)
        remote(any_block, any_block, send_sem.at[m, slot], recv_sem.at[m, slot], me.device(db=1)).wait_recv()

    def left(m, slot):
        any_block = block_of(g_ref, m, 0, 0, rows)
        remote(any_block, any_block, send_sem.at[m, slot], recv_sem.at[m, slot], me.device(db=1)).wait_send()

    meet(me)
    copies = []
    for m in range(3):
        for k in range(1, Z_SIZE):
            own(m, k, me.device(dz=Z_SIZE - k))
        own(m, 4, me.device(da=1))
        own(m, 8, me.device(db=1))
        own(m, 16, me.device(other=True))
        copy = pltpu.make_async_copy(shards[m], block_of(g_ref, m, me.dp, me.t, rows), local_sem.at[m])
        copy.start()
        copies.append(copy)
    for m in range(3):

        @pl.loop(1, Z_SIZE)
        def _(k):
            arrived(m, k)
            forward(m, 4 + k, k, 0, 0, me.device(da=1))
            forward(m, 8 + 2 * k, k, 0, 0, me.device(db=1))
            forward(m, 16 + 4 * k, k, 0, 0, me.device(other=True))

        @pl.loop(0, Z_SIZE)
        def _(k):
            arrived(m, 4 + k)
            forward(m, 9 + 2 * k, k, 1, 0, me.device(db=1))
            forward(m, 18 + 4 * k, k, 1, 0, me.device(other=True))

        @pl.loop(0, 2 * Z_SIZE)
        def _(s):
            arrived(m, 8 + s)
            forward(m, 17 + 2 * s, s // 2, s % 2, 1, me.device(other=True))

    for m in range(3):
        copies[m].wait()

        @pl.loop(16, 32)
        def _(s):
            arrived(m, s)

        @pl.loop(1, 32)
        def _(s):
            left(m, s)


def gather_all(packed, inner, outer, n_dp, n_t):
    rows, width = packed.shape
    return pl.pallas_call(
        gather_kernel,
        out_shape=jax.ShapeDtypeStruct((3, n_t, n_dp * rows, width), jnp.bfloat16),
        in_specs=[pl.BlockSpec(memory_space=pltpu.VMEM)] * 3,
        out_specs=pl.BlockSpec(memory_space=pltpu.VMEM),
        scratch_shapes=[
            pltpu.SemaphoreType.DMA((3, 32)),
            pltpu.SemaphoreType.DMA((3, 32)),
            pltpu.SemaphoreType.DMA((3,)),
        ],
        compiler_params=pltpu.CompilerParams(
            collective_id=0, has_side_effects=True, vmem_limit_bytes=60 * 2**20
        ),
    )(packed, inner, outer)


def scatter_kernel(g_ref, v_ref, out_ref, vout_ref, core_buf, b_buf, a_buf, z_buf, vec_buf, vec_z, send_sem, recv_sem, vec_send, vec_recv):
    me = Place()
    n_m, rows = out_ref.shape[0], out_ref.shape[1]
    c = me.c

    def part(m, dz, da, db, core):
        dp, y = me.chip(dz, da, db)
        return block_of(g_ref, m, dp, y * 2 + core, rows)

    def wait(m, slot):
        one = z_buf.at[m, 1]
        return remote(one, one, send_sem.at[m, slot], recv_sem.at[m, slot], me.device(db=1))

    def go(m, slot, src, dst, peer):
        remote(src, dst, send_sem.at[m, slot], recv_sem.at[m, slot], peer).start()

    def vec(step, src, dst, peer):
        return remote(src, dst, vec_send.at[step], vec_recv.at[step], peer)

    meet(me)
    partner = me.device(other=True)
    for m in range(n_m):
        for pick in (1, 0):

            @pl.loop(0, 8)
            def _(s):
                slot = 2 * s + pick
                go(m, slot, part(m, s // 2, s % 2, pick, 1 - c), core_buf.at[m, slot], partner)

    def from_core(m, dz, da, db):
        return 4 * dz + 2 * db + da

    for m in range(n_m):

        @pl.loop(0, 8)
        def _(s):
            dz, da = s // 2, s % 2
            slot = from_core(m, dz, da, 1)
            wait(m, slot).wait_recv()
            core_buf[m, slot] = part(m, dz, da, 1, c)[...] + core_buf[m, slot]
            go(m, 16 + s, core_buf.at[m, slot], b_buf.at[m, s], me.device(db=1))

        @pl.loop(0, 8)
        def _(s):
            dz, da = s // 2, s % 2
            slot = from_core(m, dz, da, 0)
            wait(m, slot).wait_recv()
            core_buf[m, slot] = part(m, dz, da, 0, c)[...] + core_buf[m, slot]

        @pl.loop(0, Z_SIZE)
        def _(k):
            wait(m, 16 + 2 * k + 1).wait_recv()
            b_buf[m, 2 * k + 1] = b_buf[m, 2 * k + 1] + core_buf[m, from_core(m, k, 1, 0)]
            go(m, 24 + k, b_buf.at[m, 2 * k + 1], a_buf.at[m, k], me.device(da=1))

        @pl.loop(0, Z_SIZE)
        def _(k):
            wait(m, 16 + 2 * k).wait_recv()
            b_buf[m, 2 * k] = b_buf[m, 2 * k] + core_buf[m, from_core(m, k, 0, 0)]

        @pl.loop(1, Z_SIZE)
        def _(k):
            wait(m, 24 + k).wait_recv()
            a_buf[m, k] = a_buf[m, k] + b_buf[m, 2 * k]
            go(m, 28 + k, a_buf.at[m, k], z_buf.at[m, k], me.device(dz=k))

        wait(m, 24).wait_recv()
        a_buf[m, 0] = a_buf[m, 0] + b_buf[m, 0]

    def peer_of(dx, dy):
        return {"dp": me.z * 2 + flip(me.x, dx), "tensor": 2 * flip(me.y, dy) + c}

    vec_buf[0] = v_ref[...]
    for step, peer in enumerate((partner, peer_of(1, 0), peer_of(0, 1))):
        copy = vec(step, vec_buf.at[2 * step], vec_buf.at[2 * step + 1], peer)
        copy.start()
        copy.wait()
        vec_buf[2 * step + 2] = vec_buf[2 * step] + vec_buf[2 * step + 1]
    vec_z[me.z] = vec_buf[6]
    zcopies = [vec(2 + k, vec_buf.at[6], vec_z.at[me.z], me.device(dz=k)) for k in range(1, Z_SIZE)]
    for copy in zcopies:
        copy.start()
    for copy in zcopies:
        copy.wait()
    vout_ref[...] = (vec_z[0] + vec_z[1]) + (vec_z[2] + vec_z[3])

    for m in range(n_m):
        total = a_buf[m, 0].astype(jnp.float32)
        for k in range(1, Z_SIZE):
            wait(m, 28 + k).wait_recv()
            total = total + z_buf[m, k].astype(jnp.float32)
        out_ref[m] = total

        @pl.loop(0, 28)
        def _(s):
            wait(m, s).wait_send()

        @pl.loop(29, 32)
        def _(s):
            wait(m, s).wait_send()


def scatter_all(grads, vector, n_dp):
    n_m, n_t, total_rows, width = grads.shape
    rows = total_rows // n_dp
    buf = lambda n: pltpu.VMEM((n_m, n, rows, width), jnp.bfloat16)
    return pl.pallas_call(
        scatter_kernel,
        out_shape=(
            jax.ShapeDtypeStruct((n_m, rows, width), jnp.float32),
            jax.ShapeDtypeStruct(vector.shape, jnp.float32),
        ),
        in_specs=[pl.BlockSpec(memory_space=pltpu.VMEM)] * 2,
        out_specs=[pl.BlockSpec(memory_space=pltpu.VMEM)] * 2,
        scratch_shapes=[
            buf(16),
            buf(8),
            buf(4),
            buf(4),
            pltpu.VMEM((7,) + vector.shape, jnp.float32),
            pltpu.VMEM((Z_SIZE,) + vector.shape, jnp.float32),
            pltpu.SemaphoreType.DMA((n_m, 32)),
            pltpu.SemaphoreType.DMA((n_m, 32)),
            pltpu.SemaphoreType.DMA((6,)),
            pltpu.SemaphoreType.DMA((6,)),
        ],
        compiler_params=pltpu.CompilerParams(
            collective_id=1, has_side_effects=True, vmem_limit_bytes=60 * 2**20
        ),
    )(grads, vector)


def data_parallel(
    hidden_in, seq_lengths, w_query, b_query, w_key, w_value, b_value, w_out, b_out, norm1_gain, norm1_bias,
    w_inner, b_inner, w_outer, b_outer, norm2_gain, norm2_bias, out_grad,
):
    n_dp, n_t = lax.axis_size("dp"), lax.axis_size("tensor")
    rows, width = hidden_in.shape
    cols = w_query.shape[1]
    heads = cols * n_t // HEAD_DIM
    scale = HEAD_DIM ** (-0.5)
    length = seq_lengths[lax.axis_index("tensor")]
    valid = lax.iota(jnp.int32, rows) < length
    mask = valid.astype(jnp.float32)[:, None]
    packed = jnp.concatenate((w_query, w_key, w_value, w_out), axis=1)
    whole = gather_all(packed, w_inner, w_outer, n_dp, n_t)
    dot = functools.partial(jnp.einsum, preferred_element_type=jnp.float32)
    low = lambda a: a.astype(jnp.bfloat16)

    def side(first):
        return whole[0, :, :, first * cols : (first + 1) * cols].transpose(1, 0, 2).reshape(width, n_t * cols)

    full_q, full_k, full_v, full_o = side(0), side(1), side(2), side(3)
    full_inner = whole[1].transpose(1, 0, 2).reshape(width, -1)
    full_outer = whole[2].transpose(1, 0, 2).reshape(width, -1)

    def heads_of(a):
        return a.reshape(rows, heads, HEAD_DIM).transpose(1, 0, 2)

    def rows_of(a):
        return a.transpose(1, 0, 2).reshape(rows, width)

    q = heads_of(low(dot("rd,dh->rh", hidden_in, full_q) + b_query))
    k = heads_of(low(dot("rd,dh->rh", hidden_in, full_k)))
    v = heads_of(low(dot("rd,dh->rh", hidden_in, full_v) + b_value))
    s = jnp.where(valid[None, None, :], dot("hqd,hkd->hqk", q, k) * scale, NEG_FILL)
    e = jnp.exp(s - jnp.max(s, axis=-1, keepdims=True))
    p = e / jnp.sum(e, axis=-1, keepdims=True)
    pb = low(p)
    attn = low(rows_of(dot("hqk,hkd->hqd", pb, v)))
    r1 = hidden_in.astype(jnp.float32) + (dot("rh,dh->rd", attn, full_o) + b_out)
    h1 = layer_norm(r1, norm1_gain, norm1_bias)
    h1b = low(h1)
    pre = dot("rd,df->rf", h1b, full_inner) + b_inner
    act = low(exact_gelu(pre))
    r2 = h1 + (dot("rf,df->rd", act, full_outer) + b_outer)
    y, back2 = jax.vjp(layer_norm, r2, norm2_gain, norm2_bias)
    layer_out = low(y * mask)
    dr2, d_gain2, d_bias2 = back2(out_grad.astype(jnp.float32) * mask)
    df = low(dr2)
    total = lambda a: jnp.sum(a, axis=0, dtype=jnp.float32)
    g_outer = low(dot("rd,rf->df", df, act))
    dact = dot("rd,df->rf", df, full_outer)
    dpre = low(jax.vjp(exact_gelu, pre)[1](dact)[0])
    g_inner = low(dot("rd,rf->df", h1b, dpre))
    dh1 = dr2 + dot("rf,df->rd", dpre, full_inner)
    dr1, d_gain1, d_bias1 = jax.vjp(layer_norm, r1, norm1_gain, norm1_bias)[1](dh1)
    dob = low(dr1)
    g_out = low(dot("rd,rh->dh", dob, attn))
    dattn = heads_of(low(dot("rd,dh->rh", dob, full_o)))
    dprob = dot("hqd,hkd->hqk", dattn, v)
    ds = low(p * (dprob - jnp.sum(p * dprob, axis=-1, keepdims=True)))
    dq = low(rows_of(dot("hqk,hkd->hqd", ds, k) * scale))
    dk = low(rows_of(dot("hqk,hqd->hkd", ds, q) * scale))
    dv = low(rows_of(dot("hqk,hqd->hkd", pb, dattn)))
    g_q, g_k, g_v = (low(dot("rd,rh->dh", hidden_in, a)) for a in (dq, dk, dv))
    grad_in = dr1 + (dot("rh,dh->rd", dq, full_q) + dot("rh,dh->rd", dk, full_k) + dot("rh,dh->rd", dv, full_v))

    split = lambda a: a.reshape(width, n_t, -1).transpose(1, 0, 2)
    grads = jnp.stack((jnp.concatenate([split(a) for a in (g_q, g_k, g_v, g_out)], axis=2), split(g_inner), split(g_outer)))
    vector = jnp.concatenate(
        (total(dq), total(dv), total(dob), d_gain1, d_bias1, total(df), d_gain2, d_bias2, total(dpre))
    ).reshape(-1, 128)
    shards, sums = scatter_all(grads, vector, n_dp)
    sums = sums.reshape(-1)
    vecs = [sums[i * width : (i + 1) * width] for i in range(8)]
    gq, gk, gv, go = (shards[0, :, i * cols : (i + 1) * cols] for i in range(4))
    return (
        layer_out, grad_in, gq, vecs[0], gk, gv, vecs[1], go, vecs[2], vecs[3], vecs[4],
        shards[1], sums[8 * width :], shards[2], vecs[5], vecs[6], vecs[7],
    )


def solution(mesh):
    in_specs = (
        P(("dp", "tensor"), None),
        P("dp"),
        P("dp", "tensor"),
        P(),
        P("dp", "tensor"),
        P("dp", "tensor"),
        P(),
        P("dp", "tensor"),
        P(),
        P(),
        P(),
        P("dp", "tensor"),
        P(),
        P("dp", "tensor"),
        P(),
        P(),
        P(),
        P(("dp", "tensor"), None),
    )
    out_specs = (
        P(("dp", "tensor"), None),
        P(("dp", "tensor"), None),
        P("dp", "tensor"),
        P(),
        P("dp", "tensor"),
        P("dp", "tensor"),
        P(),
        P("dp", "tensor"),
        P(),
        P(),
        P(),
        P("dp", "tensor"),
        P(),
        P("dp", "tensor"),
        P(),
        P(),
        P(),
    )
    small = mesh.shape["dp"] == 2 * Z_SIZE and mesh.shape["tensor"] == 4
    return jax.shard_map(
        data_parallel if small else per_device, mesh=mesh, in_specs=in_specs, out_specs=out_specs, check_vma=False
    )
```

```python
import functools

import jax
import jax.numpy as jnp
from jax import lax
from jax.experimental import pallas as pl
from jax.experimental.pallas import tpu as pltpu
from jax.sharding import PartitionSpec as P

HEAD_DIM = 64


NEG_FILL = -1000000000.0
NORM_EPS = 1e-12


def layer_norm(residual, norm_gain, norm_bias):
    centre = residual - jnp.mean(residual, axis=-1, keepdims=True)
    spread = jnp.mean(centre * centre, axis=-1, keepdims=True)
    return centre * lax.rsqrt(spread + NORM_EPS) * norm_gain + norm_bias


def exact_gelu(values):
    return jax.nn.gelu(values, approximate=False)


def contract_last(first_op, second_op):
    return lax.dot_general(
        first_op, second_op, (((1,), (1,)), ((), ())), preferred_element_type=jnp.float32
    )


def contract_first(first_op, second_op):
    return lax.dot_general(
        first_op, second_op, (((0,), (0,)), ((), ())), preferred_element_type=jnp.float32
    )


def split_blocks(heads_arr, block_rows):
    batches, length, head_size = heads_arr.shape
    return heads_arr.reshape(batches, length // block_rows, block_rows, head_size).transpose(
        1, 0, 2, 3
    )


def join_blocks(block_array):
    block_count, batches, block_rows, head_size = block_array.shape
    return block_array.transpose(1, 0, 2, 3).reshape(batches, block_count * block_rows, head_size)


def block_scores(query_portion, key_head_tensor, key_valid, score_scale):
    scores = (
        jnp.einsum(
            "eix,evx->eiv", query_portion, key_head_tensor, preferred_element_type=jnp.float32
        )
        * score_scale
    )
    return jnp.where(key_valid[:, None, :], scores, NEG_FILL)


def attend(query_heads, key_head_tensor, value_head_tensor, key_valid, block_rows, score_scale):

    def one_block(query_portion):
        scores = block_scores(query_portion, key_head_tensor, key_valid, score_scale)
        row_max = jnp.max(scores, axis=-1, keepdims=True)
        exponent = jnp.exp(scores - row_max)
        row_total = jnp.sum(exponent, axis=-1, keepdims=True)
        softmax_reduced = (exponent / row_total).astype(jnp.bfloat16)
        mixture = jnp.einsum(
            "fwj,fjt->fwt", softmax_reduced, value_head_tensor, preferred_element_type=jnp.float32
        )
        return (mixture.astype(jnp.bfloat16), row_max, row_total)

    mixture, row_max, row_total = lax.map(one_block, split_blocks(query_heads, block_rows))
    return (join_blocks(mixture), row_max, row_total)


def attend_back(
    query_heads,
    key_head_tensor,
    value_head_tensor,
    grad_heads,
    row_max,
    row_total,
    key_valid,
    block_rows,
    score_scale,
):

    def one_block(running, block_in):
        key_grad, value_grad = running
        query_portion, gradient_portion, max_part, total_part = block_in
        scores = block_scores(query_portion, key_head_tensor, key_valid, score_scale)
        softmax = jnp.exp(scores - max_part) / total_part
        softmax_reduced = softmax.astype(jnp.bfloat16)
        soft_grad = jnp.einsum(
            "eix,evx->eiv", gradient_portion, value_head_tensor, preferred_element_type=jnp.float32
        )
        centre = jnp.sum(softmax * soft_grad, axis=-1, keepdims=True)
        score_gradient = (softmax * (soft_grad - centre)).astype(jnp.bfloat16)
        query_grad = (
            jnp.einsum(
                "fwj,fjt->fwt", score_gradient, key_head_tensor, preferred_element_type=jnp.float32
            )
            * score_scale
        )
        key_grad = (
            key_grad
            + jnp.einsum(
                "oxl,oxn->oln", score_gradient, query_portion, preferred_element_type=jnp.float32
            )
            * score_scale
        )
        value_grad = value_grad + jnp.einsum(
            "oxl,oxn->oln", softmax_reduced, gradient_portion, preferred_element_type=jnp.float32
        )
        return ((key_grad, value_grad), query_grad)

    zero_grads = jnp.zeros(key_head_tensor.shape, jnp.float32)
    block_inputs = (
        split_blocks(query_heads, block_rows),
        split_blocks(grad_heads, block_rows),
        row_max,
        row_total,
    )
    (key_grad, value_grad), query_grad = lax.scan(one_block, (zero_grads, zero_grads), block_inputs)
    return (join_blocks(query_grad), key_grad, value_grad)


def per_device(
    hidden_in,
    seq_lengths,
    w_query,
    b_query,
    w_key,
    w_value,
    b_value,
    w_out,
    b_out,
    norm1_gain,
    norm1_bias,
    w_inner,
    b_inner,
    w_outer,
    b_outer,
    norm2_gain,
    norm2_bias,
    out_grad,
):
    tensor_size = lax.axis_size("tensor")
    tensor_place = lax.axis_index("tensor")
    local_rows, feature_width = hidden_in.shape
    group_rows = local_rows * tensor_size
    seq_count = seq_lengths.shape[0]
    seq_len = group_rows // seq_count
    head_cols = w_query.shape[1]
    inner_cols = w_inner.shape[1]
    heads_here = head_cols // HEAD_DIM
    block_rows = min(512, seq_len)
    score_scale = HEAD_DIM ** (-0.5)
    local_start = tensor_place * local_rows
    row_index = lax.iota(jnp.int32, group_rows)
    seq_match = (row_index[:, None] // seq_len == lax.iota(jnp.int32, seq_count)[None, :]).astype(
        jnp.int32
    )
    row_limit = jnp.sum(seq_match * seq_lengths[None, :], axis=1)
    row_valid = row_index % seq_len < row_limit
    local_mask = lax.dynamic_slice_in_dim(row_valid, local_start, local_rows).astype(jnp.float32)[
        :, None
    ]
    key_valid = jnp.repeat(row_valid.reshape(seq_count, seq_len), heads_here, axis=0)

    def heads_of(matrix):
        shaped = matrix.reshape(seq_count, seq_len, heads_here, HEAD_DIM).transpose(0, 2, 1, 3)
        return shaped.reshape(seq_count * heads_here, seq_len, HEAD_DIM)

    def rows_of(matrix):
        shaped = matrix.reshape(seq_count, heads_here, seq_len, HEAD_DIM).transpose(0, 2, 1, 3)
        return shaped.reshape(group_rows, head_cols)

    full_query, full_key, full_value, full_out, full_inner, full_outer = (
        lax.all_gather(w_query, "dp", axis=0, tiled=True),
        lax.all_gather(w_key, "dp", axis=0, tiled=True),
        lax.all_gather(w_value, "dp", axis=0, tiled=True),
        lax.all_gather(w_out, "dp", axis=0, tiled=True),
        lax.all_gather(w_inner, "dp", axis=0, tiled=True),
        lax.all_gather(w_outer, "dp", axis=0, tiled=True),
    )
    joint_weight = jnp.concatenate((full_query, full_key, full_value), axis=1)
    query_bias = lax.dynamic_slice_in_dim(b_query, tensor_place * head_cols, head_cols)
    value_bias = lax.dynamic_slice_in_dim(b_value, tensor_place * head_cols, head_cols)
    inner_bias = lax.dynamic_slice_in_dim(b_inner, tensor_place * inner_cols, inner_cols)
    joint_bias = jnp.concatenate((query_bias, jnp.zeros((head_cols,), jnp.float32), value_bias))
    whole_in = lax.all_gather(hidden_in, "tensor", axis=0, tiled=True)
    joint_rows = (
        jnp.dot(whole_in, joint_weight, preferred_element_type=jnp.float32) + joint_bias
    ).astype(jnp.bfloat16)
    query_heads = heads_of(joint_rows[:, :head_cols])
    key_head_tensor = heads_of(joint_rows[:, head_cols : 2 * head_cols])
    value_head_tensor = heads_of(joint_rows[:, 2 * head_cols :])
    mixture_heads, row_max, row_total = attend(
        query_heads, key_head_tensor, value_head_tensor, key_valid, block_rows, score_scale
    )
    mixture = rows_of(mixture_heads)
    summed_out = lax.psum_scatter(
        contract_last(mixture, full_out).astype(jnp.bfloat16),
        "tensor",
        scatter_dimension=0,
        tiled=True,
    ).astype(jnp.float32)
    first_sum = hidden_in.astype(jnp.float32) + (summed_out + b_out)
    first_norm = layer_norm(first_sum, norm1_gain, norm1_bias)
    mid_whole = lax.all_gather(first_norm.astype(jnp.bfloat16), "tensor", axis=0, tiled=True)
    pre_act = jnp.dot(mid_whole, full_inner, preferred_element_type=jnp.float32) + inner_bias
    act_low = exact_gelu(pre_act).astype(jnp.bfloat16)
    second_sum = first_norm + (
        lax.psum_scatter(
            contract_last(act_low, full_outer).astype(jnp.bfloat16),
            "tensor",
            scatter_dimension=0,
            tiled=True,
        ).astype(jnp.float32)
        + b_outer
    )
    normed, norm2_back = jax.vjp(layer_norm, second_sum, norm2_gain, norm2_bias)
    layer_out = (normed * local_mask).astype(jnp.bfloat16)
    out_cot = out_grad.astype(jnp.float32) * local_mask
    dsecond, gain2_part, bias2_part = norm2_back(out_cot)
    dffn_low = dsecond.astype(jnp.bfloat16)
    outer_bias_part = jnp.sum(dffn_low, axis=0, dtype=jnp.float32)
    dffn_whole = lax.all_gather(dffn_low, "tensor", axis=0, tiled=True)
    grad_outer = contract_first(dffn_whole, act_low)
    dact = jnp.dot(dffn_whole, full_outer, preferred_element_type=jnp.float32)
    _, gelu_back = jax.vjp(exact_gelu, pre_act)
    dpre_low = gelu_back(dact)[0].astype(jnp.bfloat16)
    inner_bias_part = jnp.sum(dpre_low, axis=0, dtype=jnp.float32)
    grad_inner = contract_first(mid_whole, dpre_low)
    dfirst_norm = dsecond + lax.psum_scatter(
        contract_last(dpre_low, full_inner).astype(jnp.bfloat16),
        "tensor",
        scatter_dimension=0,
        tiled=True,
    ).astype(jnp.float32)
    _, norm1_back = jax.vjp(layer_norm, first_sum, norm1_gain, norm1_bias)
    dfirst, gain1_part, bias1_part = norm1_back(dfirst_norm)
    dattn_low = dfirst.astype(jnp.bfloat16)
    out_bias_part = jnp.sum(dattn_low, axis=0, dtype=jnp.float32)
    dattn_whole = lax.all_gather(dattn_low, "tensor", axis=0, tiled=True)
    grad_out_w = contract_first(dattn_whole, mixture)
    dmixture = jnp.dot(dattn_whole, full_out, preferred_element_type=jnp.float32).astype(
        jnp.bfloat16
    )
    dquery_heads, dkey_heads, dvalue_heads = attend_back(
        query_heads,
        key_head_tensor,
        value_head_tensor,
        heads_of(dmixture),
        row_max,
        row_total,
        key_valid,
        block_rows,
        score_scale,
    )
    djoint = jnp.concatenate(
        (rows_of(dquery_heads), rows_of(dkey_heads), rows_of(dvalue_heads)), axis=1
    ).astype(jnp.bfloat16)
    joint_bias_part = jnp.sum(djoint, axis=0, dtype=jnp.float32)
    grad_joint = contract_first(whole_in, djoint)
    grad_in = dfirst + lax.psum_scatter(
        contract_last(djoint, joint_weight).astype(jnp.bfloat16),
        "tensor",
        scatter_dimension=0,
        tiled=True,
    ).astype(jnp.float32)
    grad_query = grad_joint[:, :head_cols]
    grad_key = grad_joint[:, head_cols : 2 * head_cols]
    grad_value = grad_joint[:, 2 * head_cols :]
    shard_grads = tuple(
        (
            lax.psum_scatter(grad_query, "dp", scatter_dimension=0, tiled=True),
            lax.psum_scatter(grad_key, "dp", scatter_dimension=0, tiled=True),
            lax.psum_scatter(grad_value, "dp", scatter_dimension=0, tiled=True),
            lax.psum_scatter(grad_out_w, "dp", scatter_dimension=0, tiled=True),
            lax.psum_scatter(grad_inner, "dp", scatter_dimension=0, tiled=True),
            lax.psum_scatter(grad_outer, "dp", scatter_dimension=0, tiled=True),
        )
    )

    def placed(vector, total_len):
        return lax.dynamic_update_slice_in_dim(
            jnp.zeros((total_len,), jnp.float32), vector, tensor_place * vector.shape[0], 0
        )

    query_bias_part = placed(joint_bias_part[:head_cols], feature_width)
    value_bias_part = placed(joint_bias_part[2 * head_cols :], feature_width)
    hidden_bias_part = placed(inner_bias_part, b_inner.shape[0])
    vector_sums = lax.psum(
        (
            query_bias_part,
            value_bias_part,
            out_bias_part,
            gain1_part,
            bias1_part,
            hidden_bias_part,
            outer_bias_part,
            gain2_part,
            bias2_part,
        ),
        ("dp", "tensor"),
    )
    return (
        layer_out,
        grad_in,
        shard_grads[0],
        vector_sums[0],
        shard_grads[1],
        shard_grads[2],
        vector_sums[1],
        shard_grads[3],
        vector_sums[2],
        vector_sums[3],
        vector_sums[4],
        shard_grads[4],
        vector_sums[5],
        shard_grads[5],
        vector_sums[6],
        vector_sums[7],
        vector_sums[8],
    )


Z_SIZE = 4
MESH_IDS = pl.DeviceIdType.MESH


def flip(place, bit):
    return place + bit - 2 * place * bit


class Place:
    def __init__(self):
        self.dp = lax.axis_index("dp")
        self.t = lax.axis_index("tensor")
        self.z = self.dp // 2
        self.x = self.dp % 2
        self.y = self.t // 2
        self.c = self.t % 2

    def chip(self, dz, da, db):
        c = self.c
        z = lax.rem(self.z - dz + Z_SIZE, Z_SIZE)
        x = flip(self.x, da * c + db * (1 - c))
        y = flip(self.y, da * (1 - c) + db * c)
        return z * 2 + x, y

    def device(self, dz=0, da=0, db=0, other=False):
        dp, y = self.chip(dz, da, db)
        core = 1 - self.c if other else self.c
        return {"dp": dp, "tensor": y * 2 + core}


def block_of(ref, m, dp, t, rows):
    return ref.at[m, t, pl.ds(pl.multiple_of(dp * rows, rows), rows), :]


def meet(me):
    barrier = pltpu.get_barrier_semaphore()
    peers = [me.device(dz=k) for k in range(1, Z_SIZE)]
    peers += [me.device(da=1), me.device(db=1), me.device(other=True)]
    for peer in peers:
        pl.semaphore_signal(barrier, inc=1, device_id=peer, device_id_type=MESH_IDS)
    pl.semaphore_wait(barrier, len(peers))


def remote(src, dst, send, recv, peer):
    return pltpu.make_async_remote_copy(
        src_ref=src, dst_ref=dst, send_sem=send, recv_sem=recv, device_id=peer, device_id_type=MESH_IDS
    )


def gather_kernel(p_ref, i_ref, o_ref, g_ref, send_sem, recv_sem, local_sem):
    me = Place()
    rows = p_ref.shape[0]
    c = me.c
    shards = (p_ref, i_ref, o_ref)

    def send(m, slot, src, chip, core, peer):
        dst = block_of(g_ref, m, chip[0], chip[1] * 2 + core, rows)
        remote(src, dst, send_sem.at[m, slot], recv_sem.at[m, slot], peer).start()

    def own(m, slot, peer):
        send(m, slot, shards[m], me.chip(0, 0, 0), c, peer)

    def forward(m, slot, dz, da, db, peer):
        chip = me.chip(dz, da, db)
        send(m, slot, block_of(g_ref, m, chip[0], chip[1] * 2 + c, rows), chip, c, peer)

    def arrived(m, slot):
        any_block = block_of(g_ref, m, 0, 0, rows)
        remote(any_block, any_block, send_sem.at[m, slot], recv_sem.at[m, slot], me.device(db=1)).wait_recv()

    def left(m, slot):
        any_block = block_of(g_ref, m, 0, 0, rows)
        remote(any_block, any_block, send_sem.at[m, slot], recv_sem.at[m, slot], me.device(db=1)).wait_send()

    meet(me)
    copies = []
    for m in range(3):
        for k in range(1, Z_SIZE):
            own(m, k, me.device(dz=Z_SIZE - k))
        own(m, 4, me.device(da=1))
        own(m, 8, me.device(db=1))
        own(m, 16, me.device(other=True))
        copy = pltpu.make_async_copy(shards[m], block_of(g_ref, m, me.dp, me.t, rows), local_sem.at[m])
        copy.start()
        copies.append(copy)
    for m in range(3):

        @pl.loop(1, Z_SIZE)
        def _(k):
            arrived(m, k)
            forward(m, 4 + k, k, 0, 0, me.device(da=1))
            forward(m, 8 + 2 * k, k, 0, 0, me.device(db=1))
            forward(m, 16 + 4 * k, k, 0, 0, me.device(other=True))

        @pl.loop(0, Z_SIZE)
        def _(k):
            arrived(m, 4 + k)
            forward(m, 9 + 2 * k, k, 1, 0, me.device(db=1))
            forward(m, 18 + 4 * k, k, 1, 0, me.device(other=True))

        @pl.loop(0, 2 * Z_SIZE)
        def _(s):
            arrived(m, 8 + s)
            forward(m, 17 + 2 * s, s // 2, s % 2, 1, me.device(other=True))

    for m in range(3):
        copies[m].wait()

        @pl.loop(16, 32)
        def _(s):
            arrived(m, s)

        @pl.loop(1, 32)
        def _(s):
            left(m, s)


def gather_all(packed, inner, outer, n_dp, n_t):
    rows, width = packed.shape
    return pl.pallas_call(
        gather_kernel,
        out_shape=jax.ShapeDtypeStruct((3, n_t, n_dp * rows, width), jnp.bfloat16),
        in_specs=[pl.BlockSpec(memory_space=pltpu.VMEM)] * 3,
        out_specs=pl.BlockSpec(memory_space=pltpu.VMEM),
        scratch_shapes=[
            pltpu.SemaphoreType.DMA((3, 32)),
            pltpu.SemaphoreType.DMA((3, 32)),
            pltpu.SemaphoreType.DMA((3,)),
        ],
        compiler_params=pltpu.CompilerParams(
            collective_id=0, has_side_effects=True, vmem_limit_bytes=60 * 2**20
        ),
    )(packed, inner, outer)


def scatter_kernel(g_ref, v_ref, out_ref, vout_ref, core_buf, b_buf, a_buf, z_buf, vec_buf, vec_z, send_sem, recv_sem, vec_send, vec_recv):
    me = Place()
    n_m, rows = out_ref.shape[0], out_ref.shape[1]
    c = me.c

    def part(m, dz, da, db, core):
        dp, y = me.chip(dz, da, db)
        return block_of(g_ref, m, dp, y * 2 + core, rows)

    def wait(m, slot):
        one = z_buf.at[m, 1]
        return remote(one, one, send_sem.at[m, slot], recv_sem.at[m, slot], me.device(db=1))

    def go(m, slot, src, dst, peer):
        remote(src, dst, send_sem.at[m, slot], recv_sem.at[m, slot], peer).start()

    def vec(step, src, dst, peer):
        return remote(src, dst, vec_send.at[step], vec_recv.at[step], peer)

    meet(me)
    partner = me.device(other=True)
    for m in range(n_m):
        for pick in (1, 0):

            @pl.loop(0, 8)
            def _(s):
                slot = 2 * s + pick
                go(m, slot, part(m, s // 2, s % 2, pick, 1 - c), core_buf.at[m, slot], partner)

    def from_core(m, dz, da, db):
        return 4 * dz + 2 * db + da

    for m in range(n_m):

        @pl.loop(0, 8)
        def _(s):
            dz, da = s // 2, s % 2
            slot = from_core(m, dz, da, 1)
            wait(m, slot).wait_recv()
            core_buf[m, slot] = part(m, dz, da, 1, c)[...] + core_buf[m, slot]
            go(m, 16 + s, core_buf.at[m, slot], b_buf.at[m, s], me.device(db=1))

        @pl.loop(0, 8)
        def _(s):
            dz, da = s // 2, s % 2
            slot = from_core(m, dz, da, 0)
            wait(m, slot).wait_recv()
            core_buf[m, slot] = part(m, dz, da, 0, c)[...] + core_buf[m, slot]

        @pl.loop(0, Z_SIZE)
        def _(k):
            wait(m, 16 + 2 * k + 1).wait_recv()
            b_buf[m, 2 * k + 1] = b_buf[m, 2 * k + 1] + core_buf[m, from_core(m, k, 1, 0)]
            go(m, 24 + k, b_buf.at[m, 2 * k + 1], a_buf.at[m, k], me.device(da=1))

        @pl.loop(0, Z_SIZE)
        def _(k):
            wait(m, 16 + 2 * k).wait_recv()
            b_buf[m, 2 * k] = b_buf[m, 2 * k] + core_buf[m, from_core(m, k, 0, 0)]

        @pl.loop(1, Z_SIZE)
        def _(k):
            wait(m, 24 + k).wait_recv()
            a_buf[m, k] = a_buf[m, k] + b_buf[m, 2 * k]
            go(m, 28 + k, a_buf.at[m, k], z_buf.at[m, k], me.device(dz=k))

        wait(m, 24).wait_recv()
        a_buf[m, 0] = a_buf[m, 0] + b_buf[m, 0]

    def peer_of(dx, dy):
        return {"dp": me.z * 2 + flip(me.x, dx), "tensor": 2 * flip(me.y, dy) + c}

    vec_buf[0] = v_ref[...]
    for step, peer in enumerate((partner, peer_of(1, 0), peer_of(0, 1))):
        copy = vec(step, vec_buf.at[2 * step], vec_buf.at[2 * step + 1], peer)
        copy.start()
        copy.wait()
        vec_buf[2 * step + 2] = vec_buf[2 * step] + vec_buf[2 * step + 1]
    vec_z[me.z] = vec_buf[6]
    zcopies = [vec(2 + k, vec_buf.at[6], vec_z.at[me.z], me.device(dz=k)) for k in range(1, Z_SIZE)]
    for copy in zcopies:
        copy.start()
    for copy in zcopies:
        copy.wait()
    vout_ref[...] = (vec_z[0] + vec_z[1]) + (vec_z[2] + vec_z[3])

    for m in range(n_m):
        total = a_buf[m, 0].astype(jnp.float32)
        for k in range(1, Z_SIZE):
            wait(m, 28 + k).wait_recv()
            total = total + z_buf[m, k].astype(jnp.float32)
        out_ref[m] = total

        @pl.loop(0, 28)
        def _(s):
            wait(m, s).wait_send()

        @pl.loop(29, 32)
        def _(s):
            wait(m, s).wait_send()


def scatter_all(grads, vector, n_dp):
    n_m, n_t, total_rows, width = grads.shape
    rows = total_rows // n_dp
    buf = lambda n: pltpu.VMEM((n_m, n, rows, width), jnp.bfloat16)
    return pl.pallas_call(
        scatter_kernel,
        out_shape=(
            jax.ShapeDtypeStruct((n_m, rows, width), jnp.float32),
            jax.ShapeDtypeStruct(vector.shape, jnp.float32),
        ),
        in_specs=[pl.BlockSpec(memory_space=pltpu.VMEM)] * 2,
        out_specs=[pl.BlockSpec(memory_space=pltpu.VMEM)] * 2,
        scratch_shapes=[
            buf(16),
            buf(8),
            buf(4),
            buf(4),
            pltpu.VMEM((7,) + vector.shape, jnp.float32),
            pltpu.VMEM((Z_SIZE,) + vector.shape, jnp.float32),
            pltpu.SemaphoreType.DMA((n_m, 32)),
            pltpu.SemaphoreType.DMA((n_m, 32)),
            pltpu.SemaphoreType.DMA((6,)),
            pltpu.SemaphoreType.DMA((6,)),
        ],
        compiler_params=pltpu.CompilerParams(
            collective_id=1, has_side_effects=True, vmem_limit_bytes=60 * 2**20
        ),
    )(grads, vector)


def dot_nn(a, b):
    return lax.dot_general(a, b, (((1,), (0,)), ((), ())), preferred_element_type=jnp.float32)


def dot_nt(a, b):
    return lax.dot_general(a, b, (((1,), (1,)), ((), ())), preferred_element_type=jnp.float32)


def dot_tn(a, b):
    return lax.dot_general(a, b, (((0,), (0,)), ((), ())), preferred_element_type=jnp.float32)


def low(a):
    return a.astype(jnp.bfloat16)


def row_mean(a):
    return jnp.mean(a, axis=-1, keepdims=True)


def normalise(r):
    centre = r - row_mean(r)
    inverse = lax.rsqrt(row_mean(centre * centre) + NORM_EPS)
    return centre * inverse, inverse


def norm_back(g, z, inverse):
    return (g - row_mean(g) - z * row_mean(g * z)) * inverse


def gelu_pair(u):
    cdf = 0.5 + 0.5 * lax.erf(u * (0.5**0.5))
    density = jnp.exp(-0.5 * u * u) * ((0.5 / jnp.pi) ** 0.5)
    return u * cdf, cdf + u * density


V_BQ, V_BV, V_BO, V_G1, V_B1, V_BF, V_G2, V_B2, V_BI = range(9)
TILE = 64


class Layer:
    def __init__(self, **refs):
        self.__dict__.update(refs)
        self.rows, self.width = self.x.shape
        self.n_t = self.w.shape[1]
        self.cols = self.width // self.n_t
        self.heads = self.cols // HEAD_DIM
        self.ocol = (3 * self.cols) // 128 * 128

    def tiles(self, body):
        @pl.loop(0, self.rows // TILE)
        def _(i):
            body(pl.ds(pl.multiple_of(i * TILE, TILE), TILE))

    def project(self, t):
        lane = lax.broadcasted_iota(jnp.int32, (1, self.width), 1)
        out = dot_nn(self.x[...], self.w[0, t]) + self.qkv_bias[t]
        self.qkv[t] = low(jnp.where(lane < 3 * self.cols, out, 0.0))

    def piece(self, t, which, j):
        first = which * self.cols + j * HEAD_DIM
        return self.qkv.at[t, :, first : first + HEAD_DIM]

    def attend(self, t, valid):
        self.att[t, :, : HEAD_DIM] = jnp.zeros((self.rows, HEAD_DIM), jnp.bfloat16)
        for j in range(self.heads):
            q, k, v = (self.piece(t, i, j)[...] for i in range(3))
            s = dot_nt(k, q * jnp.bfloat16(HEAD_DIM**-0.5))
            s = jnp.where(valid, s, NEG_FILL)
            e = jnp.exp(s - jnp.max(s, axis=0, keepdims=True))
            p = low(e * (1.0 / jnp.sum(e, axis=0, keepdims=True)))
            self.p[t * self.heads + j] = p
            mix = dot_tn(v, p)
            first = 3 * self.cols - self.ocol + j * HEAD_DIM
            self.att[t, :, first : first + HEAD_DIM] = low(mix.T)

    def out_project(self, t):
        self.acc[...] += dot_nt(self.att[t], self.w[0, t, :, self.ocol :])

    def start_residual(self):
        self.acc[...] = self.x[...].astype(jnp.float32) + self.vec[2:3, :]

    def first_norm(self):
        def body(r):
            z, inverse = normalise(self.acc[r, :])
            self.z1[r, :] = z
            self.inv1[r, :] = jnp.broadcast_to(inverse, (TILE, 128))
            h1 = z * self.vec[3:4, :] + self.vec[4:5, :]
            self.h1b[r, :] = low(h1)
            self.acc[r, :] = h1 + self.vec[0:1, :]

        self.tiles(body)

    def inner(self, t):
        @pl.loop(0, self.rows // 128)
        def _(i):
            r = pl.ds(pl.multiple_of(i * 128, 128), 128)
            pre = dot_nn(self.h1b[r, :], self.w[1, t]) + self.inner_bias[t]
            act, slope = gelu_pair(pre)
            self.act[t, r, :] = low(act)
            self.slope[t, r, :] = low(slope)

    def outer(self, t):
        self.acc[...] += dot_nt(self.act[t], self.w[2, t])

    def second_norm(self, length):
        self.sums[...] = jnp.zeros_like(self.sums)

        def body(r):
            z, inverse = normalise(self.acc[r, :])
            place = r.start + lax.broadcasted_iota(jnp.int32, (TILE, 1), 0)
            mask = (place < length).astype(jnp.float32)
            gain = self.vec[5:6, :]
            self.y[r, :] = low((z * gain + self.vec[6:7, :]) * mask)
            dy = self.og[r, :].astype(jnp.float32) * mask
            dr2 = norm_back(dy * gain, z, inverse)
            self.acc[r, :] = dr2
            df = low(dr2)
            self.df[r, :] = df
            self.sums[V_G2] += fold(dy * z)
            self.sums[V_B2] += fold(dy)
            self.sums[V_BF] += fold(df.astype(jnp.float32))

        self.tiles(body)

    def outer_back(self, t):
        self.dact[...] = dot_nn(self.df[...], self.w[2, t])

        def body(r):
            d = low(self.dact[r, :] * self.slope[t, r, :].astype(jnp.float32))
            self.slope[t, r, :] = d
            self.sums[V_BI + t] += fold(d.astype(jnp.float32))

        self.tiles(body)
        self.w[2, t] = low(dot_nn(self.df_t[...], self.act[t]))

    def inner_back(self, t):
        self.acc[...] += dot_nt(self.slope[t], self.w[1, t])
        self.w[1, t] = low(dot_nn(self.h1b_t[...], self.slope[t]))

    def first_norm_back(self):
        def body(r):
            z = self.z1[r, :]
            dh1 = self.acc[r, :]
            self.sums[V_G1] += fold(dh1 * z)
            self.sums[V_B1] += fold(dh1)
            dr1 = norm_back(dh1 * self.vec[3:4, :], z, self.inv1[r, :1])
            self.acc[r, :] = dr1
            dob = low(dr1)
            self.df[r, :] = dob
            self.sums[V_BO] += fold(dob.astype(jnp.float32))

        self.tiles(body)

    def attend_back(self, t):
        scale = HEAD_DIM**-0.5
        self.datt[...] = low(dot_nn(self.df[...], self.w[0, t, :, self.ocol :]))
        for j in range(self.heads):
            first = 3 * self.cols - self.ocol + j * HEAD_DIM
            d = self.datt[:, first : first + HEAD_DIM]
            q, k, v = (self.piece(t, i, j)[...] for i in range(3))
            p = self.p[t * self.heads + j]
            dp = dot_nt(v, d)
            pf = p.astype(jnp.float32)
            delta = jnp.sum(pf * dp, axis=0, keepdims=True)
            ds = low(pf * (dp - delta))
            self.piece(t, 2, j)[...] = low(dot_nn(p, d))
            self.piece(t, 1, j)[...] = low(dot_nn(ds, q) * scale)
            self.piece(t, 0, j)[...] = low((dot_tn(k, ds) * scale).T)

    def project_back(self, t):
        self.acc[...] += dot_nt(self.qkv[t], self.w[0, t])

        def body(r):
            self.sums[V_BI + self.n_t + t] += fold(self.qkv[t, r, :].astype(jnp.float32))

        self.tiles(body)
        self.w[0, t] = low(dot_nn(self.x_t[...], self.qkv[t]))
        out = self.w.at[0, t, :, self.ocol :]
        out[...] = low(out[...].astype(jnp.float32) + dot_nn(self.df_t[...], self.att[t]))

    def transpose(self, src, dst):
        dst[...] = src[...].T


def fold(a):
    return jnp.sum(a.reshape(a.shape[0] // 8, 8, a.shape[1]), axis=0)


def layer_kernel(
    length_ref, x_ref, og_ref, w_in, qkv_bias, inner_bias, vec_ref,
    y_ref, acc_ref, w_ref, sums_ref,
    qkv, p, att, z1, inv1, h1b, act, slope, df, datt, dact, x_t, h1b_t, df_t, sems,
):
    copies = [pltpu.make_async_copy(w_in.at[m], w_ref.at[m], sems.at[m]) for m in range(3)]
    for copy in copies:
        copy.start()
    a = Layer(
        x=x_ref, og=og_ref, w=w_ref, qkv_bias=qkv_bias, inner_bias=inner_bias, vec=vec_ref, y=y_ref, acc=acc_ref, sums=sums_ref,
        qkv=qkv, p=p, att=att, z1=z1, inv1=inv1, h1b=h1b, act=act, slope=slope, df=df, datt=datt, dact=dact, x_t=x_t, h1b_t=h1b_t, df_t=df_t,
    )
    length = length_ref[0]
    valid = lax.broadcasted_iota(jnp.int32, (a.rows, 1), 0) < length
    loop = pl.loop(0, a.n_t)
    a.transpose(a.x, a.x_t)
    a.start_residual()
    copies[0].wait()

    @loop
    def _(t):
        a.project(t)
        a.attend(t, valid)
        a.out_project(t)

    a.first_norm()
    a.transpose(a.h1b, a.h1b_t)
    copies[1].wait()
    copies[2].wait()

    @loop
    def _(t):
        a.inner(t)
        a.outer(t)

    a.second_norm(length)
    a.transpose(a.df, a.df_t)

    @loop
    def _(t):
        a.outer_back(t)
        a.inner_back(t)

    a.first_norm_back()
    a.transpose(a.df, a.df_t)

    @loop
    def _(t):
        a.attend_back(t)
        a.project_back(t)


def layer(length, x, og, whole, qkv_bias, inner_bias, vec):
    rows, width = x.shape
    n_t = whole.shape[1]
    cols = width // n_t
    heads = width // HEAD_DIM
    owidth = width - (3 * cols) // 128 * 128
    bf, f32 = jnp.bfloat16, jnp.float32
    vmem = pl.BlockSpec(memory_space=pltpu.VMEM)
    return pl.pallas_call(
        layer_kernel,
        out_shape=(
            jax.ShapeDtypeStruct((rows, width), bf),
            jax.ShapeDtypeStruct((rows, width), f32),
            jax.ShapeDtypeStruct(whole.shape, bf),
            jax.ShapeDtypeStruct((V_BI + 2 * n_t, 8, width), f32),
        ),
        in_specs=[pl.BlockSpec(memory_space=pltpu.SMEM), vmem, vmem, pl.BlockSpec(memory_space=pl.ANY), vmem, vmem, vmem],
        out_specs=[vmem] * 4,
        scratch_shapes=[
            pltpu.VMEM((n_t, rows, width), bf),
            pltpu.VMEM((heads, rows, rows), bf),
            pltpu.VMEM((n_t, rows, owidth), bf),
            pltpu.VMEM((rows, width), f32),
            pltpu.VMEM((rows, 128), f32),
            pltpu.VMEM((rows, width), bf),
            pltpu.VMEM((n_t, rows, width), bf),
            pltpu.VMEM((n_t, rows, width), bf),
            pltpu.VMEM((rows, width), bf),
            pltpu.VMEM((rows, owidth), bf),
            pltpu.VMEM((rows, width), f32),
            pltpu.VMEM((width, rows), bf),
            pltpu.VMEM((width, rows), bf),
            pltpu.VMEM((width, rows), bf),
            pltpu.SemaphoreType.DMA((3,)),
        ],
        compiler_params=pltpu.CompilerParams(vmem_limit_bytes=63 * 2**20),
    )(length, x, og, whole, qkv_bias, inner_bias, vec)


def data_parallel(
    hidden_in, seq_lengths, w_query, b_query, w_key, w_value, b_value, w_out, b_out, norm1_gain, norm1_bias,
    w_inner, b_inner, w_outer, b_outer, norm2_gain, norm2_bias, out_grad,
):
    n_dp, n_t = lax.axis_size("dp"), lax.axis_size("tensor")
    rows, width = hidden_in.shape
    cols = w_query.shape[1]
    length = lax.dynamic_slice_in_dim(seq_lengths, lax.axis_index("tensor"), 1)
    packed = jnp.concatenate((w_query, w_key, w_value, w_out), axis=1)
    whole = gather_all(packed, w_inner, w_outer, n_dp, n_t)
    split = lambda a: a.reshape(n_t, 1, -1)
    zeros = jnp.zeros((n_t, 1, cols), jnp.float32)
    qkv_bias = jnp.concatenate((split(b_query), zeros, split(b_value), zeros), axis=2)
    vec = jnp.stack((b_outer, b_outer, b_out, norm1_gain, norm1_bias, norm2_gain, norm2_bias, b_out))
    y, grad_in, grads, sums = layer(length, hidden_in, out_grad, whole, qkv_bias, split(b_inner), vec)
    shards, sums = scatter_all(grads, sums.sum(axis=1), n_dp)
    heads = sums[V_BI + n_t :]
    join = lambda a: a.reshape(-1)
    gq, gk, gv, go = (shards[0, :, i * cols : (i + 1) * cols] for i in range(4))
    return (
        y, grad_in, gq, join(heads[:, :cols]), gk, gv, join(heads[:, 2 * cols : 3 * cols]), go, sums[V_BO], sums[V_G1], sums[V_B1],
        shards[1], join(sums[V_BI : V_BI + n_t]), shards[2], sums[V_BF], sums[V_G2], sums[V_B2],
    )


def solution(mesh):
    in_specs = (
        P(("dp", "tensor"), None),
        P("dp"),
        P("dp", "tensor"),
        P(),
        P("dp", "tensor"),
        P("dp", "tensor"),
        P(),
        P("dp", "tensor"),
        P(),
        P(),
        P(),
        P("dp", "tensor"),
        P(),
        P("dp", "tensor"),
        P(),
        P(),
        P(),
        P(("dp", "tensor"), None),
    )
    out_specs = (
        P(("dp", "tensor"), None),
        P(("dp", "tensor"), None),
        P("dp", "tensor"),
        P(),
        P("dp", "tensor"),
        P("dp", "tensor"),
        P(),
        P("dp", "tensor"),
        P(),
        P(),
        P(),
        P("dp", "tensor"),
        P(),
        P("dp", "tensor"),
        P(),
        P(),
        P(),
    )
    small = mesh.shape["dp"] == 2 * Z_SIZE and mesh.shape["tensor"] == 4
    return jax.shard_map(
        data_parallel if small else per_device, mesh=mesh, in_specs=in_specs, out_specs=out_specs, check_vma=False
    )
```

```python
import functools

import jax
import jax.numpy as jnp
from jax import lax
from jax.experimental import pallas as pl
from jax.experimental.pallas import tpu as pltpu
from jax.sharding import PartitionSpec as P

HEAD_DIM = 64


NEG_FILL = -1000000000.0
NORM_EPS = 1e-12


def layer_norm(residual, norm_gain, norm_bias):
    centre = residual - jnp.mean(residual, axis=-1, keepdims=True)
    spread = jnp.mean(centre * centre, axis=-1, keepdims=True)
    return centre * lax.rsqrt(spread + NORM_EPS) * norm_gain + norm_bias


def exact_gelu(values):
    return jax.nn.gelu(values, approximate=False)


def contract_last(first_op, second_op):
    return lax.dot_general(
        first_op, second_op, (((1,), (1,)), ((), ())), preferred_element_type=jnp.float32
    )


def contract_first(first_op, second_op):
    return lax.dot_general(
        first_op, second_op, (((0,), (0,)), ((), ())), preferred_element_type=jnp.float32
    )


def split_blocks(heads_arr, block_rows):
    batches, length, head_size = heads_arr.shape
    return heads_arr.reshape(batches, length // block_rows, block_rows, head_size).transpose(
        1, 0, 2, 3
    )


def join_blocks(block_array):
    block_count, batches, block_rows, head_size = block_array.shape
    return block_array.transpose(1, 0, 2, 3).reshape(batches, block_count * block_rows, head_size)


def block_scores(query_portion, key_head_tensor, key_valid, score_scale):
    scores = (
        jnp.einsum(
            "eix,evx->eiv", query_portion, key_head_tensor, preferred_element_type=jnp.float32
        )
        * score_scale
    )
    return jnp.where(key_valid[:, None, :], scores, NEG_FILL)


def attend(query_heads, key_head_tensor, value_head_tensor, key_valid, block_rows, score_scale):

    def one_block(query_portion):
        scores = block_scores(query_portion, key_head_tensor, key_valid, score_scale)
        row_max = jnp.max(scores, axis=-1, keepdims=True)
        exponent = jnp.exp(scores - row_max)
        row_total = jnp.sum(exponent, axis=-1, keepdims=True)
        softmax_reduced = (exponent / row_total).astype(jnp.bfloat16)
        mixture = jnp.einsum(
            "fwj,fjt->fwt", softmax_reduced, value_head_tensor, preferred_element_type=jnp.float32
        )
        return (mixture.astype(jnp.bfloat16), row_max, row_total)

    mixture, row_max, row_total = lax.map(one_block, split_blocks(query_heads, block_rows))
    return (join_blocks(mixture), row_max, row_total)


def attend_back(
    query_heads,
    key_head_tensor,
    value_head_tensor,
    grad_heads,
    row_max,
    row_total,
    key_valid,
    block_rows,
    score_scale,
):

    def one_block(running, block_in):
        key_grad, value_grad = running
        query_portion, gradient_portion, max_part, total_part = block_in
        scores = block_scores(query_portion, key_head_tensor, key_valid, score_scale)
        softmax = jnp.exp(scores - max_part) / total_part
        softmax_reduced = softmax.astype(jnp.bfloat16)
        soft_grad = jnp.einsum(
            "eix,evx->eiv", gradient_portion, value_head_tensor, preferred_element_type=jnp.float32
        )
        centre = jnp.sum(softmax * soft_grad, axis=-1, keepdims=True)
        score_gradient = (softmax * (soft_grad - centre)).astype(jnp.bfloat16)
        query_grad = (
            jnp.einsum(
                "fwj,fjt->fwt", score_gradient, key_head_tensor, preferred_element_type=jnp.float32
            )
            * score_scale
        )
        key_grad = (
            key_grad
            + jnp.einsum(
                "oxl,oxn->oln", score_gradient, query_portion, preferred_element_type=jnp.float32
            )
            * score_scale
        )
        value_grad = value_grad + jnp.einsum(
            "oxl,oxn->oln", softmax_reduced, gradient_portion, preferred_element_type=jnp.float32
        )
        return ((key_grad, value_grad), query_grad)

    zero_grads = jnp.zeros(key_head_tensor.shape, jnp.float32)
    block_inputs = (
        split_blocks(query_heads, block_rows),
        split_blocks(grad_heads, block_rows),
        row_max,
        row_total,
    )
    (key_grad, value_grad), query_grad = lax.scan(one_block, (zero_grads, zero_grads), block_inputs)
    return (join_blocks(query_grad), key_grad, value_grad)


def per_device(
    hidden_in,
    seq_lengths,
    w_query,
    b_query,
    w_key,
    w_value,
    b_value,
    w_out,
    b_out,
    norm1_gain,
    norm1_bias,
    w_inner,
    b_inner,
    w_outer,
    b_outer,
    norm2_gain,
    norm2_bias,
    out_grad,
):
    tensor_size = lax.axis_size("tensor")
    tensor_place = lax.axis_index("tensor")
    local_rows, feature_width = hidden_in.shape
    group_rows = local_rows * tensor_size
    seq_count = seq_lengths.shape[0]
    seq_len = group_rows // seq_count
    head_cols = w_query.shape[1]
    inner_cols = w_inner.shape[1]
    heads_here = head_cols // HEAD_DIM
    block_rows = min(512, seq_len)
    score_scale = HEAD_DIM ** (-0.5)
    local_start = tensor_place * local_rows
    row_index = lax.iota(jnp.int32, group_rows)
    seq_match = (row_index[:, None] // seq_len == lax.iota(jnp.int32, seq_count)[None, :]).astype(
        jnp.int32
    )
    row_limit = jnp.sum(seq_match * seq_lengths[None, :], axis=1)
    row_valid = row_index % seq_len < row_limit
    local_mask = lax.dynamic_slice_in_dim(row_valid, local_start, local_rows).astype(jnp.float32)[
        :, None
    ]
    key_valid = jnp.repeat(row_valid.reshape(seq_count, seq_len), heads_here, axis=0)

    def heads_of(matrix):
        shaped = matrix.reshape(seq_count, seq_len, heads_here, HEAD_DIM).transpose(0, 2, 1, 3)
        return shaped.reshape(seq_count * heads_here, seq_len, HEAD_DIM)

    def rows_of(matrix):
        shaped = matrix.reshape(seq_count, heads_here, seq_len, HEAD_DIM).transpose(0, 2, 1, 3)
        return shaped.reshape(group_rows, head_cols)

    full_query, full_key, full_value, full_out, full_inner, full_outer = (
        lax.all_gather(w_query, "dp", axis=0, tiled=True),
        lax.all_gather(w_key, "dp", axis=0, tiled=True),
        lax.all_gather(w_value, "dp", axis=0, tiled=True),
        lax.all_gather(w_out, "dp", axis=0, tiled=True),
        lax.all_gather(w_inner, "dp", axis=0, tiled=True),
        lax.all_gather(w_outer, "dp", axis=0, tiled=True),
    )
    joint_weight = jnp.concatenate((full_query, full_key, full_value), axis=1)
    query_bias = lax.dynamic_slice_in_dim(b_query, tensor_place * head_cols, head_cols)
    value_bias = lax.dynamic_slice_in_dim(b_value, tensor_place * head_cols, head_cols)
    inner_bias = lax.dynamic_slice_in_dim(b_inner, tensor_place * inner_cols, inner_cols)
    joint_bias = jnp.concatenate((query_bias, jnp.zeros((head_cols,), jnp.float32), value_bias))
    whole_in = lax.all_gather(hidden_in, "tensor", axis=0, tiled=True)
    joint_rows = (
        jnp.dot(whole_in, joint_weight, preferred_element_type=jnp.float32) + joint_bias
    ).astype(jnp.bfloat16)
    query_heads = heads_of(joint_rows[:, :head_cols])
    key_head_tensor = heads_of(joint_rows[:, head_cols : 2 * head_cols])
    value_head_tensor = heads_of(joint_rows[:, 2 * head_cols :])
    mixture_heads, row_max, row_total = attend(
        query_heads, key_head_tensor, value_head_tensor, key_valid, block_rows, score_scale
    )
    mixture = rows_of(mixture_heads)
    summed_out = lax.psum_scatter(
        contract_last(mixture, full_out).astype(jnp.bfloat16),
        "tensor",
        scatter_dimension=0,
        tiled=True,
    ).astype(jnp.float32)
    first_sum = hidden_in.astype(jnp.float32) + (summed_out + b_out)
    first_norm = layer_norm(first_sum, norm1_gain, norm1_bias)
    mid_whole = lax.all_gather(first_norm.astype(jnp.bfloat16), "tensor", axis=0, tiled=True)
    pre_act = jnp.dot(mid_whole, full_inner, preferred_element_type=jnp.float32) + inner_bias
    act_low = exact_gelu(pre_act).astype(jnp.bfloat16)
    second_sum = first_norm + (
        lax.psum_scatter(
            contract_last(act_low, full_outer).astype(jnp.bfloat16),
            "tensor",
            scatter_dimension=0,
            tiled=True,
        ).astype(jnp.float32)
        + b_outer
    )
    normed, norm2_back = jax.vjp(layer_norm, second_sum, norm2_gain, norm2_bias)
    layer_out = (normed * local_mask).astype(jnp.bfloat16)
    out_cot = out_grad.astype(jnp.float32) * local_mask
    dsecond, gain2_part, bias2_part = norm2_back(out_cot)
    dffn_low = dsecond.astype(jnp.bfloat16)
    outer_bias_part = jnp.sum(dffn_low, axis=0, dtype=jnp.float32)
    dffn_whole = lax.all_gather(dffn_low, "tensor", axis=0, tiled=True)
    grad_outer = contract_first(dffn_whole, act_low)
    dact = jnp.dot(dffn_whole, full_outer, preferred_element_type=jnp.float32)
    _, gelu_back = jax.vjp(exact_gelu, pre_act)
    dpre_low = gelu_back(dact)[0].astype(jnp.bfloat16)
    inner_bias_part = jnp.sum(dpre_low, axis=0, dtype=jnp.float32)
    grad_inner = contract_first(mid_whole, dpre_low)
    dfirst_norm = dsecond + lax.psum_scatter(
        contract_last(dpre_low, full_inner).astype(jnp.bfloat16),
        "tensor",
        scatter_dimension=0,
        tiled=True,
    ).astype(jnp.float32)
    _, norm1_back = jax.vjp(layer_norm, first_sum, norm1_gain, norm1_bias)
    dfirst, gain1_part, bias1_part = norm1_back(dfirst_norm)
    dattn_low = dfirst.astype(jnp.bfloat16)
    out_bias_part = jnp.sum(dattn_low, axis=0, dtype=jnp.float32)
    dattn_whole = lax.all_gather(dattn_low, "tensor", axis=0, tiled=True)
    grad_out_w = contract_first(dattn_whole, mixture)
    dmixture = jnp.dot(dattn_whole, full_out, preferred_element_type=jnp.float32).astype(
        jnp.bfloat16
    )
    dquery_heads, dkey_heads, dvalue_heads = attend_back(
        query_heads,
        key_head_tensor,
        value_head_tensor,
        heads_of(dmixture),
        row_max,
        row_total,
        key_valid,
        block_rows,
        score_scale,
    )
    djoint = jnp.concatenate(
        (rows_of(dquery_heads), rows_of(dkey_heads), rows_of(dvalue_heads)), axis=1
    ).astype(jnp.bfloat16)
    joint_bias_part = jnp.sum(djoint, axis=0, dtype=jnp.float32)
    grad_joint = contract_first(whole_in, djoint)
    grad_in = dfirst + lax.psum_scatter(
        contract_last(djoint, joint_weight).astype(jnp.bfloat16),
        "tensor",
        scatter_dimension=0,
        tiled=True,
    ).astype(jnp.float32)
    grad_query = grad_joint[:, :head_cols]
    grad_key = grad_joint[:, head_cols : 2 * head_cols]
    grad_value = grad_joint[:, 2 * head_cols :]
    shard_grads = tuple(
        (
            lax.psum_scatter(grad_query, "dp", scatter_dimension=0, tiled=True),
            lax.psum_scatter(grad_key, "dp", scatter_dimension=0, tiled=True),
            lax.psum_scatter(grad_value, "dp", scatter_dimension=0, tiled=True),
            lax.psum_scatter(grad_out_w, "dp", scatter_dimension=0, tiled=True),
            lax.psum_scatter(grad_inner, "dp", scatter_dimension=0, tiled=True),
            lax.psum_scatter(grad_outer, "dp", scatter_dimension=0, tiled=True),
        )
    )

    def placed(vector, total_len):
        return lax.dynamic_update_slice_in_dim(
            jnp.zeros((total_len,), jnp.float32), vector, tensor_place * vector.shape[0], 0
        )

    query_bias_part = placed(joint_bias_part[:head_cols], feature_width)
    value_bias_part = placed(joint_bias_part[2 * head_cols :], feature_width)
    hidden_bias_part = placed(inner_bias_part, b_inner.shape[0])
    vector_sums = lax.psum(
        (
            query_bias_part,
            value_bias_part,
            out_bias_part,
            gain1_part,
            bias1_part,
            hidden_bias_part,
            outer_bias_part,
            gain2_part,
            bias2_part,
        ),
        ("dp", "tensor"),
    )
    return (
        layer_out,
        grad_in,
        shard_grads[0],
        vector_sums[0],
        shard_grads[1],
        shard_grads[2],
        vector_sums[1],
        shard_grads[3],
        vector_sums[2],
        vector_sums[3],
        vector_sums[4],
        shard_grads[4],
        vector_sums[5],
        shard_grads[5],
        vector_sums[6],
        vector_sums[7],
        vector_sums[8],
    )


Z_SIZE = 4
MESH_IDS = pl.DeviceIdType.MESH


def flip(place, bit):
    return place + bit - 2 * place * bit


class Place:
    def __init__(self):
        self.dp = lax.axis_index("dp")
        self.t = lax.axis_index("tensor")
        self.z = self.dp // 2
        self.x = self.dp % 2
        self.y = self.t // 2
        self.c = self.t % 2

    def chip(self, dz, da, db):
        c = self.c
        z = lax.rem(self.z - dz + Z_SIZE, Z_SIZE)
        x = flip(self.x, da * c + db * (1 - c))
        y = flip(self.y, da * (1 - c) + db * c)
        return z * 2 + x, y

    def device(self, dz=0, da=0, db=0, other=False):
        dp, y = self.chip(dz, da, db)
        core = 1 - self.c if other else self.c
        return {"dp": dp, "tensor": y * 2 + core}


def block_of(ref, m, dp, t, rows):
    return ref.at[m, t, pl.ds(pl.multiple_of(dp * rows, rows), rows), :]


def meet(me):
    barrier = pltpu.get_barrier_semaphore()
    peers = [me.device(dz=k) for k in range(1, Z_SIZE)]
    peers += [me.device(da=1), me.device(db=1), me.device(other=True)]
    for peer in peers:
        pl.semaphore_signal(barrier, inc=1, device_id=peer, device_id_type=MESH_IDS)
    pl.semaphore_wait(barrier, len(peers))


def remote(src, dst, send, recv, peer):
    return pltpu.make_async_remote_copy(
        src_ref=src, dst_ref=dst, send_sem=send, recv_sem=recv, device_id=peer, device_id_type=MESH_IDS
    )


class Gather:
    def __init__(self, me, shards, w, send_sem, recv_sem, local_sem):
        self.me, self.shards, self.w = me, shards, w
        self.send_sem, self.recv_sem, self.local_sem = send_sem, recv_sem, local_sem
        self.rows = shards[0].shape[0]

    def block(self, m, chip, core):
        return block_of(self.w, m, chip[0], chip[1] * 2 + core, self.rows)

    def send(self, m, slot, src, chip, peer):
        dst = self.block(m, chip, self.me.c)
        remote(src, dst, self.send_sem.at[m, slot], self.recv_sem.at[m, slot], peer).start()

    def own(self, m, slot, peer):
        self.send(m, slot, self.shards[m], self.me.chip(0, 0, 0), peer)

    def forward(self, m, slot, dz, da, db, peer):
        chip = self.me.chip(dz, da, db)
        self.send(m, slot, self.block(m, chip, self.me.c), chip, peer)

    def slot(self, m, slot):
        one = block_of(self.w, m, 0, 0, self.rows)
        return remote(one, one, self.send_sem.at[m, slot], self.recv_sem.at[m, slot], self.me.device(db=1))

    def local(self, m):
        me = self.me
        dst = block_of(self.w, m, me.dp, me.t, self.rows)
        return pltpu.make_async_copy(self.shards[m], dst, self.local_sem.at[m])

    def begin(self):
        me = self.me
        for m in range(3):
            for k in range(1, Z_SIZE):
                self.own(m, k, me.device(dz=Z_SIZE - k))
            self.own(m, 4, me.device(da=1))
            self.own(m, 8, me.device(db=1))
            self.own(m, 16, me.device(other=True))
            self.local(m).start()

    def pump(self, m, s):
        me = self.me
        self.slot(m, s).wait_recv()

        @pl.when(s < 4)
        def _():
            self.forward(m, 4 + s, s, 0, 0, me.device(da=1))
            self.forward(m, 8 + 2 * s, s, 0, 0, me.device(db=1))
            self.forward(m, 16 + 4 * s, s, 0, 0, me.device(other=True))

        @pl.when((s >= 4) & (s < 8))
        def _():
            k = s - 4
            self.forward(m, 9 + 2 * k, k, 1, 0, me.device(db=1))
            self.forward(m, 18 + 4 * k, k, 1, 0, me.device(other=True))

        @pl.when(s >= 8)
        def _():
            k = s - 8
            self.forward(m, 17 + 2 * k, k // 2, k % 2, 1, me.device(other=True))

    def pumps(self, m, first, last):
        @pl.loop(first, last)
        def _(s):
            self.pump(m, s)

    def collect(self, m):
        self.local(m).wait()

        @pl.loop(16, 32)
        def _(s):
            self.slot(m, s).wait_recv()

    def drain(self):
        for m in range(3):

            @pl.loop(1, 32)
            def _(s):
                self.slot(m, s).wait_send()


class Scatter:
    def __init__(self, me, w, core_buf, b_buf, a_buf, z_buf, send_sem, recv_sem):
        self.me, self.w = me, w
        self.core_buf, self.b_buf, self.a_buf, self.z_buf = core_buf, b_buf, a_buf, z_buf
        self.send_sem, self.recv_sem = send_sem, recv_sem
        self.rows = z_buf.shape[2]

    def order(self, i):
        me = self.me
        mine = i // 2
        core = flip(1 - me.c, mine)
        return flip(me.y, 1 - i % 2) * 2 + core

    def part(self, m, dz, da, db, core):
        dp, y = self.me.chip(dz, da, db)
        return block_of(self.w, m, dp, y * 2 + core, self.rows)

    def wait(self, m, slot):
        one = self.z_buf.at[m, 1]
        return remote(one, one, self.send_sem.at[m, slot], self.recv_sem.at[m, slot], self.me.device(db=1))

    def go(self, m, slot, src, dst, peer):
        remote(src, dst, self.send_sem.at[m, slot], self.recv_sem.at[m, slot], peer).start()

    def from_core(self, dz, da, db):
        return 4 * dz + 2 * db + da

    def ready(self, m, i):
        me = self.me
        c = me.c
        side = 1 - i % 2

        @pl.when(i < 2)
        def _():
            @pl.loop(0, 8)
            def _(s):
                dz, other = s // 2, s % 2
                da = side * (1 - c) + other * c
                db = other * (1 - c) + side * c
                slot = 4 * dz + 2 * da + db
                self.go(m, slot, self.part(m, dz, da, db, 1 - c), self.core_buf.at[m, slot], me.device(other=True))

        @pl.when(i >= 2)
        def _():
            @pl.loop(0, 8)
            def _(s):
                dz, other = s // 2, s % 2
                da = side * (1 - c) + other * c
                db = other * (1 - c) + side * c
                slot = self.from_core(dz, da, db)
                self.wait(m, slot).wait_recv()
                self.core_buf[m, slot] = self.part(m, dz, da, db, c)[...] + self.core_buf[m, slot]

                @pl.when(db == 1)
                def _():
                    place = 2 * dz + da
                    self.go(m, 16 + place, self.core_buf.at[m, slot], self.b_buf.at[m, place], me.device(db=1))

    def b_step(self, m, k):
        for da in (1, 0):
            self.wait(m, 16 + 2 * k + da).wait_recv()
            self.b_buf[m, 2 * k + da] = self.b_buf[m, 2 * k + da] + self.core_buf[m, self.from_core(k, da, 0)]
            if da:
                self.go(m, 24 + k, self.b_buf.at[m, 2 * k + 1], self.a_buf.at[m, k], self.me.device(da=1))

    def a_step(self, m, k):
        self.wait(m, 24 + k).wait_recv()
        self.a_buf[m, k] = self.a_buf[m, k] + self.b_buf[m, 2 * k]

        @pl.when(k > 0)
        def _():
            self.go(m, 28 + k, self.a_buf.at[m, k], self.z_buf.at[m, k], self.me.device(dz=k))

    def steps(self, step, m):
        @pl.loop(0, Z_SIZE)
        def _(k):
            step(m, k)

    def finish(self, m, out_ref):
        total = self.a_buf[m, 0].astype(jnp.float32)
        for k in range(1, Z_SIZE):
            self.wait(m, 28 + k).wait_recv()
            total = total + self.z_buf[m, k].astype(jnp.float32)
        out_ref[m] = total

    def drain(self):
        for m in range(3):

            @pl.loop(0, 28)
            def _(s):
                self.wait(m, s).wait_send()

            @pl.loop(29, 32)
            def _(s):
                self.wait(m, s).wait_send()


class VectorSum:
    def __init__(self, me, buf, zbuf, send_sem, recv_sem):
        self.me, self.buf, self.zbuf, self.send_sem, self.recv_sem = me, buf, zbuf, send_sem, recv_sem

    def copy(self, step, src, dst, peer):
        return remote(src, dst, self.send_sem.at[step], self.recv_sem.at[step], peer)

    def peer(self, step):
        me = self.me
        if step == 0:
            return me.device(other=True)
        dx, dy = ((1, 0), (0, 1))[step - 1]
        return {"dp": me.z * 2 + flip(me.x, dx), "tensor": 2 * flip(me.y, dy) + me.c}

    def pair(self, step):
        return self.copy(step, self.buf.at[2 * step], self.buf.at[2 * step + 1], self.peer(step))

    def start(self, value):
        self.buf[0] = value
        self.pair(0).start()

    def advance(self, step):
        self.pair(step).wait()
        self.buf[2 * step + 2] = self.buf[2 * step] + self.buf[2 * step + 1]
        if step < 2:
            self.pair(step + 1).start()
        else:
            self.zbuf[self.me.z] = self.buf[6]
            for k in range(1, Z_SIZE):
                self.z_copy(k).start()

    def z_copy(self, k):
        return self.copy(2 + k, self.buf.at[6], self.zbuf.at[self.me.z], self.me.device(dz=k))

    def result(self):
        for k in range(1, Z_SIZE):
            self.z_copy(k).wait()
        return (self.zbuf[0] + self.zbuf[1]) + (self.zbuf[2] + self.zbuf[3])


def dot_nn(a, b):
    return lax.dot_general(a, b, (((1,), (0,)), ((), ())), preferred_element_type=jnp.float32)


def dot_nt(a, b):
    return lax.dot_general(a, b, (((1,), (1,)), ((), ())), preferred_element_type=jnp.float32)


def dot_tn(a, b):
    return lax.dot_general(a, b, (((0,), (0,)), ((), ())), preferred_element_type=jnp.float32)


def low(a):
    return a.astype(jnp.bfloat16)


def row_mean(a):
    return jnp.mean(a, axis=-1, keepdims=True)


def normalise(r):
    centre = r - row_mean(r)
    inverse = lax.rsqrt(row_mean(centre * centre) + NORM_EPS)
    return centre * inverse, inverse


def norm_back(g, z, inverse):
    return (g - row_mean(g) - z * row_mean(g * z)) * inverse


def gelu_pair(u):
    cdf = 0.5 + 0.5 * lax.erf(u * (0.5**0.5))
    density = jnp.exp(-0.5 * u * u) * ((0.5 / jnp.pi) ** 0.5)
    return u * cdf, cdf + u * density


V_BQ, V_BV, V_BO, V_G1, V_B1, V_BF, V_G2, V_B2, V_BI = range(9)
TILE = 64


class Layer:
    def __init__(self, **refs):
        self.__dict__.update(refs)
        self.rows, self.width = self.x.shape
        self.n_t = self.w.shape[1]
        self.cols = self.width // self.n_t
        self.heads = self.cols // HEAD_DIM
        self.ocol = (3 * self.cols) // 128 * 128

    def tiles(self, body):
        @pl.loop(0, self.rows // TILE)
        def _(i):
            body(pl.ds(pl.multiple_of(i * TILE, TILE), TILE))

    def project(self, t):
        lane = lax.broadcasted_iota(jnp.int32, (1, self.width), 1)
        out = dot_nn(self.x[...], self.w[0, t]) + self.qkv_bias[t]
        self.qkv[t] = low(jnp.where(lane < 3 * self.cols, out, 0.0))

    def piece(self, t, which, j):
        first = which * self.cols + j * HEAD_DIM
        return self.qkv.at[t, :, first : first + HEAD_DIM]

    def attend(self, t, valid, between):
        self.att[t, :, : HEAD_DIM] = jnp.zeros((self.rows, HEAD_DIM), jnp.bfloat16)
        for j in range(self.heads):
            q, k, v = (self.piece(t, i, j)[...] for i in range(3))
            s = dot_nt(k, q * jnp.bfloat16(HEAD_DIM**-0.5))
            s = jnp.where(valid, s, NEG_FILL)
            e = jnp.exp(s - jnp.max(s, axis=0, keepdims=True))
            p = low(e * (1.0 / jnp.sum(e, axis=0, keepdims=True)))
            self.p[t * self.heads + j] = p
            mix = dot_tn(v, p)
            first = 3 * self.cols - self.ocol + j * HEAD_DIM
            self.att[t, :, first : first + HEAD_DIM] = low(mix.T)
            between(j)

    def out_project(self, t):
        self.acc[...] += dot_nt(self.att[t], self.w[0, t, :, self.ocol :])

    def start_residual(self):
        self.acc[...] = self.x[...].astype(jnp.float32) + self.vec[2:3, :]

    def first_norm(self):
        def body(r):
            z, inverse = normalise(self.acc[r, :])
            self.z1[r, :] = z
            self.inv1[r, :] = jnp.broadcast_to(inverse, (TILE, 128))
            h1 = z * self.vec[3:4, :] + self.vec[4:5, :]
            self.h1b[r, :] = low(h1)
            self.acc[r, :] = h1 + self.vec[0:1, :]

        self.tiles(body)

    def inner(self, t):
        @pl.loop(0, self.rows // 128)
        def _(i):
            r = pl.ds(pl.multiple_of(i * 128, 128), 128)
            pre = dot_nn(self.h1b[r, :], self.w[1, t]) + self.inner_bias[t]
            act, slope = gelu_pair(pre)
            self.act[t, r, :] = low(act)
            self.slope[t, r, :] = low(slope)

    def outer(self, t):
        self.acc[...] += dot_nt(self.act[t], self.w[2, t])

    def second_norm(self, length):
        self.sums[...] = jnp.zeros_like(self.sums)

        def body(r):
            z, inverse = normalise(self.acc[r, :])
            place = r.start + lax.broadcasted_iota(jnp.int32, (TILE, 1), 0)
            mask = (place < length).astype(jnp.float32)
            gain = self.vec[5:6, :]
            self.y[r, :] = low((z * gain + self.vec[6:7, :]) * mask)
            dy = self.og[r, :].astype(jnp.float32) * mask
            dr2 = norm_back(dy * gain, z, inverse)
            self.acc[r, :] = dr2
            df = low(dr2)
            self.df[r, :] = df
            self.sums[V_G2] += fold(dy * z)
            self.sums[V_B2] += fold(dy)
            self.sums[V_BF] += fold(df.astype(jnp.float32))

        self.tiles(body)

    def outer_back(self, t):
        self.dact[...] = dot_nn(self.df[...], self.w[2, t])

        def body(r):
            d = low(self.dact[r, :] * self.slope[t, r, :].astype(jnp.float32))
            self.slope[t, r, :] = d
            self.sums[V_BI + t] += fold(d.astype(jnp.float32))

        self.tiles(body)
        self.w[2, t] = low(dot_nn(self.df_t[...], self.act[t]))

    def inner_back(self, t):
        self.acc[...] += dot_nt(self.slope[t], self.w[1, t])
        self.w[1, t] = low(dot_nn(self.h1b_t[...], self.slope[t]))

    def first_norm_back(self):
        def body(r):
            z = self.z1[r, :]
            dh1 = self.acc[r, :]
            self.sums[V_G1] += fold(dh1 * z)
            self.sums[V_B1] += fold(dh1)
            dr1 = norm_back(dh1 * self.vec[3:4, :], z, self.inv1[r, :1])
            self.acc[r, :] = dr1
            dob = low(dr1)
            self.df[r, :] = dob
            self.sums[V_BO] += fold(dob.astype(jnp.float32))

        self.tiles(body)

    def attend_back(self, t, between):
        scale = HEAD_DIM**-0.5
        self.datt[...] = low(dot_nn(self.df[...], self.w[0, t, :, self.ocol :]))
        for j in range(self.heads):
            first = 3 * self.cols - self.ocol + j * HEAD_DIM
            d = self.datt[:, first : first + HEAD_DIM]
            q, k, v = (self.piece(t, i, j)[...] for i in range(3))
            p = self.p[t * self.heads + j]
            dp = dot_nt(v, d)
            pf = p.astype(jnp.float32)
            delta = jnp.sum(pf * dp, axis=0, keepdims=True)
            ds = low(pf * (dp - delta))
            self.piece(t, 2, j)[...] = low(dot_nn(p, d))
            self.piece(t, 1, j)[...] = low(dot_nn(ds, q) * scale)
            self.piece(t, 0, j)[...] = low((dot_tn(k, ds) * scale).T)
            between(j)

    def project_back(self, t):
        self.acc[...] += dot_nt(self.qkv[t], self.w[0, t])

        def body(r):
            self.sums[V_BI + self.n_t + t] += fold(self.qkv[t, r, :].astype(jnp.float32))

        self.tiles(body)
        self.w[0, t] = low(dot_nn(self.x_t[...], self.qkv[t]))
        out = self.w.at[0, t, :, self.ocol :]
        out[...] = low(out[...].astype(jnp.float32) + dot_nn(self.df_t[...], self.att[t]))

    def transpose(self, src, dst):
        dst[...] = src[...].T


def fold(a):
    return jnp.sum(a.reshape(a.shape[0] // 8, 8, a.shape[1]), axis=0)


def step_kernel(
    length_ref, x_ref, og_ref, packed_ref, wi_ref, wo_ref, qkv_bias, inner_bias, vec_ref,
    y_ref, acc_ref, out_ref, vout_ref,
    w, sums, qkv, p, att, z1, inv1, h1b, act, slope, df, datt, dact, x_t, h1b_t, df_t,
    core_buf, b_buf, a_buf, z_buf, vec_buf, vec_z,
    gather_send, gather_recv, local_sem, send_sem, recv_sem, vec_send, vec_recv,
):
    me = Place()
    gather = Gather(me, (packed_ref, wi_ref, wo_ref), w, gather_send, gather_recv, local_sem)
    scatter = Scatter(me, w, core_buf, b_buf, a_buf, z_buf, send_sem, recv_sem)
    small = VectorSum(me, vec_buf, vec_z, vec_send, vec_recv)
    meet(me)
    gather.begin()
    a = Layer(
        x=x_ref, og=og_ref, w=w, qkv_bias=qkv_bias, inner_bias=inner_bias, vec=vec_ref, y=y_ref, acc=acc_ref, sums=sums,
        qkv=qkv, p=p, att=att, z1=z1, inv1=inv1, h1b=h1b, act=act, slope=slope, df=df, datt=datt, dact=dact, x_t=x_t, h1b_t=h1b_t, df_t=df_t,
    )
    length = length_ref[0]
    valid = lax.broadcasted_iota(jnp.int32, (a.rows, 1), 0) < length
    a.transpose(a.x, a.x_t)
    a.start_residual()
    gather.pumps(0, 1, 16)
    gather.collect(0)

    @pl.loop(0, a.n_t)
    def _(t):
        a.project(t)
        a.attend(t, valid, lambda j: gather.pump(1, a.heads * t + j + 1))
        a.out_project(t)

    gather.pumps(1, 1 + a.n_t * a.heads, 16)
    a.first_norm()
    a.transpose(a.h1b, a.h1b_t)
    gather.pumps(2, 1, 4)
    gather.collect(1)

    @pl.loop(0, a.n_t)
    def _(t):
        gather.pumps(2, 4 + 3 * t, 7 + 3 * t)
        a.inner(t)

    gather.collect(2)

    @pl.loop(0, a.n_t)
    def _(t):
        a.outer(t)

    a.second_norm(length)
    a.transpose(a.df, a.df_t)
    gather.drain()

    @pl.loop(0, a.n_t)
    def _(i):
        a.outer_back(scatter.order(i))
        scatter.ready(2, i)

    @pl.loop(0, a.n_t)
    def _(i):
        a.inner_back(scatter.order(i))
        scatter.ready(1, i)

    a.first_norm_back()
    a.transpose(a.df, a.df_t)

    def between(i, j):
        n = a.heads * i + j

        @pl.when(n < 4)
        def _():
            scatter.b_step(2, n)

        @pl.when((n >= 4) & (n < 8))
        def _():
            scatter.a_step(2, n - 4)

        @pl.when((n >= 6) & (n < 10))
        def _():
            scatter.b_step(1, n - 6)

    @pl.loop(0, a.n_t)
    def _(i):
        t = scatter.order(i)
        a.attend_back(t, lambda j: between(i, j))
        a.project_back(t)
        scatter.ready(0, i)

    small.start(jnp.sum(sums[...], axis=1))
    scatter.steps(scatter.a_step, 1)
    small.advance(0)
    scatter.steps(scatter.b_step, 0)
    small.advance(1)
    scatter.steps(scatter.a_step, 0)
    small.advance(2)
    for m in (2, 1):
        scatter.finish(m, out_ref)
    vout_ref[...] = small.result()
    scatter.finish(0, out_ref)
    scatter.drain()


def step(length, x, og, packed, inner, outer, qkv_bias, inner_bias, vec, n_t):
    rows, width = x.shape
    cols = width // n_t
    heads = width // HEAD_DIM
    owidth = width - (3 * cols) // 128 * 128
    shard = packed.shape[0]
    bf, f32 = jnp.bfloat16, jnp.float32
    vmem = pl.BlockSpec(memory_space=pltpu.VMEM)
    n_v = V_BI + 2 * n_t
    n_w = shard * lax.axis_size("dp")
    buf = lambda n: pltpu.VMEM((3, n, shard, width), bf)
    dma = pltpu.SemaphoreType.DMA
    return pl.pallas_call(
        step_kernel,
        out_shape=(
            jax.ShapeDtypeStruct((rows, width), bf),
            jax.ShapeDtypeStruct((rows, width), f32),
            jax.ShapeDtypeStruct((3, shard, width), f32),
            jax.ShapeDtypeStruct((n_v, width), f32),
        ),
        in_specs=[pl.BlockSpec(memory_space=pltpu.SMEM)] + [vmem] * 8,
        out_specs=[vmem] * 4,
        scratch_shapes=[
            pltpu.VMEM((3, n_t, n_w, width), bf),
            pltpu.VMEM((n_v, 8, width), f32),
            pltpu.VMEM((n_t, rows, width), bf),
            pltpu.VMEM((heads, rows, rows), bf),
            pltpu.VMEM((n_t, rows, owidth), bf),
            pltpu.VMEM((rows, width), f32),
            pltpu.VMEM((rows, 128), f32),
            pltpu.VMEM((rows, width), bf),
            pltpu.VMEM((n_t, rows, width), bf),
            pltpu.VMEM((n_t, rows, width), bf),
            pltpu.VMEM((rows, width), bf),
            pltpu.VMEM((rows, owidth), bf),
            pltpu.VMEM((rows, width), f32),
            pltpu.VMEM((width, rows), bf),
            pltpu.VMEM((width, rows), bf),
            pltpu.VMEM((width, rows), bf),
            buf(16),
            buf(8),
            buf(4),
            buf(4),
            pltpu.VMEM((7, n_v, width), f32),
            pltpu.VMEM((Z_SIZE, n_v, width), f32),
            dma((3, 32)),
            dma((3, 32)),
            dma((3,)),
            dma((3, 32)),
            dma((3, 32)),
            dma((6,)),
            dma((6,)),
        ],
        compiler_params=pltpu.CompilerParams(collective_id=0, has_side_effects=True, vmem_limit_bytes=63 * 2**20),
    )(length, x, og, packed, inner, outer, qkv_bias, inner_bias, vec)


def data_parallel(
    hidden_in, seq_lengths, w_query, b_query, w_key, w_value, b_value, w_out, b_out, norm1_gain, norm1_bias,
    w_inner, b_inner, w_outer, b_outer, norm2_gain, norm2_bias, out_grad,
):
    n_t = lax.axis_size("tensor")
    cols = w_query.shape[1]
    length = lax.dynamic_slice_in_dim(seq_lengths, lax.axis_index("tensor"), 1)
    packed = jnp.concatenate((w_query, w_key, w_value, w_out), axis=1)
    split = lambda a: a.reshape(n_t, 1, -1)
    zeros = jnp.zeros((n_t, 1, cols), jnp.float32)
    qkv_bias = jnp.concatenate((split(b_query), zeros, split(b_value), zeros), axis=2)
    vec = jnp.stack((b_outer, b_outer, b_out, norm1_gain, norm1_bias, norm2_gain, norm2_bias, b_out))
    y, grad_in, shards, sums = step(
        length, hidden_in, out_grad, packed, w_inner, w_outer, qkv_bias, split(b_inner), vec, n_t
    )
    heads = sums[V_BI + n_t :]
    join = lambda a: a.reshape(-1)
    gq, gk, gv, go = (shards[0, :, i * cols : (i + 1) * cols] for i in range(4))
    return (
        y, grad_in, gq, join(heads[:, :cols]), gk, gv, join(heads[:, 2 * cols : 3 * cols]), go, sums[V_BO], sums[V_G1], sums[V_B1],
        shards[1], join(sums[V_BI : V_BI + n_t]), shards[2], sums[V_BF], sums[V_G2], sums[V_B2],
    )


def solution(mesh):
    in_specs = (
        P(("dp", "tensor"), None),
        P("dp"),
        P("dp", "tensor"),
        P(),
        P("dp", "tensor"),
        P("dp", "tensor"),
        P(),
        P("dp", "tensor"),
        P(),
        P(),
        P(),
        P("dp", "tensor"),
        P(),
        P("dp", "tensor"),
        P(),
        P(),
        P(),
        P(("dp", "tensor"), None),
    )
    out_specs = (
        P(("dp", "tensor"), None),
        P(("dp", "tensor"), None),
        P("dp", "tensor"),
        P(),
        P("dp", "tensor"),
        P("dp", "tensor"),
        P(),
        P("dp", "tensor"),
        P(),
        P(),
        P(),
        P("dp", "tensor"),
        P(),
        P("dp", "tensor"),
        P(),
        P(),
        P(),
    )
    small = mesh.shape["dp"] == 2 * Z_SIZE and mesh.shape["tensor"] == 4
    return jax.shard_map(
        data_parallel if small else per_device, mesh=mesh, in_specs=in_specs, out_specs=out_specs, check_vma=False
    )
```

```python
import functools

import jax
import jax.numpy as jnp
from jax import lax
from jax.experimental import pallas as pl
from jax.experimental.pallas import tpu as pltpu
from jax.sharding import PartitionSpec as P

HEAD_DIM = 64


NEG_FILL = -1000000000.0
NORM_EPS = 1e-12


def layer_norm(residual, norm_gain, norm_bias):
    centre = residual - jnp.mean(residual, axis=-1, keepdims=True)
    spread = jnp.mean(centre * centre, axis=-1, keepdims=True)
    return centre * lax.rsqrt(spread + NORM_EPS) * norm_gain + norm_bias


def exact_gelu(values):
    return jax.nn.gelu(values, approximate=False)


def contract_last(first_op, second_op):
    return lax.dot_general(
        first_op, second_op, (((1,), (1,)), ((), ())), preferred_element_type=jnp.float32
    )


def contract_first(first_op, second_op):
    return lax.dot_general(
        first_op, second_op, (((0,), (0,)), ((), ())), preferred_element_type=jnp.float32
    )


def split_blocks(heads_arr, block_rows):
    batches, length, head_size = heads_arr.shape
    return heads_arr.reshape(batches, length // block_rows, block_rows, head_size).transpose(
        1, 0, 2, 3
    )


def join_blocks(block_array):
    block_count, batches, block_rows, head_size = block_array.shape
    return block_array.transpose(1, 0, 2, 3).reshape(batches, block_count * block_rows, head_size)


def block_scores(query_portion, key_head_tensor, key_valid, score_scale):
    scores = (
        jnp.einsum(
            "eix,evx->eiv", query_portion, key_head_tensor, preferred_element_type=jnp.float32
        )
        * score_scale
    )
    return jnp.where(key_valid[:, None, :], scores, NEG_FILL)


def attend(query_heads, key_head_tensor, value_head_tensor, key_valid, block_rows, score_scale):

    def one_block(query_portion):
        scores = block_scores(query_portion, key_head_tensor, key_valid, score_scale)
        row_max = jnp.max(scores, axis=-1, keepdims=True)
        exponent = jnp.exp(scores - row_max)
        row_total = jnp.sum(exponent, axis=-1, keepdims=True)
        softmax_reduced = (exponent / row_total).astype(jnp.bfloat16)
        mixture = jnp.einsum(
            "fwj,fjt->fwt", softmax_reduced, value_head_tensor, preferred_element_type=jnp.float32
        )
        return (mixture.astype(jnp.bfloat16), row_max, row_total)

    mixture, row_max, row_total = lax.map(one_block, split_blocks(query_heads, block_rows))
    return (join_blocks(mixture), row_max, row_total)


def attend_back(
    query_heads,
    key_head_tensor,
    value_head_tensor,
    grad_heads,
    row_max,
    row_total,
    key_valid,
    block_rows,
    score_scale,
):

    def one_block(running, block_in):
        key_grad, value_grad = running
        query_portion, gradient_portion, max_part, total_part = block_in
        scores = block_scores(query_portion, key_head_tensor, key_valid, score_scale)
        softmax = jnp.exp(scores - max_part) / total_part
        softmax_reduced = softmax.astype(jnp.bfloat16)
        soft_grad = jnp.einsum(
            "eix,evx->eiv", gradient_portion, value_head_tensor, preferred_element_type=jnp.float32
        )
        centre = jnp.sum(softmax * soft_grad, axis=-1, keepdims=True)
        score_gradient = (softmax * (soft_grad - centre)).astype(jnp.bfloat16)
        query_grad = (
            jnp.einsum(
                "fwj,fjt->fwt", score_gradient, key_head_tensor, preferred_element_type=jnp.float32
            )
            * score_scale
        )
        key_grad = (
            key_grad
            + jnp.einsum(
                "oxl,oxn->oln", score_gradient, query_portion, preferred_element_type=jnp.float32
            )
            * score_scale
        )
        value_grad = value_grad + jnp.einsum(
            "oxl,oxn->oln", softmax_reduced, gradient_portion, preferred_element_type=jnp.float32
        )
        return ((key_grad, value_grad), query_grad)

    zero_grads = jnp.zeros(key_head_tensor.shape, jnp.float32)
    block_inputs = (
        split_blocks(query_heads, block_rows),
        split_blocks(grad_heads, block_rows),
        row_max,
        row_total,
    )
    (key_grad, value_grad), query_grad = lax.scan(one_block, (zero_grads, zero_grads), block_inputs)
    return (join_blocks(query_grad), key_grad, value_grad)


def per_device(
    hidden_in,
    seq_lengths,
    w_query,
    b_query,
    w_key,
    w_value,
    b_value,
    w_out,
    b_out,
    norm1_gain,
    norm1_bias,
    w_inner,
    b_inner,
    w_outer,
    b_outer,
    norm2_gain,
    norm2_bias,
    out_grad,
):
    tensor_size = lax.axis_size("tensor")
    tensor_place = lax.axis_index("tensor")
    local_rows, feature_width = hidden_in.shape
    group_rows = local_rows * tensor_size
    seq_count = seq_lengths.shape[0]
    seq_len = group_rows // seq_count
    head_cols = w_query.shape[1]
    inner_cols = w_inner.shape[1]
    heads_here = head_cols // HEAD_DIM
    block_rows = min(512, seq_len)
    score_scale = HEAD_DIM ** (-0.5)
    local_start = tensor_place * local_rows
    row_index = lax.iota(jnp.int32, group_rows)
    seq_match = (row_index[:, None] // seq_len == lax.iota(jnp.int32, seq_count)[None, :]).astype(
        jnp.int32
    )
    row_limit = jnp.sum(seq_match * seq_lengths[None, :], axis=1)
    row_valid = row_index % seq_len < row_limit
    local_mask = lax.dynamic_slice_in_dim(row_valid, local_start, local_rows).astype(jnp.float32)[
        :, None
    ]
    key_valid = jnp.repeat(row_valid.reshape(seq_count, seq_len), heads_here, axis=0)

    def heads_of(matrix):
        shaped = matrix.reshape(seq_count, seq_len, heads_here, HEAD_DIM).transpose(0, 2, 1, 3)
        return shaped.reshape(seq_count * heads_here, seq_len, HEAD_DIM)

    def rows_of(matrix):
        shaped = matrix.reshape(seq_count, heads_here, seq_len, HEAD_DIM).transpose(0, 2, 1, 3)
        return shaped.reshape(group_rows, head_cols)

    full_query, full_key, full_value, full_out, full_inner, full_outer = (
        lax.all_gather(w_query, "dp", axis=0, tiled=True),
        lax.all_gather(w_key, "dp", axis=0, tiled=True),
        lax.all_gather(w_value, "dp", axis=0, tiled=True),
        lax.all_gather(w_out, "dp", axis=0, tiled=True),
        lax.all_gather(w_inner, "dp", axis=0, tiled=True),
        lax.all_gather(w_outer, "dp", axis=0, tiled=True),
    )
    joint_weight = jnp.concatenate((full_query, full_key, full_value), axis=1)
    query_bias = lax.dynamic_slice_in_dim(b_query, tensor_place * head_cols, head_cols)
    value_bias = lax.dynamic_slice_in_dim(b_value, tensor_place * head_cols, head_cols)
    inner_bias = lax.dynamic_slice_in_dim(b_inner, tensor_place * inner_cols, inner_cols)
    joint_bias = jnp.concatenate((query_bias, jnp.zeros((head_cols,), jnp.float32), value_bias))
    whole_in = lax.all_gather(hidden_in, "tensor", axis=0, tiled=True)
    joint_rows = (
        jnp.dot(whole_in, joint_weight, preferred_element_type=jnp.float32) + joint_bias
    ).astype(jnp.bfloat16)
    query_heads = heads_of(joint_rows[:, :head_cols])
    key_head_tensor = heads_of(joint_rows[:, head_cols : 2 * head_cols])
    value_head_tensor = heads_of(joint_rows[:, 2 * head_cols :])
    mixture_heads, row_max, row_total = attend(
        query_heads, key_head_tensor, value_head_tensor, key_valid, block_rows, score_scale
    )
    mixture = rows_of(mixture_heads)
    summed_out = lax.psum_scatter(
        contract_last(mixture, full_out).astype(jnp.bfloat16),
        "tensor",
        scatter_dimension=0,
        tiled=True,
    ).astype(jnp.float32)
    first_sum = hidden_in.astype(jnp.float32) + (summed_out + b_out)
    first_norm = layer_norm(first_sum, norm1_gain, norm1_bias)
    mid_whole = lax.all_gather(first_norm.astype(jnp.bfloat16), "tensor", axis=0, tiled=True)
    pre_act = jnp.dot(mid_whole, full_inner, preferred_element_type=jnp.float32) + inner_bias
    act_low = exact_gelu(pre_act).astype(jnp.bfloat16)
    second_sum = first_norm + (
        lax.psum_scatter(
            contract_last(act_low, full_outer).astype(jnp.bfloat16),
            "tensor",
            scatter_dimension=0,
            tiled=True,
        ).astype(jnp.float32)
        + b_outer
    )
    normed, norm2_back = jax.vjp(layer_norm, second_sum, norm2_gain, norm2_bias)
    layer_out = (normed * local_mask).astype(jnp.bfloat16)
    out_cot = out_grad.astype(jnp.float32) * local_mask
    dsecond, gain2_part, bias2_part = norm2_back(out_cot)
    dffn_low = dsecond.astype(jnp.bfloat16)
    outer_bias_part = jnp.sum(dffn_low, axis=0, dtype=jnp.float32)
    dffn_whole = lax.all_gather(dffn_low, "tensor", axis=0, tiled=True)
    grad_outer = contract_first(dffn_whole, act_low)
    dact = jnp.dot(dffn_whole, full_outer, preferred_element_type=jnp.float32)
    _, gelu_back = jax.vjp(exact_gelu, pre_act)
    dpre_low = gelu_back(dact)[0].astype(jnp.bfloat16)
    inner_bias_part = jnp.sum(dpre_low, axis=0, dtype=jnp.float32)
    grad_inner = contract_first(mid_whole, dpre_low)
    dfirst_norm = dsecond + lax.psum_scatter(
        contract_last(dpre_low, full_inner).astype(jnp.bfloat16),
        "tensor",
        scatter_dimension=0,
        tiled=True,
    ).astype(jnp.float32)
    _, norm1_back = jax.vjp(layer_norm, first_sum, norm1_gain, norm1_bias)
    dfirst, gain1_part, bias1_part = norm1_back(dfirst_norm)
    dattn_low = dfirst.astype(jnp.bfloat16)
    out_bias_part = jnp.sum(dattn_low, axis=0, dtype=jnp.float32)
    dattn_whole = lax.all_gather(dattn_low, "tensor", axis=0, tiled=True)
    grad_out_w = contract_first(dattn_whole, mixture)
    dmixture = jnp.dot(dattn_whole, full_out, preferred_element_type=jnp.float32).astype(
        jnp.bfloat16
    )
    dquery_heads, dkey_heads, dvalue_heads = attend_back(
        query_heads,
        key_head_tensor,
        value_head_tensor,
        heads_of(dmixture),
        row_max,
        row_total,
        key_valid,
        block_rows,
        score_scale,
    )
    djoint = jnp.concatenate(
        (rows_of(dquery_heads), rows_of(dkey_heads), rows_of(dvalue_heads)), axis=1
    ).astype(jnp.bfloat16)
    joint_bias_part = jnp.sum(djoint, axis=0, dtype=jnp.float32)
    grad_joint = contract_first(whole_in, djoint)
    grad_in = dfirst + lax.psum_scatter(
        contract_last(djoint, joint_weight).astype(jnp.bfloat16),
        "tensor",
        scatter_dimension=0,
        tiled=True,
    ).astype(jnp.float32)
    grad_query = grad_joint[:, :head_cols]
    grad_key = grad_joint[:, head_cols : 2 * head_cols]
    grad_value = grad_joint[:, 2 * head_cols :]
    shard_grads = tuple(
        (
            lax.psum_scatter(grad_query, "dp", scatter_dimension=0, tiled=True),
            lax.psum_scatter(grad_key, "dp", scatter_dimension=0, tiled=True),
            lax.psum_scatter(grad_value, "dp", scatter_dimension=0, tiled=True),
            lax.psum_scatter(grad_out_w, "dp", scatter_dimension=0, tiled=True),
            lax.psum_scatter(grad_inner, "dp", scatter_dimension=0, tiled=True),
            lax.psum_scatter(grad_outer, "dp", scatter_dimension=0, tiled=True),
        )
    )

    def placed(vector, total_len):
        return lax.dynamic_update_slice_in_dim(
            jnp.zeros((total_len,), jnp.float32), vector, tensor_place * vector.shape[0], 0
        )

    query_bias_part = placed(joint_bias_part[:head_cols], feature_width)
    value_bias_part = placed(joint_bias_part[2 * head_cols :], feature_width)
    hidden_bias_part = placed(inner_bias_part, b_inner.shape[0])
    vector_sums = lax.psum(
        (
            query_bias_part,
            value_bias_part,
            out_bias_part,
            gain1_part,
            bias1_part,
            hidden_bias_part,
            outer_bias_part,
            gain2_part,
            bias2_part,
        ),
        ("dp", "tensor"),
    )
    return (
        layer_out,
        grad_in,
        shard_grads[0],
        vector_sums[0],
        shard_grads[1],
        shard_grads[2],
        vector_sums[1],
        shard_grads[3],
        vector_sums[2],
        vector_sums[3],
        vector_sums[4],
        shard_grads[4],
        vector_sums[5],
        shard_grads[5],
        vector_sums[6],
        vector_sums[7],
        vector_sums[8],
    )


Z_SIZE = 4
MESH_IDS = pl.DeviceIdType.MESH


def flip(place, bit):
    return place + bit - 2 * place * bit


class Place:
    def __init__(self):
        self.dp = lax.axis_index("dp")
        self.t = lax.axis_index("tensor")
        self.z = self.dp // 2
        self.x = self.dp % 2
        self.y = self.t // 2
        self.c = self.t % 2

    def chip(self, dz, da, db):
        c = self.c
        z = lax.rem(self.z - dz + Z_SIZE, Z_SIZE)
        x = flip(self.x, da * c + db * (1 - c))
        y = flip(self.y, da * (1 - c) + db * c)
        return z * 2 + x, y

    def device(self, dz=0, da=0, db=0, other=False):
        dp, y = self.chip(dz, da, db)
        core = 1 - self.c if other else self.c
        return {"dp": dp, "tensor": y * 2 + core}


def block_of(ref, m, dp, t, rows):
    return ref.at[m, t, pl.ds(pl.multiple_of(dp * rows, rows), rows), :]


def meet(me):
    barrier = pltpu.get_barrier_semaphore()
    peers = [me.device(dz=k) for k in range(1, Z_SIZE)]
    peers += [me.device(da=1), me.device(db=1), me.device(other=True)]
    for peer in peers:
        pl.semaphore_signal(barrier, inc=1, device_id=peer, device_id_type=MESH_IDS)
    pl.semaphore_wait(barrier, len(peers))


def remote(src, dst, send, recv, peer):
    return pltpu.make_async_remote_copy(
        src_ref=src, dst_ref=dst, send_sem=send, recv_sem=recv, device_id=peer, device_id_type=MESH_IDS
    )


def parse(steps):
    for step in steps:
        first, _, stop = step[3:].partition("-")
        for q in range(int(first or 0), int(stop or first or 0) + 1):
            yield step[0], int(step[1]), q


class Routes:
    def __init__(self, me):
        self.me = me
        self.half = me.z // 2
        self.far = 2 - self.half
        self.near = 2 * self.half + (1 - me.z % 2)
        self.mid = (me.z == 1) | (me.z == 2)

    def z_peer(self, z):
        return {"dp": z * 2 + self.me.x, "tensor": self.me.t}

    def dz_of(self, k):
        return lax.rem(k * self.half + (4 - k) * (1 - self.half), Z_SIZE)

    def back(self, z):
        return lax.rem(self.me.z - z + Z_SIZE, Z_SIZE)


class Gather(Routes):
    def __init__(self, me, modes, shards, w, send_sem, recv_sem, local_sem):
        super().__init__(me)
        self.modes, self.shards, self.w = modes, shards, w
        self.send_sem, self.recv_sem, self.local_sem = send_sem, recv_sem, local_sem
        self.rows = shards[0].shape[0]

    def sem(self, m, send, recv):
        one = block_of(self.w, m, 0, 0, self.rows)
        return remote(one, one, self.send_sem.at[m, send], self.recv_sem.at[m, recv], self.me.device(db=1))

    def wait(self, m, slot):
        self.sem(m, slot, slot).wait_recv()

    def send(self, m, slot, dz, da, db, peer, own=False, leave=None):
        dp, y = self.me.chip(dz, da, db)
        dst = block_of(self.w, m, dp, y * 2 + self.me.c, self.rows)
        leave = slot if leave is None else leave
        remote(self.shards[m] if own else dst, dst, self.send_sem.at[m, leave], self.recv_sem.at[m, slot], peer).start()

    def z_slots(self, da):
        return [(4 * lax.rem(z - self.me.z + Z_SIZE, Z_SIZE) + 2 * da, z) for z in (self.far, self.near)]

    def z_send(self, m, da, own=False):
        for slot, z in self.z_slots(da):
            self.send(m, slot, 0, da, 0, self.z_peer(z), own)

    def local(self, m):
        me = self.me
        return pltpu.make_async_copy(self.shards[m], block_of(self.w, m, me.dp, me.t, self.rows), self.local_sem.at[m])

    def place(self, m, q):
        if self.modes[m] == 0:
            return q % 4, q // 4
        return (0, q) if q < 2 else (1 + (q - 2) % 3, (q - 2) // 3)

    def pump(self, m, q):
        me = self.me
        k, da = self.place(m, q)
        dz = self.dz_of(k) if k else 0
        slot = 4 * dz + 2 * da
        self.wait(m, slot)
        if k in (1, 2) and (self.modes[m] == 1 or da == 0):

            @pl.when(self.mid)
            def _():
                there = lax.rem(self.near - me.z + dz + Z_SIZE, Z_SIZE)
                self.send(m, 4 * there + 2 * da, dz, da, 0, self.z_peer(self.near), leave=31 + 2 * da + k)

        if self.modes[m] == 0 and da == 0:
            self.send(m, 4 * dz + 2, dz, 0, 0, me.device(da=1))
        if self.modes[m] == 1 and k == 0:
            self.z_send(m, 1)
        self.send(m, slot + 1, dz, da, 0, me.device(db=1))
        self.send(m, 16 + slot, dz, da, 0, me.device(other=True))

    def last(self, m, q):
        k, da = self.place(m, q)
        dz = self.dz_of(k) if k else 0
        slot = 4 * dz + 2 * da + 1
        self.wait(m, slot)
        self.send(m, 16 + slot, dz, da, 1, self.me.device(other=True))

    def run(self, steps):
        me = self.me
        for op, m, q in parse(steps):
            if op == "A":
                self.send(m, 2, 0, 0, 0, me.device(da=1), True)
            elif op == "B":
                self.send(m, 1, 0, 0, 0, me.device(db=1), True)
                self.send(m, 16, 0, 0, 0, me.device(other=True), True)
                self.local(m).start()
            elif op == "y":
                self.z_send(m, 0, True)
            elif op == "p":
                self.pump(m, q)
            else:
                self.last(m, q)

    def collect(self, m):
        self.local(m).wait()

        @pl.loop(16, 32)
        def _(s):
            self.wait(m, s)

    def drain(self):
        for m in range(3):
            left = lambda s: self.sem(m, s, s).wait_send()
            for da in range(1 + self.modes[m]):
                for slot, _ in self.z_slots(da):
                    left(slot)

                @pl.when(self.mid)
                def _():
                    left(32 + 2 * da)
                    left(33 + 2 * da)

            for dz in range(1 if self.modes[m] else Z_SIZE):
                left(4 * dz + 2)

            @pl.loop(0, 8)
            def _(s):
                left(2 * s + 1)

            @pl.loop(16, 32)
            def _(s):
                left(s)


class Scatter(Routes):
    def __init__(self, me, modes, w, w0_grad, out_ref, core_buf, b_buf, t_buf, send_sem, recv_sem):
        super().__init__(me)
        self.out_ref = out_ref
        self.modes, self.w, self.w0_grad = modes, w, w0_grad
        self.core_buf, self.b_buf, self.t_buf = core_buf, b_buf, t_buf
        self.send_sem, self.recv_sem = send_sem, recv_sem
        self.rows = b_buf.shape[2]

    def order(self, i):
        me = self.me
        return flip(me.y, 1 - i // 2) * 2 + flip(1 - me.c, i % 2)

    def part(self, m, dz, da, db, core):
        dp, y = self.me.chip(dz, da, db)
        if m == 0:
            return self.w0_grad.at[y * 2 + core, pl.ds(pl.multiple_of(dp * self.rows, self.rows), self.rows), :]
        return block_of(self.w, m, dp, y * 2 + core, self.rows)

    def sem(self, m, send, recv):
        one = self.b_buf.at[m, 0]
        return remote(one, one, self.send_sem.at[m, send], self.recv_sem.at[m, recv], self.me.device(db=1))

    def wait(self, m, slot):
        self.sem(m, slot, slot).wait_recv()

    def go(self, m, slot, src, dst, peer, leave=None):
        leave = slot if leave is None else leave
        remote(src, dst, self.send_sem.at[m, leave], self.recv_sem.at[m, slot], peer).start()

    def from_core(self, dz, da, db):
        return 4 * dz + 2 * db + da

    def ready(self, m, i):
        me = self.me
        c = me.c
        side = 1 - i // 2

        def where(s):
            other = 1 - s // 4
            return self.dz_of(3 - s % 4), side * (1 - c) + other * c, other * (1 - c) + side * c

        @pl.when(i % 2 == 0)
        def _():
            @pl.loop(0, 8)
            def _(s):
                dz, da, db = where(s)
                slot = 4 * dz + 2 * da + db
                self.go(m, slot, self.part(m, dz, da, db, 1 - c), self.core_buf.at[m, slot], me.device(other=True))

        @pl.when(i % 2 == 1)
        def _():
            @pl.loop(0, 8)
            def _(s):
                dz, da, db = where(s)
                slot = self.from_core(dz, da, db)
                self.wait(m, slot)
                self.core_buf[m, slot] = self.part(m, dz, da, db, c)[...] + self.core_buf[m, slot]

                @pl.when(db == 1)
                def _():
                    place = 2 * dz + da
                    self.go(m, 16 + place, self.core_buf.at[m, slot], self.b_buf.at[m, place], me.device(db=1))

    def way(self, m, da, j):
        return 2 * da + j if self.modes[m] else 4 + j

    def end(self, m, da, far):
        return (4 + 2 * da if self.modes[m] else 6) + far

    def z_out(self, m, dz, da, src):
        owner = lax.rem(self.me.z - dz + Z_SIZE, Z_SIZE)
        is_near = owner == self.near

        @pl.when(is_near)
        def _():
            j = self.end(m, da, 0)
            self.go(m, 24 + j, src, self.t_buf.at[m, j], self.z_peer(self.near))

        @pl.when(jnp.logical_not(is_near | self.mid) & (dz != 0))
        def _():
            j = self.way(m, da, 0) + (owner != self.far).astype(jnp.int32)
            self.go(m, 24 + j, src, self.t_buf.at[m, j], self.z_peer(self.near))

    def source(self, m, dz, da):
        return self.b_buf.at[m, 2 * dz + da] if self.modes[m] else self.t_buf.at[m, dz]

    def b_step(self, m, k, da):
        dz = self.dz_of(k)
        place = 2 * dz + da
        self.wait(m, 16 + place)
        self.b_buf[m, place] = self.b_buf[m, place] + self.core_buf[m, self.from_core(dz, da, 0)]
        if self.modes[m] == 1:
            self.z_out(m, dz, da, self.b_buf.at[m, place])
        elif da == 1:
            self.go(m, 24 + dz, self.b_buf.at[m, place], self.t_buf.at[m, dz], self.me.device(da=1))

    def a_step(self, m, k):
        dz = self.dz_of(k)
        self.wait(m, 24 + dz)
        self.t_buf[m, dz] = self.t_buf[m, dz] + self.b_buf[m, 2 * dz]
        self.z_out(m, dz, 0, self.t_buf.at[m, dz])

    def z_step(self, m, da, j):
        @pl.when(self.mid)
        def _():
            owner = flip(self.far % 2, j) + 2 * (1 - self.half)
            way, end = self.way(m, da, j), self.end(m, da, 1)
            self.wait(m, 24 + way)
            self.t_buf[m, way] = self.t_buf[m, way] + self.source(m, self.back(owner), da)[...]
            self.go(m, 24 + end, self.t_buf.at[m, way], self.t_buf.at[m, end], self.z_peer(owner), leave=24 + way)

    def last_step(self, m):
        near, far = self.end(m, 1, 0), self.end(m, 1, 1)
        self.wait(m, 24 + near)
        self.wait(m, 24 + far)
        self.t_buf[m, near] = self.t_buf[m, near] + self.t_buf[m, far] + self.b_buf[m, 1]
        self.go(m, 32, self.t_buf.at[m, near], self.t_buf.at[m, 8], self.me.device(da=1))

    def run(self, steps):
        for op, m, q in parse(steps):
            if op == "b":
                self.b_step(m, 3 - q // 2, 1 - q % 2)
            elif op == "c":
                self.b_step(m, 3 - q % 4, 1 - q // 4)
            elif op == "a":
                self.a_step(m, 3 - q)
            elif op == "z":
                self.z_step(m, (1 - q // 2) * self.modes[m], 1 - q % 2)
            elif op == "e":
                self.last_step(m)
            else:
                self.finish(m)

    def finish(self, m):
        wide = lambda ref: ref[...].astype(jnp.float32)
        near = self.end(m, 0, 0)
        self.wait(m, 24 + near)
        self.wait(m, 25 + near)
        total = wide(self.source(m, 0, 0)) + wide(self.t_buf.at[m, near]) + wide(self.t_buf.at[m, near + 1])
        if self.modes[m] == 1:
            self.wait(m, 32)
            total = total + wide(self.t_buf.at[m, 8])
        self.out_ref[m] = total

    def drain(self):
        for m in range(3):
            left = lambda s: self.sem(m, s, s).wait_send()

            @pl.loop(0, 24)
            def _(s):
                left(s)

            for da in range(1 + self.modes[m]):
                for j in (self.way(m, da, 0), self.way(m, da, 1), self.end(m, da, 0)):
                    left(24 + j)
            for j in (8,) if self.modes[m] else range(Z_SIZE):
                left(24 + j)


class VectorSum:
    def __init__(self, me, buf, zbuf, send_sem, recv_sem):
        self.me, self.buf, self.zbuf, self.send_sem, self.recv_sem = me, buf, zbuf, send_sem, recv_sem

    def copy(self, step, src, dst, peer):
        return remote(src, dst, self.send_sem.at[step], self.recv_sem.at[step], peer)

    def peer(self, step):
        me = self.me
        if step == 0:
            return me.device(other=True)
        dx, dy = ((1, 0), (0, 1))[step - 1]
        return {"dp": me.z * 2 + flip(me.x, dx), "tensor": 2 * flip(me.y, dy) + me.c}

    def pair(self, step):
        return self.copy(step, self.buf.at[2 * step], self.buf.at[2 * step + 1], self.peer(step))

    def start(self, value):
        self.buf[0] = value
        self.pair(0).start()

    def advance(self, step):
        self.pair(step).wait()
        self.buf[2 * step + 2] = self.buf[2 * step] + self.buf[2 * step + 1]
        if step < 2:
            self.pair(step + 1).start()
        else:
            self.zbuf[self.me.z] = self.buf[6]
            for k in range(1, Z_SIZE):
                self.z_copy(k).start()

    def z_copy(self, k):
        return self.copy(2 + k, self.buf.at[6], self.zbuf.at[self.me.z], self.me.device(dz=k))

    def result(self):
        for k in range(1, Z_SIZE):
            self.z_copy(k).wait()
        return (self.zbuf[0] + self.zbuf[1]) + (self.zbuf[2] + self.zbuf[3])


def dot_nn(a, b):
    return lax.dot_general(a, b, (((1,), (0,)), ((), ())), preferred_element_type=jnp.float32)


def dot_nt(a, b):
    return lax.dot_general(a, b, (((1,), (1,)), ((), ())), preferred_element_type=jnp.float32)


def dot_tn(a, b):
    return lax.dot_general(a, b, (((0,), (0,)), ((), ())), preferred_element_type=jnp.float32)


def low(a):
    return a.astype(jnp.bfloat16)


def row_mean(a):
    return jnp.mean(a, axis=-1, keepdims=True)


def normalise(r):
    centre = r - row_mean(r)
    inverse = lax.rsqrt(row_mean(centre * centre) + NORM_EPS)
    return centre * inverse, inverse


def norm_back(g, z, inverse):
    return (g - row_mean(g) - z * row_mean(g * z)) * inverse


def gelu_pair(u):
    cdf = 0.5 + 0.5 * lax.erf(u * (0.5**0.5))
    density = jnp.exp(-0.5 * u * u) * ((0.5 / jnp.pi) ** 0.5)
    return u * cdf, cdf + u * density


V_BQ, V_BV, V_BO, V_G1, V_B1, V_BF, V_G2, V_B2, V_BI = range(9)
TILE = 64


class Layer:
    def __init__(self, **refs):
        self.__dict__.update(refs)
        self.rows, self.width = self.x.shape
        self.n_t = self.w.shape[1]
        self.cols = self.width // self.n_t
        self.heads = self.cols // HEAD_DIM
        self.ocol = (3 * self.cols) // 128 * 128

    def tiles(self, body):
        @pl.loop(0, self.rows // TILE)
        def _(i):
            body(pl.ds(pl.multiple_of(i * TILE, TILE), TILE))

    def project(self, t):
        lane = lax.broadcasted_iota(jnp.int32, (1, self.width), 1)
        out = dot_nn(self.x[...], self.w[0, t]) + self.qkv_bias[t]
        self.qkv[t] = low(jnp.where(lane < 3 * self.cols, out, 0.0))

    def piece(self, t, which, j):
        first = which * self.cols + j * HEAD_DIM
        return self.qkv.at[t, :, first : first + HEAD_DIM]

    def attend(self, t, valid, between):
        self.att[t, :, : HEAD_DIM] = jnp.zeros((self.rows, HEAD_DIM), jnp.bfloat16)
        for j in range(self.heads):
            q, k, v = (self.piece(t, i, j)[...] for i in range(3))
            s = dot_nt(k, q * jnp.bfloat16(HEAD_DIM**-0.5))
            s = jnp.where(valid, s, NEG_FILL)
            e = jnp.exp(s - jnp.max(s, axis=0, keepdims=True))
            p = low(e * (1.0 / jnp.sum(e, axis=0, keepdims=True)))
            self.p[t * self.heads + j] = p
            mix = dot_tn(v, p)
            first = 3 * self.cols - self.ocol + j * HEAD_DIM
            self.att[t, :, first : first + HEAD_DIM] = low(mix.T)
            between(j)

    def out_project(self, t):
        self.acc[...] += dot_nt(self.att[t], self.w[0, t, :, self.ocol :])

    def start_residual(self):
        self.acc[...] = self.x[...].astype(jnp.float32) + self.vec[2:3, :]

    def first_norm(self):
        def body(r):
            z, inverse = normalise(self.acc[r, :])
            self.z1[r, :] = z
            self.inv1[r, :] = jnp.broadcast_to(inverse, (TILE, 128))
            h1 = z * self.vec[3:4, :] + self.vec[4:5, :]
            self.h1b[r, :] = low(h1)
            self.acc[r, :] = h1 + self.vec[0:1, :]

        self.tiles(body)

    def inner(self, t):
        @pl.loop(0, self.rows // 128)
        def _(i):
            r = pl.ds(pl.multiple_of(i * 128, 128), 128)
            pre = dot_nn(self.h1b[r, :], self.w[1, t]) + self.inner_bias[t]
            act, slope = gelu_pair(pre)
            self.act[t, r, :] = low(act)
            self.slope[t, r, :] = low(slope)

    def outer(self, t):
        self.acc[...] += dot_nt(self.act[t], self.w[2, t])

    def second_norm(self, length):
        self.sums[...] = jnp.zeros_like(self.sums)

        def body(r):
            z, inverse = normalise(self.acc[r, :])
            place = r.start + lax.broadcasted_iota(jnp.int32, (TILE, 1), 0)
            mask = (place < length).astype(jnp.float32)
            gain = self.vec[5:6, :]
            self.y[r, :] = low((z * gain + self.vec[6:7, :]) * mask)
            dy = self.og[r, :].astype(jnp.float32) * mask
            dr2 = norm_back(dy * gain, z, inverse)
            self.acc[r, :] = dr2
            df = low(dr2)
            self.df[r, :] = df
            self.sums[V_G2] += fold(dy * z)
            self.sums[V_B2] += fold(dy)
            self.sums[V_BF] += fold(df.astype(jnp.float32))

        self.tiles(body)

    def outer_back(self, t):
        self.dact[...] = dot_nn(self.df[...], self.w[2, t])

        def body(r):
            d = low(self.dact[r, :] * self.slope[t, r, :].astype(jnp.float32))
            self.slope[t, r, :] = d
            self.sums[V_BI + t] += fold(d.astype(jnp.float32))

        self.tiles(body)
        self.w[2, t] = low(dot_nn(self.df_t[...], self.act[t]))

    def inner_back(self, t):
        self.acc[...] += dot_nt(self.slope[t], self.w[1, t])
        self.w[1, t] = low(dot_nn(self.h1b_t[...], self.slope[t]))

    def first_norm_back(self):
        def body(r):
            z = self.z1[r, :]
            dh1 = self.acc[r, :]
            self.sums[V_G1] += fold(dh1 * z)
            self.sums[V_B1] += fold(dh1)
            dr1 = norm_back(dh1 * self.vec[3:4, :], z, self.inv1[r, :1])
            self.acc[r, :] = dr1
            dob = low(dr1)
            self.df[r, :] = dob
            self.sums[V_BO] += fold(dob.astype(jnp.float32))

        self.tiles(body)

    def attend_back(self, t, between):
        scale = HEAD_DIM**-0.5
        self.datt[...] = low(dot_nn(self.df[...], self.w[0, t, :, self.ocol :]))
        for j in range(self.heads):
            first = 3 * self.cols - self.ocol + j * HEAD_DIM
            d = self.datt[:, first : first + HEAD_DIM]
            q, k, v = (self.piece(t, i, j)[...] for i in range(3))
            p = self.p[t * self.heads + j]
            dp = dot_nt(v, d)
            pf = p.astype(jnp.float32)
            delta = jnp.sum(pf * dp, axis=0, keepdims=True)
            ds = low(pf * (dp - delta))
            self.piece(t, 2, j)[...] = low(dot_nn(p, d))
            self.piece(t, 1, j)[...] = low(dot_nn(ds, q) * scale)
            self.piece(t, 0, j)[...] = low((dot_tn(k, ds) * scale).T)
            between(j)

    def head_sums(self, t):
        def body(r):
            self.sums[V_BI + self.n_t + t] += fold(self.qkv[t, r, :].astype(jnp.float32))

        self.tiles(body)

    def project_grad(self, t):
        self.w0_grad[t] = low(dot_nn(self.x_t[...], self.qkv[t]))
        out = self.w0_grad.at[t, :, self.ocol :]
        out[...] = low(out[...].astype(jnp.float32) + dot_nn(self.df_t[...], self.att[t]))

    def project_back(self, t):
        self.acc[...] += dot_nt(self.qkv[t], self.w[0, t])

    def transpose(self, src, dst):
        dst[...] = src[...].T


def fold(a):
    return jnp.sum(a.reshape(a.shape[0] // 8, 8, a.shape[1]), axis=0)


GATHER_MODES = (0, 1, 1)
SCATTER_MODES = (0, 1, 1)
GATHER_MODES = (0, 1, 1)
SCATTER_MODES = (0, 1, 1)
GATHER = {
    "first": ("A0:0", "y0:0", "B1:0"),
    "start": ("B0:0", "A2:0", "A1:0", "y1:0", "p0:4", "p0:1", "l0:0", "p0:2", "p1:2", "y2:0", "l0:1", "p0:5", "l0:4", "p0:3",
        "p0:6-7", "p1:1", "l0:5", "l1:2", "p2:2", "l0:6", "p2:1", "p1:5", "l0:3", "l0:2", "l0:7", "p1:3"),
    "attend": (),
    "heads": {3: ("l1:0",), 4: ("l1:5", "l1:1"), 5: ("l2:2", "p1:6"), 6: ("p1:4", "p2:5"), 8: ("l1:6", "l1:3"), 9: ("p2:3",),
        10: ("l1:4", "l2:0"), 11: ("p2:6",)},
    "out": {1: ("B2:0",), 2: ("l2:1", "p1:7"), 3: ("l1:7",)},
    "norm": ("p2:4",),
    "ffn": ("l2:6",),
    "inner": {0: ("p2:7",), 2: ("l2:4", "l2:3", "l2:5", "l2:7")},
}
SCATTER = {
    "outer": {},
    "inner": {0: ("b2:0",), 1: ("b2:2",), 2: ("b2:1", "z2:0", "b2:4", "b2:3")},
    "norm": ("b2:5",),
    "heads": {0: ("b1:2",), 2: ("z2:2", "b1:0"), 5: ("z2:3", "b2:6", "b1:1"), 7: ("b1:3", "b1:6"), 8: ("z1:1",), 9:
        ("e2:0",), 10: ("z1:0",)},
    "grad": {0: ("b1:4",), 1: ("z2:1",), 3: ("b0:0", "b1:7", "z1:2", "b0:2", "b1:5", "b0:4", "b0:1")},
    "last": ((), (), ("e1:0", "z1:3", "b0:6", "b0:3", "a0:0", "b0:5", "a0:1", "z0:0", "a0:2", "z0:1", "b0:7"), ("b2:7",
        "F2:0", "a0:3", "F1:0", "F0:0")),
}


def step_kernel(
    length_ref, x_ref, og_ref, packed_ref, wi_ref, wo_ref, qkv_bias, inner_bias, vec_ref,
    y_ref, acc_ref, out_ref, vout_ref,
    w, sums, qkv, p, att, z1, inv1, h1b, ffn, df, datt, dact, x_t, h1b_t, df_t,
    core_buf, b_buf, t_buf, vec_buf, vec_z,
    gather_send, gather_recv, local_sem, send_sem, recv_sem, vec_send, vec_recv,
):
    me = Place()
    rows, width = x_ref.shape
    act, slope, w0_grad = ffn.at[:, :rows], ffn.at[:, rows:], ffn.at[:, :width]
    gather = Gather(me, GATHER_MODES, (packed_ref, wi_ref, wo_ref), w, gather_send, gather_recv, local_sem)
    scatter = Scatter(me, SCATTER_MODES, w, w0_grad, out_ref, core_buf, b_buf, t_buf, send_sem, recv_sem)
    small = VectorSum(me, vec_buf, vec_z, vec_send, vec_recv)
    a = Layer(
        x=x_ref, og=og_ref, w=w, w0_grad=w0_grad, qkv_bias=qkv_bias, inner_bias=inner_bias, vec=vec_ref, y=y_ref, acc=acc_ref, sums=sums,
        qkv=qkv, p=p, att=att, z1=z1, inv1=inv1, h1b=h1b, act=act, slope=slope, df=df, datt=datt, dact=dact, x_t=x_t, h1b_t=h1b_t, df_t=df_t,
    )

    def at(run, slots, i):
        for n, steps in slots.items():

            @pl.when(i == n)
            def _():
                run(steps)

    def heads(run, slots, i, j):
        at(run, {n // a.heads: steps for n, steps in slots.items() if n % a.heads == j}, i)

    meet(me)
    gather.run(GATHER["first"])
    length = length_ref[0]
    valid = lax.broadcasted_iota(jnp.int32, (a.rows, 1), 0) < length
    a.transpose(a.x, a.x_t)
    a.start_residual()
    gather.run(GATHER["start"])
    gather.collect(0)
    gather.run(GATHER["attend"])

    @pl.loop(0, a.n_t)
    def _(t):
        a.project(t)
        a.attend(t, valid, lambda j: heads(gather.run, GATHER["heads"], t, j))
        a.out_project(t)
        at(gather.run, GATHER["out"], t)

    a.first_norm()
    a.transpose(a.h1b, a.h1b_t)
    gather.run(GATHER["norm"])
    gather.collect(1)
    gather.run(GATHER["ffn"])

    @pl.loop(0, a.n_t)
    def _(t):
        a.inner(t)
        at(gather.run, GATHER["inner"], t)

    gather.collect(2)

    @pl.loop(0, a.n_t)
    def _(t):
        a.outer(t)

    a.second_norm(length)
    a.transpose(a.df, a.df_t)
    gather.drain()

    @pl.loop(0, a.n_t)
    def _(i):
        a.outer_back(scatter.order(i))
        scatter.ready(2, i)
        at(scatter.run, SCATTER["outer"], i)

    @pl.loop(0, a.n_t)
    def _(i):
        a.inner_back(scatter.order(i))
        scatter.ready(1, i)
        at(scatter.run, SCATTER["inner"], i)

    a.first_norm_back()
    a.transpose(a.df, a.df_t)
    scatter.run(SCATTER["norm"])

    @pl.loop(0, a.n_t)
    def _(i):
        t = scatter.order(i)
        a.attend_back(t, lambda j: heads(scatter.run, SCATTER["heads"], i, j))
        a.head_sums(t)

        @pl.when(i == a.n_t - 1)
        def _():
            small.start(jnp.sum(sums[...], axis=1))

        a.project_grad(t)

        @pl.when(i == a.n_t - 1)
        def _():
            small.advance(0)

        scatter.ready(0, i)
        at(scatter.run, SCATTER["grad"], i)

    for t, steps in enumerate(SCATTER["last"]):
        a.project_back(t)
        if t in (1, 3):
            small.advance((t + 1) // 2)
        scatter.run(steps)
    vout_ref[...] = small.result()
    scatter.drain()


def step(length, x, og, packed, inner, outer, qkv_bias, inner_bias, vec, n_t):
    rows, width = x.shape
    cols = width // n_t
    heads = width // HEAD_DIM
    owidth = width - (3 * cols) // 128 * 128
    shard = packed.shape[0]
    bf, f32 = jnp.bfloat16, jnp.float32
    vmem = pl.BlockSpec(memory_space=pltpu.VMEM)
    n_v = V_BI + 2 * n_t
    n_w = shard * lax.axis_size("dp")
    buf = lambda n: pltpu.VMEM((3, n, shard, width), bf)
    dma = pltpu.SemaphoreType.DMA
    return pl.pallas_call(
        step_kernel,
        out_shape=(
            jax.ShapeDtypeStruct((rows, width), bf),
            jax.ShapeDtypeStruct((rows, width), f32),
            jax.ShapeDtypeStruct((3, shard, width), f32),
            jax.ShapeDtypeStruct((n_v, width), f32),
        ),
        in_specs=[pl.BlockSpec(memory_space=pltpu.SMEM)] + [vmem] * 8,
        out_specs=[vmem] * 4,
        scratch_shapes=[
            pltpu.VMEM((3, n_t, n_w, width), bf),
            pltpu.VMEM((n_v, 8, width), f32),
            pltpu.VMEM((n_t, rows, width), bf),
            pltpu.VMEM((heads, rows, rows), bf),
            pltpu.VMEM((n_t, rows, owidth), bf),
            pltpu.VMEM((rows, width), f32),
            pltpu.VMEM((rows, 128), f32),
            pltpu.VMEM((rows, width), bf),
            pltpu.VMEM((n_t, max(2 * rows, width), width), bf),
            pltpu.VMEM((rows, width), bf),
            pltpu.VMEM((rows, owidth), bf),
            pltpu.VMEM((rows, width), f32),
            pltpu.VMEM((width, rows), bf),
            pltpu.VMEM((width, rows), bf),
            pltpu.VMEM((width, rows), bf),
            buf(16),
            buf(8),
            buf(9),
            pltpu.VMEM((7, n_v, width), f32),
            pltpu.VMEM((Z_SIZE, n_v, width), f32),
            dma((3, 36)),
            dma((3, 36)),
            dma((3,)),
            dma((3, 33)),
            dma((3, 33)),
            dma((6,)),
            dma((6,)),
        ],
        compiler_params=pltpu.CompilerParams(collective_id=0, has_side_effects=True, vmem_limit_bytes=63 * 2**20),
    )(length, x, og, packed, inner, outer, qkv_bias, inner_bias, vec)


def data_parallel(
    hidden_in, seq_lengths, w_query, b_query, w_key, w_value, b_value, w_out, b_out, norm1_gain, norm1_bias,
    w_inner, b_inner, w_outer, b_outer, norm2_gain, norm2_bias, out_grad,
):
    n_t = lax.axis_size("tensor")
    cols = w_query.shape[1]
    length = lax.dynamic_slice_in_dim(seq_lengths, lax.axis_index("tensor"), 1)
    packed = jnp.concatenate((w_query, w_key, w_value, w_out), axis=1)
    split = lambda a: a.reshape(n_t, 1, -1)
    zeros = jnp.zeros((n_t, 1, cols), jnp.float32)
    qkv_bias = jnp.concatenate((split(b_query), zeros, split(b_value), zeros), axis=2)
    vec = jnp.stack((b_outer, b_outer, b_out, norm1_gain, norm1_bias, norm2_gain, norm2_bias, b_out))
    y, grad_in, shards, sums = step(
        length, hidden_in, out_grad, packed, w_inner, w_outer, qkv_bias, split(b_inner), vec, n_t
    )
    heads = sums[V_BI + n_t :]
    join = lambda a: a.reshape(-1)
    gq, gk, gv, go = (shards[0, :, i * cols : (i + 1) * cols] for i in range(4))
    return (
        y, grad_in, gq, join(heads[:, :cols]), gk, gv, join(heads[:, 2 * cols : 3 * cols]), go, sums[V_BO], sums[V_G1], sums[V_B1],
        shards[1], join(sums[V_BI : V_BI + n_t]), shards[2], sums[V_BF], sums[V_G2], sums[V_B2],
    )


def solution(mesh):
    in_specs = (
        P(("dp", "tensor"), None),
        P("dp"),
        P("dp", "tensor"),
        P(),
        P("dp", "tensor"),
        P("dp", "tensor"),
        P(),
        P("dp", "tensor"),
        P(),
        P(),
        P(),
        P("dp", "tensor"),
        P(),
        P("dp", "tensor"),
        P(),
        P(),
        P(),
        P(("dp", "tensor"), None),
    )
    out_specs = (
        P(("dp", "tensor"), None),
        P(("dp", "tensor"), None),
        P("dp", "tensor"),
        P(),
        P("dp", "tensor"),
        P("dp", "tensor"),
        P(),
        P("dp", "tensor"),
        P(),
        P(),
        P(),
        P("dp", "tensor"),
        P(),
        P("dp", "tensor"),
        P(),
        P(),
        P(),
    )
    small = mesh.shape["dp"] == 2 * Z_SIZE and mesh.shape["tensor"] == 4
    return jax.shard_map(
        data_parallel if small else per_device, mesh=mesh, in_specs=in_specs, out_specs=out_specs, check_vma=False
    )
```

```python
import functools

import jax
import jax.numpy as jnp
from jax import lax
from jax.experimental import pallas as pl
from jax.experimental.pallas import tpu as pltpu
from jax.sharding import PartitionSpec as P

HEAD_DIM = 64


NEG_FILL = -1000000000.0
NORM_EPS = 1e-12


def layer_norm(residual, norm_gain, norm_bias):
    centre = residual - jnp.mean(residual, axis=-1, keepdims=True)
    spread = jnp.mean(centre * centre, axis=-1, keepdims=True)
    return centre * lax.rsqrt(spread + NORM_EPS) * norm_gain + norm_bias


def exact_gelu(values):
    return jax.nn.gelu(values, approximate=False)


def contract_last(first_op, second_op):
    return lax.dot_general(
        first_op, second_op, (((1,), (1,)), ((), ())), preferred_element_type=jnp.float32
    )


def contract_first(first_op, second_op):
    return lax.dot_general(
        first_op, second_op, (((0,), (0,)), ((), ())), preferred_element_type=jnp.float32
    )


def split_blocks(heads_arr, block_rows):
    batches, length, head_size = heads_arr.shape
    return heads_arr.reshape(batches, length // block_rows, block_rows, head_size).transpose(
        1, 0, 2, 3
    )


def join_blocks(block_array):
    block_count, batches, block_rows, head_size = block_array.shape
    return block_array.transpose(1, 0, 2, 3).reshape(batches, block_count * block_rows, head_size)


def block_scores(query_portion, key_head_tensor, key_valid, score_scale):
    scores = (
        jnp.einsum(
            "eix,evx->eiv", query_portion, key_head_tensor, preferred_element_type=jnp.float32
        )
        * score_scale
    )
    return jnp.where(key_valid[:, None, :], scores, NEG_FILL)


def attend(query_heads, key_head_tensor, value_head_tensor, key_valid, block_rows, score_scale):

    def one_block(query_portion):
        scores = block_scores(query_portion, key_head_tensor, key_valid, score_scale)
        row_max = jnp.max(scores, axis=-1, keepdims=True)
        exponent = jnp.exp(scores - row_max)
        row_total = jnp.sum(exponent, axis=-1, keepdims=True)
        softmax_reduced = (exponent / row_total).astype(jnp.bfloat16)
        mixture = jnp.einsum(
            "fwj,fjt->fwt", softmax_reduced, value_head_tensor, preferred_element_type=jnp.float32
        )
        return (mixture.astype(jnp.bfloat16), row_max, row_total)

    mixture, row_max, row_total = lax.map(one_block, split_blocks(query_heads, block_rows))
    return (join_blocks(mixture), row_max, row_total)


def attend_back(
    query_heads,
    key_head_tensor,
    value_head_tensor,
    grad_heads,
    row_max,
    row_total,
    key_valid,
    block_rows,
    score_scale,
):

    def one_block(running, block_in):
        key_grad, value_grad = running
        query_portion, gradient_portion, max_part, total_part = block_in
        scores = block_scores(query_portion, key_head_tensor, key_valid, score_scale)
        softmax = jnp.exp(scores - max_part) / total_part
        softmax_reduced = softmax.astype(jnp.bfloat16)
        soft_grad = jnp.einsum(
            "eix,evx->eiv", gradient_portion, value_head_tensor, preferred_element_type=jnp.float32
        )
        centre = jnp.sum(softmax * soft_grad, axis=-1, keepdims=True)
        score_gradient = (softmax * (soft_grad - centre)).astype(jnp.bfloat16)
        query_grad = (
            jnp.einsum(
                "fwj,fjt->fwt", score_gradient, key_head_tensor, preferred_element_type=jnp.float32
            )
            * score_scale
        )
        key_grad = (
            key_grad
            + jnp.einsum(
                "oxl,oxn->oln", score_gradient, query_portion, preferred_element_type=jnp.float32
            )
            * score_scale
        )
        value_grad = value_grad + jnp.einsum(
            "oxl,oxn->oln", softmax_reduced, gradient_portion, preferred_element_type=jnp.float32
        )
        return ((key_grad, value_grad), query_grad)

    zero_grads = jnp.zeros(key_head_tensor.shape, jnp.float32)
    block_inputs = (
        split_blocks(query_heads, block_rows),
        split_blocks(grad_heads, block_rows),
        row_max,
        row_total,
    )
    (key_grad, value_grad), query_grad = lax.scan(one_block, (zero_grads, zero_grads), block_inputs)
    return (join_blocks(query_grad), key_grad, value_grad)


def per_device(
    hidden_in,
    seq_lengths,
    w_query,
    b_query,
    w_key,
    w_value,
    b_value,
    w_out,
    b_out,
    norm1_gain,
    norm1_bias,
    w_inner,
    b_inner,
    w_outer,
    b_outer,
    norm2_gain,
    norm2_bias,
    out_grad,
):
    tensor_size = lax.axis_size("tensor")
    tensor_place = lax.axis_index("tensor")
    local_rows, feature_width = hidden_in.shape
    group_rows = local_rows * tensor_size
    seq_count = seq_lengths.shape[0]
    seq_len = group_rows // seq_count
    head_cols = w_query.shape[1]
    inner_cols = w_inner.shape[1]
    heads_here = head_cols // HEAD_DIM
    block_rows = min(512, seq_len)
    score_scale = HEAD_DIM ** (-0.5)
    local_start = tensor_place * local_rows
    row_index = lax.iota(jnp.int32, group_rows)
    seq_match = (row_index[:, None] // seq_len == lax.iota(jnp.int32, seq_count)[None, :]).astype(
        jnp.int32
    )
    row_limit = jnp.sum(seq_match * seq_lengths[None, :], axis=1)
    row_valid = row_index % seq_len < row_limit
    local_mask = lax.dynamic_slice_in_dim(row_valid, local_start, local_rows).astype(jnp.float32)[
        :, None
    ]
    key_valid = jnp.repeat(row_valid.reshape(seq_count, seq_len), heads_here, axis=0)

    def heads_of(matrix):
        shaped = matrix.reshape(seq_count, seq_len, heads_here, HEAD_DIM).transpose(0, 2, 1, 3)
        return shaped.reshape(seq_count * heads_here, seq_len, HEAD_DIM)

    def rows_of(matrix):
        shaped = matrix.reshape(seq_count, heads_here, seq_len, HEAD_DIM).transpose(0, 2, 1, 3)
        return shaped.reshape(group_rows, head_cols)

    full_query, full_key, full_value, full_out, full_inner, full_outer = (
        lax.all_gather(w_query, "dp", axis=0, tiled=True),
        lax.all_gather(w_key, "dp", axis=0, tiled=True),
        lax.all_gather(w_value, "dp", axis=0, tiled=True),
        lax.all_gather(w_out, "dp", axis=0, tiled=True),
        lax.all_gather(w_inner, "dp", axis=0, tiled=True),
        lax.all_gather(w_outer, "dp", axis=0, tiled=True),
    )
    joint_weight = jnp.concatenate((full_query, full_key, full_value), axis=1)
    query_bias = lax.dynamic_slice_in_dim(b_query, tensor_place * head_cols, head_cols)
    value_bias = lax.dynamic_slice_in_dim(b_value, tensor_place * head_cols, head_cols)
    inner_bias = lax.dynamic_slice_in_dim(b_inner, tensor_place * inner_cols, inner_cols)
    joint_bias = jnp.concatenate((query_bias, jnp.zeros((head_cols,), jnp.float32), value_bias))
    whole_in = lax.all_gather(hidden_in, "tensor", axis=0, tiled=True)
    joint_rows = (
        jnp.dot(whole_in, joint_weight, preferred_element_type=jnp.float32) + joint_bias
    ).astype(jnp.bfloat16)
    query_heads = heads_of(joint_rows[:, :head_cols])
    key_head_tensor = heads_of(joint_rows[:, head_cols : 2 * head_cols])
    value_head_tensor = heads_of(joint_rows[:, 2 * head_cols :])
    mixture_heads, row_max, row_total = attend(
        query_heads, key_head_tensor, value_head_tensor, key_valid, block_rows, score_scale
    )
    mixture = rows_of(mixture_heads)
    summed_out = lax.psum_scatter(
        contract_last(mixture, full_out).astype(jnp.bfloat16),
        "tensor",
        scatter_dimension=0,
        tiled=True,
    ).astype(jnp.float32)
    first_sum = hidden_in.astype(jnp.float32) + (summed_out + b_out)
    first_norm = layer_norm(first_sum, norm1_gain, norm1_bias)
    mid_whole = lax.all_gather(first_norm.astype(jnp.bfloat16), "tensor", axis=0, tiled=True)
    pre_act = jnp.dot(mid_whole, full_inner, preferred_element_type=jnp.float32) + inner_bias
    act_low = exact_gelu(pre_act).astype(jnp.bfloat16)
    second_sum = first_norm + (
        lax.psum_scatter(
            contract_last(act_low, full_outer).astype(jnp.bfloat16),
            "tensor",
            scatter_dimension=0,
            tiled=True,
        ).astype(jnp.float32)
        + b_outer
    )
    normed, norm2_back = jax.vjp(layer_norm, second_sum, norm2_gain, norm2_bias)
    layer_out = (normed * local_mask).astype(jnp.bfloat16)
    out_cot = out_grad.astype(jnp.float32) * local_mask
    dsecond, gain2_part, bias2_part = norm2_back(out_cot)
    dffn_low = dsecond.astype(jnp.bfloat16)
    outer_bias_part = jnp.sum(dffn_low, axis=0, dtype=jnp.float32)
    dffn_whole = lax.all_gather(dffn_low, "tensor", axis=0, tiled=True)
    grad_outer = contract_first(dffn_whole, act_low)
    dact = jnp.dot(dffn_whole, full_outer, preferred_element_type=jnp.float32)
    _, gelu_back = jax.vjp(exact_gelu, pre_act)
    dpre_low = gelu_back(dact)[0].astype(jnp.bfloat16)
    inner_bias_part = jnp.sum(dpre_low, axis=0, dtype=jnp.float32)
    grad_inner = contract_first(mid_whole, dpre_low)
    dfirst_norm = dsecond + lax.psum_scatter(
        contract_last(dpre_low, full_inner).astype(jnp.bfloat16),
        "tensor",
        scatter_dimension=0,
        tiled=True,
    ).astype(jnp.float32)
    _, norm1_back = jax.vjp(layer_norm, first_sum, norm1_gain, norm1_bias)
    dfirst, gain1_part, bias1_part = norm1_back(dfirst_norm)
    dattn_low = dfirst.astype(jnp.bfloat16)
    out_bias_part = jnp.sum(dattn_low, axis=0, dtype=jnp.float32)
    dattn_whole = lax.all_gather(dattn_low, "tensor", axis=0, tiled=True)
    grad_out_w = contract_first(dattn_whole, mixture)
    dmixture = jnp.dot(dattn_whole, full_out, preferred_element_type=jnp.float32).astype(
        jnp.bfloat16
    )
    dquery_heads, dkey_heads, dvalue_heads = attend_back(
        query_heads,
        key_head_tensor,
        value_head_tensor,
        heads_of(dmixture),
        row_max,
        row_total,
        key_valid,
        block_rows,
        score_scale,
    )
    djoint = jnp.concatenate(
        (rows_of(dquery_heads), rows_of(dkey_heads), rows_of(dvalue_heads)), axis=1
    ).astype(jnp.bfloat16)
    joint_bias_part = jnp.sum(djoint, axis=0, dtype=jnp.float32)
    grad_joint = contract_first(whole_in, djoint)
    grad_in = dfirst + lax.psum_scatter(
        contract_last(djoint, joint_weight).astype(jnp.bfloat16),
        "tensor",
        scatter_dimension=0,
        tiled=True,
    ).astype(jnp.float32)
    grad_query = grad_joint[:, :head_cols]
    grad_key = grad_joint[:, head_cols : 2 * head_cols]
    grad_value = grad_joint[:, 2 * head_cols :]
    shard_grads = tuple(
        (
            lax.psum_scatter(grad_query, "dp", scatter_dimension=0, tiled=True),
            lax.psum_scatter(grad_key, "dp", scatter_dimension=0, tiled=True),
            lax.psum_scatter(grad_value, "dp", scatter_dimension=0, tiled=True),
            lax.psum_scatter(grad_out_w, "dp", scatter_dimension=0, tiled=True),
            lax.psum_scatter(grad_inner, "dp", scatter_dimension=0, tiled=True),
            lax.psum_scatter(grad_outer, "dp", scatter_dimension=0, tiled=True),
        )
    )

    def placed(vector, total_len):
        return lax.dynamic_update_slice_in_dim(
            jnp.zeros((total_len,), jnp.float32), vector, tensor_place * vector.shape[0], 0
        )

    query_bias_part = placed(joint_bias_part[:head_cols], feature_width)
    value_bias_part = placed(joint_bias_part[2 * head_cols :], feature_width)
    hidden_bias_part = placed(inner_bias_part, b_inner.shape[0])
    vector_sums = lax.psum(
        (
            query_bias_part,
            value_bias_part,
            out_bias_part,
            gain1_part,
            bias1_part,
            hidden_bias_part,
            outer_bias_part,
            gain2_part,
            bias2_part,
        ),
        ("dp", "tensor"),
    )
    return (
        layer_out,
        grad_in,
        shard_grads[0],
        vector_sums[0],
        shard_grads[1],
        shard_grads[2],
        vector_sums[1],
        shard_grads[3],
        vector_sums[2],
        vector_sums[3],
        vector_sums[4],
        shard_grads[4],
        vector_sums[5],
        shard_grads[5],
        vector_sums[6],
        vector_sums[7],
        vector_sums[8],
    )


Z_SIZE = 4
MESH_IDS = pl.DeviceIdType.MESH


def flip(place, bit):
    return place + bit - 2 * place * bit


class Place:
    def __init__(self):
        self.dp = lax.axis_index("dp")
        self.t = lax.axis_index("tensor")
        self.z = self.dp // 2
        self.x = self.dp % 2
        self.y = self.t // 2
        self.c = self.t % 2

    def chip(self, dz, da, db):
        c = self.c
        z = lax.rem(self.z - dz + Z_SIZE, Z_SIZE)
        x = flip(self.x, da * c + db * (1 - c))
        y = flip(self.y, da * (1 - c) + db * c)
        return z * 2 + x, y

    def device(self, dz=0, da=0, db=0, other=False):
        dp, y = self.chip(dz, da, db)
        core = 1 - self.c if other else self.c
        return {"dp": dp, "tensor": y * 2 + core}


def block_of(ref, m, dp, t, rows):
    return ref.at[m, t, pl.ds(pl.multiple_of(dp * rows, rows), rows), :]


def peers_of(me):
    return [me.device(dz=k) for k in range(1, Z_SIZE)] + [me.device(da=1), me.device(db=1), me.device(other=True)]


def greet(me):
    for peer in peers_of(me):
        pl.semaphore_signal(pltpu.get_barrier_semaphore(), inc=1, device_id=peer, device_id_type=MESH_IDS)


def meet(me):
    pl.semaphore_wait(pltpu.get_barrier_semaphore(), len(peers_of(me)))


def remote(src, dst, send, recv, peer):
    return pltpu.make_async_remote_copy(
        src_ref=src, dst_ref=dst, send_sem=send, recv_sem=recv, device_id=peer, device_id_type=MESH_IDS
    )


def parse(steps):
    for step in steps:
        first, _, stop = step[3:].partition("-")
        for q in range(int(first or 0), int(stop or first or 0) + 1):
            yield step[0], int(step[1]), q


class Routes:
    def __init__(self, me):
        self.me = me
        self.half = me.z // 2
        self.far = 2 - self.half
        self.near = 2 * self.half + (1 - me.z % 2)
        self.mid = (me.z == 1) | (me.z == 2)

    def z_peer(self, z):
        return {"dp": z * 2 + self.me.x, "tensor": self.me.t}

    def dz_of(self, k):
        return lax.rem(k * self.half + (4 - k) * (1 - self.half), Z_SIZE)

    def back(self, z):
        return lax.rem(self.me.z - z + Z_SIZE, Z_SIZE)


class Gather(Routes):
    def __init__(self, me, modes, w, send_sem, recv_sem):
        super().__init__(me)
        self.modes, self.w = modes, w
        self.send_sem, self.recv_sem = send_sem, recv_sem
        self.rows = w.shape[2] // lax.axis_size("dp")

    def sem(self, m, send, recv):
        one = block_of(self.w, m, 0, 0, self.rows)
        return remote(one, one, self.send_sem.at[m, send], self.recv_sem.at[m, recv], self.me.device(db=1))

    def wait(self, m, slot):
        self.sem(m, slot, slot).wait_recv()

    def send(self, m, slot, dz, da, db, peer, leave=None):
        dp, y = self.me.chip(dz, da, db)
        dst = block_of(self.w, m, dp, y * 2 + self.me.c, self.rows)
        leave = slot if leave is None else leave
        remote(dst, dst, self.send_sem.at[m, leave], self.recv_sem.at[m, slot], peer).start()

    def z_slots(self, da):
        return [(4 * lax.rem(z - self.me.z + Z_SIZE, Z_SIZE) + 2 * da, z) for z in (self.far, self.near)]

    def z_send(self, m, da):
        for slot, z in self.z_slots(da):
            self.send(m, slot, 0, da, 0, self.z_peer(z))

    def own(self, m):
        return block_of(self.w, m, self.me.dp, self.me.t, self.rows)

    def place(self, m, q):
        if self.modes[m] == 0:
            return q % 4, q // 4
        return (0, q) if q < 2 else (1 + (q - 2) % 3, (q - 2) // 3)

    def pump(self, m, q):
        me = self.me
        k, da = self.place(m, q)
        dz = self.dz_of(k) if k else 0
        slot = 4 * dz + 2 * da
        self.wait(m, slot)
        if k in (1, 2) and (self.modes[m] == 1 or da == 0):

            @pl.when(self.mid)
            def _():
                there = lax.rem(self.near - me.z + dz + Z_SIZE, Z_SIZE)
                self.send(m, 4 * there + 2 * da, dz, da, 0, self.z_peer(self.near), leave=31 + 2 * da + k)

        if self.modes[m] == 0 and da == 0:
            self.send(m, 4 * dz + 2, dz, 0, 0, me.device(da=1))
        if self.modes[m] == 1 and k == 0:
            self.z_send(m, 1)
        self.send(m, slot + 1, dz, da, 0, me.device(db=1))
        self.send(m, 16 + slot, dz, da, 0, me.device(other=True))

    def last(self, m, q):
        k, da = self.place(m, q)
        dz = self.dz_of(k) if k else 0
        slot = 4 * dz + 2 * da + 1
        self.wait(m, slot)
        self.send(m, 16 + slot, dz, da, 1, self.me.device(other=True))

    def run(self, steps):
        me = self.me
        for op, m, q in parse(steps):
            if op == "A":
                self.send(m, 2, 0, 0, 0, me.device(da=1))
            elif op == "B":
                self.send(m, 1, 0, 0, 0, me.device(db=1))
                self.send(m, 16, 0, 0, 0, me.device(other=True))
            elif op == "y":
                self.z_send(m, 0)
            elif op == "p":
                self.pump(m, q)
            else:
                self.last(m, q)

    def collect(self, m):
        @pl.loop(16, 32)
        def _(s):
            self.wait(m, s)

    def drain(self):
        for m in range(3):
            left = lambda s: self.sem(m, s, s).wait_send()
            for da in range(1 + self.modes[m]):
                for slot, _ in self.z_slots(da):
                    left(slot)

                @pl.when(self.mid)
                def _():
                    left(32 + 2 * da)
                    left(33 + 2 * da)

            for dz in range(1 if self.modes[m] else Z_SIZE):
                left(4 * dz + 2)

            @pl.loop(0, 8)
            def _(s):
                left(2 * s + 1)

            @pl.loop(16, 32)
            def _(s):
                left(s)


class Scatter(Routes):
    def __init__(self, me, modes, w, w0_grad, out_ref, core_buf, b_buf, t_buf, send_sem, recv_sem):
        super().__init__(me)
        self.out_ref = out_ref
        self.modes, self.w, self.w0_grad = modes, w, w0_grad
        self.core_buf, self.b_buf, self.t_buf = core_buf, b_buf, t_buf
        self.send_sem, self.recv_sem = send_sem, recv_sem
        self.rows = b_buf.shape[2]

    def order(self, i):
        me = self.me
        return flip(me.y, 1 - i // 2) * 2 + flip(1 - me.c, i % 2)

    def part(self, m, dz, da, db, core):
        dp, y = self.me.chip(dz, da, db)
        if m == 0:
            return self.w0_grad.at[y * 2 + core, pl.ds(pl.multiple_of(dp * self.rows, self.rows), self.rows), :]
        return block_of(self.w, m, dp, y * 2 + core, self.rows)

    def sem(self, m, send, recv):
        one = self.b_buf.at[m, 0]
        return remote(one, one, self.send_sem.at[m, send], self.recv_sem.at[m, recv], self.me.device(db=1))

    def wait(self, m, slot):
        self.sem(m, slot, slot).wait_recv()

    def go(self, m, slot, src, dst, peer, leave=None):
        leave = slot if leave is None else leave
        remote(src, dst, self.send_sem.at[m, leave], self.recv_sem.at[m, slot], peer).start()

    def from_core(self, dz, da, db):
        return 4 * dz + 2 * db + da

    def ready(self, m, i):
        me = self.me
        c = me.c
        side = 1 - i // 2

        def where(s):
            other = 1 - s // 4
            return self.dz_of(3 - s % 4), side * (1 - c) + other * c, other * (1 - c) + side * c

        @pl.when(i % 2 == 0)
        def _():
            @pl.loop(0, 8)
            def _(s):
                dz, da, db = where(s)
                slot = 4 * dz + 2 * da + db
                self.go(m, slot, self.part(m, dz, da, db, 1 - c), self.core_buf.at[m, slot], me.device(other=True))

        @pl.when(i % 2 == 1)
        def _():
            @pl.loop(0, 8)
            def _(s):
                dz, da, db = where(s)
                slot = self.from_core(dz, da, db)
                self.wait(m, slot)
                self.core_buf[m, slot] = self.part(m, dz, da, db, c)[...] + self.core_buf[m, slot]

                @pl.when(db == 1)
                def _():
                    place = 2 * dz + da
                    self.go(m, 16 + place, self.core_buf.at[m, slot], self.b_buf.at[m, place], me.device(db=1))

    def way(self, m, da, j):
        return 2 * da + j if self.modes[m] else 4 + j

    def end(self, m, da, far):
        return (4 + 2 * da if self.modes[m] else 6) + far

    def z_out(self, m, dz, da, src):
        owner = lax.rem(self.me.z - dz + Z_SIZE, Z_SIZE)
        is_near = owner == self.near

        @pl.when(is_near)
        def _():
            j = self.end(m, da, 0)
            self.go(m, 24 + j, src, self.t_buf.at[m, j], self.z_peer(self.near))

        @pl.when(jnp.logical_not(is_near | self.mid) & (dz != 0))
        def _():
            j = self.way(m, da, 0) + (owner != self.far).astype(jnp.int32)
            self.go(m, 24 + j, src, self.t_buf.at[m, j], self.z_peer(self.near))

    def source(self, m, dz, da):
        return self.b_buf.at[m, 2 * dz + da] if self.modes[m] else self.t_buf.at[m, dz]

    def b_step(self, m, k, da):
        dz = self.dz_of(k)
        place = 2 * dz + da
        self.wait(m, 16 + place)
        self.b_buf[m, place] = self.b_buf[m, place] + self.core_buf[m, self.from_core(dz, da, 0)]
        if self.modes[m] == 1:
            self.z_out(m, dz, da, self.b_buf.at[m, place])
        elif da == 1:
            self.go(m, 24 + dz, self.b_buf.at[m, place], self.t_buf.at[m, dz], self.me.device(da=1))

    def a_step(self, m, k):
        dz = self.dz_of(k)
        self.wait(m, 24 + dz)
        self.t_buf[m, dz] = self.t_buf[m, dz] + self.b_buf[m, 2 * dz]
        self.z_out(m, dz, 0, self.t_buf.at[m, dz])

    def z_step(self, m, da, j):
        @pl.when(self.mid)
        def _():
            owner = flip(self.far % 2, j) + 2 * (1 - self.half)
            way, end = self.way(m, da, j), self.end(m, da, 1)
            self.wait(m, 24 + way)
            self.t_buf[m, way] = self.t_buf[m, way] + self.source(m, self.back(owner), da)[...]
            self.go(m, 24 + end, self.t_buf.at[m, way], self.t_buf.at[m, end], self.z_peer(owner), leave=24 + way)

    def last_step(self, m):
        near, far = self.end(m, 1, 0), self.end(m, 1, 1)
        self.wait(m, 24 + near)
        self.wait(m, 24 + far)
        self.t_buf[m, near] = self.t_buf[m, near] + self.t_buf[m, far] + self.b_buf[m, 1]
        self.go(m, 32, self.t_buf.at[m, near], self.t_buf.at[m, 8], self.me.device(da=1))

    def run(self, steps):
        for op, m, q in parse(steps):
            if op == "b":
                self.b_step(m, 3 - q // 2, 1 - q % 2)
            elif op == "c":
                self.b_step(m, 3 - q % 4, 1 - q // 4)
            elif op == "a":
                self.a_step(m, 3 - q)
            elif op == "z":
                self.z_step(m, (1 - q // 2) * self.modes[m], 1 - q % 2)
            elif op == "e":
                self.last_step(m)
            else:
                self.finish(m)

    def finish(self, m):
        wide = lambda ref: ref[...].astype(jnp.float32)
        near = self.end(m, 0, 0)
        self.wait(m, 24 + near)
        self.wait(m, 25 + near)
        total = wide(self.source(m, 0, 0)) + wide(self.t_buf.at[m, near]) + wide(self.t_buf.at[m, near + 1])
        if self.modes[m] == 1:
            self.wait(m, 32)
            total = total + wide(self.t_buf.at[m, 8])
        self.out_ref[m] = total

    def drain(self):
        for m in range(3):
            left = lambda s: self.sem(m, s, s).wait_send()

            @pl.loop(0, 24)
            def _(s):
                left(s)

            for da in range(1 + self.modes[m]):
                for j in (self.way(m, da, 0), self.way(m, da, 1), self.end(m, da, 0)):
                    left(24 + j)
            for j in (8,) if self.modes[m] else range(Z_SIZE):
                left(24 + j)


class VectorSum:
    def __init__(self, me, buf, zbuf, send_sem, recv_sem):
        self.me, self.buf, self.zbuf, self.send_sem, self.recv_sem = me, buf, zbuf, send_sem, recv_sem

    def copy(self, step, src, dst, peer):
        return remote(src, dst, self.send_sem.at[step], self.recv_sem.at[step], peer)

    def peer(self, step):
        me = self.me
        if step == 0:
            return me.device(other=True)
        dx, dy = ((1, 0), (0, 1))[step - 1]
        return {"dp": me.z * 2 + flip(me.x, dx), "tensor": 2 * flip(me.y, dy) + me.c}

    def pair(self, step):
        return self.copy(step, self.buf.at[2 * step], self.buf.at[2 * step + 1], self.peer(step))

    def start(self, value):
        self.buf[0] = value
        self.pair(0).start()

    def advance(self, step):
        self.pair(step).wait()
        self.buf[2 * step + 2] = self.buf[2 * step] + self.buf[2 * step + 1]
        if step < 2:
            self.pair(step + 1).start()
        else:
            self.zbuf[self.me.z] = self.buf[6]
            for k in range(1, Z_SIZE):
                self.z_copy(k).start()

    def z_copy(self, k):
        return self.copy(2 + k, self.buf.at[6], self.zbuf.at[self.me.z], self.me.device(dz=k))

    def result(self):
        for k in range(1, Z_SIZE):
            self.z_copy(k).wait()
        return (self.zbuf[0] + self.zbuf[1]) + (self.zbuf[2] + self.zbuf[3])


def dot_nn(a, b):
    return lax.dot_general(a, b, (((1,), (0,)), ((), ())), preferred_element_type=jnp.float32)


def dot_nt(a, b):
    return lax.dot_general(a, b, (((1,), (1,)), ((), ())), preferred_element_type=jnp.float32)


def dot_tn(a, b):
    return lax.dot_general(a, b, (((0,), (0,)), ((), ())), preferred_element_type=jnp.float32)


def low(a):
    return a.astype(jnp.bfloat16)


def row_mean(a):
    return jnp.mean(a, axis=-1, keepdims=True)


def normalise(r):
    centre = r - row_mean(r)
    inverse = lax.rsqrt(row_mean(centre * centre) + NORM_EPS)
    return centre * inverse, inverse


def norm_back(g, z, inverse):
    return (g - row_mean(g) - z * row_mean(g * z)) * inverse


def gelu_pair(u):
    cdf = 0.5 + 0.5 * lax.erf(u * (0.5**0.5))
    density = jnp.exp(-0.5 * u * u) * ((0.5 / jnp.pi) ** 0.5)
    return u * cdf, cdf + u * density


V_BQ, V_BV, V_BO, V_G1, V_B1, V_BF, V_G2, V_B2, V_BI = range(9)
TILE = 64


class Layer:
    def __init__(self, **refs):
        self.__dict__.update(refs)
        self.rows, self.width = self.x.shape
        self.n_t = self.w.shape[1]
        self.cols = self.width // self.n_t
        self.heads = self.cols // HEAD_DIM
        self.ocol = (3 * self.cols) // 128 * 128

    def tiles(self, body):
        @pl.loop(0, self.rows // TILE)
        def _(i):
            body(pl.ds(pl.multiple_of(i * TILE, TILE), TILE))

    def project(self, t):
        lane = lax.broadcasted_iota(jnp.int32, (1, self.width), 1)
        out = dot_nn(self.x[...], self.w[0, t]) + self.qkv_bias[t]
        self.qkv[t] = low(jnp.where(lane < 3 * self.cols, out, 0.0))

    def piece(self, t, which, j):
        first = which * self.cols + j * HEAD_DIM
        return self.qkv.at[t, :, first : first + HEAD_DIM]

    def attend(self, t, valid, between):
        self.att[t, :, : HEAD_DIM] = jnp.zeros((self.rows, HEAD_DIM), jnp.bfloat16)
        for j in range(self.heads):
            q, k, v = (self.piece(t, i, j)[...] for i in range(3))
            s = dot_nt(k, q * jnp.bfloat16(HEAD_DIM**-0.5))
            s = jnp.where(valid, s, NEG_FILL)
            e = jnp.exp(s - jnp.max(s, axis=0, keepdims=True))
            p = low(e * (1.0 / jnp.sum(e, axis=0, keepdims=True)))
            self.p[t * self.heads + j] = p
            mix = dot_tn(v, p)
            first = 3 * self.cols - self.ocol + j * HEAD_DIM
            self.att[t, :, first : first + HEAD_DIM] = low(mix.T)
            between(j)

    def out_project(self, t):
        self.acc[...] += dot_nt(self.att[t], self.w[0, t, :, self.ocol :])

    def start_residual(self):
        self.acc[...] = self.x[...].astype(jnp.float32) + self.vec[2:3, :]

    def first_norm(self):
        def body(r):
            z, inverse = normalise(self.acc[r, :])
            self.z1[r, :] = z
            self.inv1[r, :] = jnp.broadcast_to(inverse, (TILE, 128))
            h1 = z * self.vec[3:4, :] + self.vec[4:5, :]
            self.h1b[r, :] = low(h1)
            self.acc[r, :] = h1 + self.vec[0:1, :]

        self.tiles(body)

    def inner(self, t):
        @pl.loop(0, self.rows // 128)
        def _(i):
            r = pl.ds(pl.multiple_of(i * 128, 128), 128)
            pre = dot_nn(self.h1b[r, :], self.w[1, t]) + self.inner_bias[t]
            act, slope = gelu_pair(pre)
            self.act[t, r, :] = low(act)
            self.slope[t, r, :] = low(slope)

    def outer(self, t):
        self.acc[...] += dot_nt(self.act[t], self.w[2, t])

    def second_norm(self, length):
        self.sums[...] = jnp.zeros_like(self.sums)

        def body(r):
            z, inverse = normalise(self.acc[r, :])
            place = r.start + lax.broadcasted_iota(jnp.int32, (TILE, 1), 0)
            mask = (place < length).astype(jnp.float32)
            gain = self.vec[5:6, :]
            self.y[r, :] = low((z * gain + self.vec[6:7, :]) * mask)
            dy = self.og[r, :].astype(jnp.float32) * mask
            dr2 = norm_back(dy * gain, z, inverse)
            self.acc[r, :] = dr2
            df = low(dr2)
            self.df[r, :] = df
            self.sums[V_G2] += fold(dy * z)
            self.sums[V_B2] += fold(dy)
            self.sums[V_BF] += fold(df.astype(jnp.float32))

        self.tiles(body)

    def outer_back(self, t):
        self.dact[...] = dot_nn(self.df[...], self.w[2, t])

        def body(r):
            d = low(self.dact[r, :] * self.slope[t, r, :].astype(jnp.float32))
            self.slope[t, r, :] = d
            self.sums[V_BI + t] += fold(d.astype(jnp.float32))

        self.tiles(body)
        self.w[2, t] = low(dot_nn(self.df_t[...], self.act[t]))

    def inner_back(self, t):
        self.acc[...] += dot_nt(self.slope[t], self.w[1, t])
        self.w[1, t] = low(dot_nn(self.h1b_t[...], self.slope[t]))

    def first_norm_back(self):
        def body(r):
            z = self.z1[r, :]
            dh1 = self.acc[r, :]
            self.sums[V_G1] += fold(dh1 * z)
            self.sums[V_B1] += fold(dh1)
            dr1 = norm_back(dh1 * self.vec[3:4, :], z, self.inv1[r, :1])
            self.acc[r, :] = dr1
            dob = low(dr1)
            self.df[r, :] = dob
            self.sums[V_BO] += fold(dob.astype(jnp.float32))

        self.tiles(body)

    def attend_back(self, t, between):
        scale = HEAD_DIM**-0.5
        self.datt[...] = low(dot_nn(self.df[...], self.w[0, t, :, self.ocol :]))
        for j in range(self.heads):
            first = 3 * self.cols - self.ocol + j * HEAD_DIM
            d = self.datt[:, first : first + HEAD_DIM]
            q, k, v = (self.piece(t, i, j)[...] for i in range(3))
            p = self.p[t * self.heads + j]
            dp = dot_nt(v, d)
            pf = p.astype(jnp.float32)
            delta = jnp.sum(pf * dp, axis=0, keepdims=True)
            ds = low(pf * (dp - delta))
            self.piece(t, 2, j)[...] = low(dot_nn(p, d))
            self.piece(t, 1, j)[...] = low(dot_nn(ds, q) * scale)
            self.piece(t, 0, j)[...] = low((dot_tn(k, ds) * scale).T)
            between(j)

    def head_sums(self, t):
        def body(r):
            self.sums[V_BI + self.n_t + t] += fold(self.qkv[t, r, :].astype(jnp.float32))

        self.tiles(body)

    def project_grad(self, t):
        self.w0_grad[t] = low(dot_nn(self.x_t[...], self.qkv[t]))
        out = self.w0_grad.at[t, :, self.ocol :]
        out[...] = low(out[...].astype(jnp.float32) + dot_nn(self.df_t[...], self.att[t]))

    def project_back(self, t):
        self.acc[...] += dot_nt(self.qkv[t], self.w[0, t])

    def transpose(self, src, dst):
        dst[...] = src[...].T


def fold(a):
    return jnp.sum(a.reshape(a.shape[0] // 8, 8, a.shape[1]), axis=0)


GATHER_MODES = (0, 1, 1)
SCATTER_MODES = (0, 1, 1)
GATHER_MODES = (0, 1, 1)
SCATTER_MODES = (0, 1, 1)
GATHER = {
    "first": ("A0:0", "y0:0", "B1:0"),
    "start": ("B0:0", "A2:0", "A1:0", "y1:0", "p0:4", "p0:1", "l0:0", "p0:2", "p1:2", "y2:0", "l0:1", "p0:5", "l0:4", "p0:3",
        "p0:6-7", "p1:1", "l0:5", "l1:2", "p2:2", "l0:6", "p2:1", "p1:5", "l0:3", "l0:2", "l0:7", "p1:3"),
    "attend": (),
    "heads": {3: ("l1:0",), 4: ("l1:5", "l1:1"), 5: ("l2:2", "p1:6"), 6: ("p1:4", "p2:5"), 8: ("l1:6", "l1:3"), 9: ("p2:3",),
        10: ("l1:4", "l2:0"), 11: ("p2:6",)},
    "out": {1: ("B2:0",), 2: ("l2:1", "p1:7"), 3: ("l1:7",)},
    "norm": ("p2:4",),
    "ffn": ("l2:6",),
    "inner": {0: ("p2:7",), 2: ("l2:4", "l2:3", "l2:5", "l2:7")},
}
SCATTER = {
    "outer": {},
    "inner": {0: ("b2:0",), 1: ("b2:2",), 2: ("b2:1", "z2:0", "b2:4", "b2:3")},
    "norm": ("b2:5",),
    "heads": {0: ("b1:2",), 2: ("z2:2", "b1:0"), 5: ("z2:3", "b2:6", "b1:1"), 7: ("b1:3", "b1:6"), 8: ("z1:1",), 9:
        ("e2:0",), 10: ("z1:0",)},
    "grad": {0: ("b1:4",), 1: ("z2:1",), 3: ("b0:0", "b1:7", "z1:2", "b0:2", "b1:5", "b0:4", "b0:1")},
    "last": ((), (), ("e1:0", "z1:3", "b0:6", "b0:3", "a0:0", "b0:5", "a0:1", "z0:0", "a0:2", "z0:1", "b0:7"), ("b2:7",
        "F2:0", "a0:3", "F1:0", "F0:0")),
}


def step_kernel(
    length_ref, x_in, og_in, wq, wk, wv, wo, w_inner, w_outer, b_outer, b_value, b_out, gain1, bias1, gain2, bias2, b_query, b_inner,
    y_ref, acc_ref, out_ref, vout_ref,
    x_ref, og_ref, parts, vec_ref, qkv_bias, inner_bias,
    w, sums, qkv, p, att, z1, inv1, h1b, ffn, df, datt, dact, x_t, h1b_t, df_t,
    core_buf, b_buf, t_buf, vec_buf, vec_z,
    load_sem, gather_send, gather_recv, send_sem, recv_sem, vec_send, vec_recv,
):
    me = Place()
    rows, width = x_ref.shape
    act, slope, w0_grad = ffn.at[:, :rows], ffn.at[:, rows:], ffn.at[:, :width]
    gather = Gather(me, GATHER_MODES, w, gather_send, gather_recv)
    scatter = Scatter(me, SCATTER_MODES, w, w0_grad, out_ref, core_buf, b_buf, t_buf, send_sem, recv_sem)
    small = VectorSum(me, vec_buf, vec_z, vec_send, vec_recv)
    a = Layer(
        x=x_ref, og=og_ref, w=w, w0_grad=w0_grad, qkv_bias=qkv_bias, inner_bias=inner_bias, vec=vec_ref, y=y_ref, acc=acc_ref, sums=sums,
        qkv=qkv, p=p, att=att, z1=z1, inv1=inv1, h1b=h1b, act=act, slope=slope, df=df, datt=datt, dact=dact, x_t=x_t, h1b_t=h1b_t, df_t=df_t,
    )
    vectors = (b_outer, b_value, b_out, gain1, bias1, gain2, bias2, b_query)
    pairs = [(ref, parts.at[i]) for i, ref in enumerate((wq, wk, wv, wo))]
    pairs += [(w_inner, gather.own(1)), (w_outer, gather.own(2)), (x_in, x_ref), (b_inner, inner_bias)]
    pairs += [(ref, vec_ref.at[i]) for i, ref in enumerate(vectors)] + [(og_in, og_ref)]
    loads = [pltpu.make_async_copy(src, dst, load_sem.at[i]) for i, (src, dst) in enumerate(pairs)]
    for load in loads:
        load.start()

    def at(run, slots, i):
        for n, steps in slots.items():

            @pl.when(i == n)
            def _():
                run(steps)

    def heads(run, slots, i, j):
        at(run, {n // a.heads: steps for n, steps in slots.items() if n % a.heads == j}, i)

    greet(me)
    for load in loads[:6]:
        load.wait()
    packed = gather.own(0)
    for i in range(4):
        packed[:, i * a.cols : (i + 1) * a.cols] = parts[i]
    meet(me)
    gather.run(GATHER["first"])
    for load in loads[6:]:
        load.wait()
    for t in range(a.n_t):
        here = slice(t * a.cols, (t + 1) * a.cols)
        qkv_bias[t] = jnp.zeros((1, width), jnp.float32)
        qkv_bias[t, :, : a.cols] = vec_ref[7:8, here]
        qkv_bias[t, :, 2 * a.cols : 3 * a.cols] = vec_ref[1:2, here]
    length = length_ref[me.t]
    valid = lax.broadcasted_iota(jnp.int32, (a.rows, 1), 0) < length
    a.transpose(a.x, a.x_t)
    a.start_residual()
    gather.run(GATHER["start"])
    gather.collect(0)
    gather.run(GATHER["attend"])

    @pl.loop(0, a.n_t)
    def _(t):
        a.project(t)
        a.attend(t, valid, lambda j: heads(gather.run, GATHER["heads"], t, j))
        a.out_project(t)
        at(gather.run, GATHER["out"], t)

    a.first_norm()
    a.transpose(a.h1b, a.h1b_t)
    gather.run(GATHER["norm"])
    gather.collect(1)
    gather.run(GATHER["ffn"])

    @pl.loop(0, a.n_t)
    def _(t):
        a.inner(t)
        at(gather.run, GATHER["inner"], t)

    gather.collect(2)

    @pl.loop(0, a.n_t)
    def _(t):
        a.outer(t)

    a.second_norm(length)
    a.transpose(a.df, a.df_t)
    gather.drain()

    @pl.loop(0, a.n_t)
    def _(i):
        a.outer_back(scatter.order(i))
        scatter.ready(2, i)
        at(scatter.run, SCATTER["outer"], i)

    @pl.loop(0, a.n_t)
    def _(i):
        a.inner_back(scatter.order(i))
        scatter.ready(1, i)
        at(scatter.run, SCATTER["inner"], i)

    a.first_norm_back()
    a.transpose(a.df, a.df_t)
    scatter.run(SCATTER["norm"])

    @pl.loop(0, a.n_t)
    def _(i):
        t = scatter.order(i)
        a.attend_back(t, lambda j: heads(scatter.run, SCATTER["heads"], i, j))
        a.head_sums(t)

        @pl.when(i == a.n_t - 1)
        def _():
            small.start(jnp.sum(sums[...], axis=1))

        a.project_grad(t)

        @pl.when(i == a.n_t - 1)
        def _():
            small.advance(0)

        scatter.ready(0, i)
        at(scatter.run, SCATTER["grad"], i)

    for t, steps in enumerate(SCATTER["last"]):
        a.project_back(t)
        if t in (1, 3):
            small.advance((t + 1) // 2)
        scatter.run(steps)
    vout_ref[...] = small.result()
    scatter.drain()


def step(seq_lengths, x, og, weights, vectors, b_inner, n_t):
    rows, width = x.shape
    cols = width // n_t
    heads = width // HEAD_DIM
    owidth = width - (3 * cols) // 128 * 128
    shard = weights[0].shape[0]
    bf, f32 = jnp.bfloat16, jnp.float32
    vmem, anywhere = pl.BlockSpec(memory_space=pltpu.VMEM), pl.BlockSpec(memory_space=pl.ANY)
    n_v = V_BI + 2 * n_t
    n_w = shard * lax.axis_size("dp")
    buf = lambda n: pltpu.VMEM((3, n, shard, width), bf)
    dma = pltpu.SemaphoreType.DMA
    n_loads = 3 + len(weights) + len(vectors)
    return pl.pallas_call(
        step_kernel,
        out_shape=(
            jax.ShapeDtypeStruct((rows, width), bf),
            jax.ShapeDtypeStruct((rows, width), f32),
            jax.ShapeDtypeStruct((3, shard, width), f32),
            jax.ShapeDtypeStruct((n_v, width), f32),
        ),
        in_specs=[pl.BlockSpec(memory_space=pltpu.SMEM)] + [anywhere] * n_loads,
        out_specs=[vmem] * 4,
        scratch_shapes=[
            pltpu.VMEM((rows, width), bf),
            pltpu.VMEM((rows, width), bf),
            pltpu.VMEM((4, shard, cols), bf),
            pltpu.VMEM((len(vectors), width), f32),
            pltpu.VMEM((n_t, 1, width), f32),
            pltpu.VMEM((n_t, 1, width), f32),
            pltpu.VMEM((3, n_t, n_w, width), bf),
            pltpu.VMEM((n_v, 8, width), f32),
            pltpu.VMEM((n_t, rows, width), bf),
            pltpu.VMEM((heads, rows, rows), bf),
            pltpu.VMEM((n_t, rows, owidth), bf),
            pltpu.VMEM((rows, width), f32),
            pltpu.VMEM((rows, 128), f32),
            pltpu.VMEM((rows, width), bf),
            pltpu.VMEM((n_t, max(2 * rows, width), width), bf),
            pltpu.VMEM((rows, width), bf),
            pltpu.VMEM((rows, owidth), bf),
            pltpu.VMEM((rows, width), f32),
            pltpu.VMEM((width, rows), bf),
            pltpu.VMEM((width, rows), bf),
            pltpu.VMEM((width, rows), bf),
            buf(16),
            buf(8),
            buf(9),
            pltpu.VMEM((7, n_v, width), f32),
            pltpu.VMEM((Z_SIZE, n_v, width), f32),
            dma((n_loads,)),
            dma((3, 36)),
            dma((3, 36)),
            dma((3, 33)),
            dma((3, 33)),
            dma((6,)),
            dma((6,)),
        ],
        compiler_params=pltpu.CompilerParams(collective_id=0, has_side_effects=True, vmem_limit_bytes=63 * 2**20),
    )(seq_lengths, x, og, *weights, *vectors, b_inner)


def place_kernel(n_t, y_in, gin_in, shards, sums, y, gin, gq, gk, gv, go, gi, gf, bq, bv, bo, g1, b1, bi, bf, g2, b2, y_buf, gin_buf, sems):
    first = [pltpu.make_async_copy(y_in, y_buf, sems.at[0]), pltpu.make_async_copy(gin_in, gin_buf, sems.at[1])]
    then = [pltpu.make_async_copy(y_buf, y, sems.at[2]), pltpu.make_async_copy(gin_buf, gin, sems.at[3])]
    direct = [pltpu.make_async_copy(shards.at[i], ref, sems.at[3 + i]) for i, ref in ((1, gi), (2, gf))]
    for copy in first + direct:
        copy.start()
    cols = gq.shape[1]
    for i, ref in enumerate((gq, gk, gv, go)):
        ref[...] = shards[0, :, i * cols : (i + 1) * cols]
    for row, ref in ((V_BO, bo), (V_G1, g1), (V_B1, b1), (V_BF, bf), (V_G2, g2), (V_B2, b2)):
        ref[...] = sums[row : row + 1, :].reshape(ref.shape)
    for t in range(n_t):
        bi[t] = sums[V_BI + t : V_BI + t + 1, :]
    heads = [sums[V_BI + n_t + t : V_BI + n_t + t + 1, :] for t in range(n_t)]
    bq[...] = jnp.concatenate([h[:, :cols] for h in heads], axis=1).reshape(bq.shape)
    bv[...] = jnp.concatenate([h[:, 2 * cols : 3 * cols] for h in heads], axis=1).reshape(bv.shape)
    for copy, after in zip(first, then):
        copy.wait()
        after.start()
    for copy in direct + then:
        copy.wait()


def place(y, gin, shards, sums, n_t):
    shard, width = shards.shape[1:]
    cols = width // n_t
    f32 = jnp.float32
    vmem, anywhere = pl.BlockSpec(memory_space=pltpu.VMEM), pl.BlockSpec(memory_space=pl.ANY)
    row = jax.ShapeDtypeStruct((width,), f32)
    return pl.pallas_call(
        functools.partial(place_kernel, n_t),
        out_shape=(
            [jax.ShapeDtypeStruct(y.shape, y.dtype), jax.ShapeDtypeStruct(gin.shape, f32)]
            + [jax.ShapeDtypeStruct((shard, cols), f32)] * 4
            + [jax.ShapeDtypeStruct((shard, width), f32)] * 2
            + [row] * 5
            + [jax.ShapeDtypeStruct((n_t, 1, width), f32)]
            + [row] * 3
        ),
        in_specs=[anywhere, anywhere, vmem, vmem],
        out_specs=[anywhere] * 2 + [vmem] * 4 + [anywhere] * 2 + [vmem] * 9,
        scratch_shapes=[pltpu.VMEM(y.shape, y.dtype), pltpu.VMEM(gin.shape, f32), pltpu.SemaphoreType.DMA((6,))],
    )(y, gin, shards, sums)


def data_parallel(
    hidden_in, seq_lengths, w_query, b_query, w_key, w_value, b_value, w_out, b_out, norm1_gain, norm1_bias,
    w_inner, b_inner, w_outer, b_outer, norm2_gain, norm2_bias, out_grad,
):
    n_t = lax.axis_size("tensor")
    width = hidden_in.shape[1]
    vectors = (b_outer, b_value, b_out, norm1_gain, norm1_bias, norm2_gain, norm2_bias, b_query)
    weights = (w_query, w_key, w_value, w_out, w_inner, w_outer)
    done = step(seq_lengths, hidden_in, out_grad, weights, vectors, b_inner.reshape(n_t, 1, width), n_t)
    y, gin, gq, gk, gv, go, gi, gf, *small = place(*done, n_t)
    bq, bv, bo, g1, b1, bi, bf, g2, b2 = small
    return y, gin, gq, bq, gk, gv, bv, go, bo, g1, b1, gi, bi.reshape(-1), gf, bf, g2, b2


def solution(mesh):
    in_specs = (
        P(("dp", "tensor"), None),
        P("dp"),
        P("dp", "tensor"),
        P(),
        P("dp", "tensor"),
        P("dp", "tensor"),
        P(),
        P("dp", "tensor"),
        P(),
        P(),
        P(),
        P("dp", "tensor"),
        P(),
        P("dp", "tensor"),
        P(),
        P(),
        P(),
        P(("dp", "tensor"), None),
    )
    out_specs = (
        P(("dp", "tensor"), None),
        P(("dp", "tensor"), None),
        P("dp", "tensor"),
        P(),
        P("dp", "tensor"),
        P("dp", "tensor"),
        P(),
        P("dp", "tensor"),
        P(),
        P(),
        P(),
        P("dp", "tensor"),
        P(),
        P("dp", "tensor"),
        P(),
        P(),
        P(),
    )
    small = mesh.shape["dp"] == 2 * Z_SIZE and mesh.shape["tensor"] == 4
    return jax.shard_map(
        data_parallel if small else per_device, mesh=mesh, in_specs=in_specs, out_specs=out_specs, check_vma=False
    )
```

```python
import functools

import jax
import jax.numpy as jnp
from jax import lax
from jax.experimental import pallas as pl
from jax.experimental.pallas import tpu as pltpu
from jax.sharding import PartitionSpec as P

HEAD_DIM = 64


NEG_FILL = -1000000000.0
NORM_EPS = 1e-12


def layer_norm(residual, norm_gain, norm_bias):
    centre = residual - jnp.mean(residual, axis=-1, keepdims=True)
    spread = jnp.mean(centre * centre, axis=-1, keepdims=True)
    return centre * lax.rsqrt(spread + NORM_EPS) * norm_gain + norm_bias


def exact_gelu(values):
    return jax.nn.gelu(values, approximate=False)


def contract_last(first_op, second_op):
    return lax.dot_general(
        first_op, second_op, (((1,), (1,)), ((), ())), preferred_element_type=jnp.float32
    )


def contract_first(first_op, second_op):
    return lax.dot_general(
        first_op, second_op, (((0,), (0,)), ((), ())), preferred_element_type=jnp.float32
    )


def split_blocks(heads_arr, block_rows):
    batches, length, head_size = heads_arr.shape
    return heads_arr.reshape(batches, length // block_rows, block_rows, head_size).transpose(
        1, 0, 2, 3
    )


def join_blocks(block_array):
    block_count, batches, block_rows, head_size = block_array.shape
    return block_array.transpose(1, 0, 2, 3).reshape(batches, block_count * block_rows, head_size)


def block_scores(query_portion, key_head_tensor, key_valid, score_scale):
    scores = (
        jnp.einsum(
            "eix,evx->eiv", query_portion, key_head_tensor, preferred_element_type=jnp.float32
        )
        * score_scale
    )
    return jnp.where(key_valid[:, None, :], scores, NEG_FILL)


def attend(query_heads, key_head_tensor, value_head_tensor, key_valid, block_rows, score_scale):

    def one_block(query_portion):
        scores = block_scores(query_portion, key_head_tensor, key_valid, score_scale)
        row_max = jnp.max(scores, axis=-1, keepdims=True)
        exponent = jnp.exp(scores - row_max)
        row_total = jnp.sum(exponent, axis=-1, keepdims=True)
        softmax_reduced = (exponent / row_total).astype(jnp.bfloat16)
        mixture = jnp.einsum(
            "fwj,fjt->fwt", softmax_reduced, value_head_tensor, preferred_element_type=jnp.float32
        )
        return (mixture.astype(jnp.bfloat16), row_max, row_total)

    mixture, row_max, row_total = lax.map(one_block, split_blocks(query_heads, block_rows))
    return (join_blocks(mixture), row_max, row_total)


def attend_back(
    query_heads,
    key_head_tensor,
    value_head_tensor,
    grad_heads,
    row_max,
    row_total,
    key_valid,
    block_rows,
    score_scale,
):

    def one_block(running, block_in):
        key_grad, value_grad = running
        query_portion, gradient_portion, max_part, total_part = block_in
        scores = block_scores(query_portion, key_head_tensor, key_valid, score_scale)
        softmax = jnp.exp(scores - max_part) / total_part
        softmax_reduced = softmax.astype(jnp.bfloat16)
        soft_grad = jnp.einsum(
            "eix,evx->eiv", gradient_portion, value_head_tensor, preferred_element_type=jnp.float32
        )
        centre = jnp.sum(softmax * soft_grad, axis=-1, keepdims=True)
        score_gradient = (softmax * (soft_grad - centre)).astype(jnp.bfloat16)
        query_grad = (
            jnp.einsum(
                "fwj,fjt->fwt", score_gradient, key_head_tensor, preferred_element_type=jnp.float32
            )
            * score_scale
        )
        key_grad = (
            key_grad
            + jnp.einsum(
                "oxl,oxn->oln", score_gradient, query_portion, preferred_element_type=jnp.float32
            )
            * score_scale
        )
        value_grad = value_grad + jnp.einsum(
            "oxl,oxn->oln", softmax_reduced, gradient_portion, preferred_element_type=jnp.float32
        )
        return ((key_grad, value_grad), query_grad)

    zero_grads = jnp.zeros(key_head_tensor.shape, jnp.float32)
    block_inputs = (
        split_blocks(query_heads, block_rows),
        split_blocks(grad_heads, block_rows),
        row_max,
        row_total,
    )
    (key_grad, value_grad), query_grad = lax.scan(one_block, (zero_grads, zero_grads), block_inputs)
    return (join_blocks(query_grad), key_grad, value_grad)


def per_device(
    hidden_in,
    seq_lengths,
    w_query,
    b_query,
    w_key,
    w_value,
    b_value,
    w_out,
    b_out,
    norm1_gain,
    norm1_bias,
    w_inner,
    b_inner,
    w_outer,
    b_outer,
    norm2_gain,
    norm2_bias,
    out_grad,
):
    tensor_size = lax.axis_size("tensor")
    tensor_place = lax.axis_index("tensor")
    local_rows, feature_width = hidden_in.shape
    group_rows = local_rows * tensor_size
    seq_count = seq_lengths.shape[0]
    seq_len = group_rows // seq_count
    head_cols = w_query.shape[1]
    inner_cols = w_inner.shape[1]
    heads_here = head_cols // HEAD_DIM
    block_rows = min(512, seq_len)
    score_scale = HEAD_DIM ** (-0.5)
    local_start = tensor_place * local_rows
    row_index = lax.iota(jnp.int32, group_rows)
    seq_match = (row_index[:, None] // seq_len == lax.iota(jnp.int32, seq_count)[None, :]).astype(
        jnp.int32
    )
    row_limit = jnp.sum(seq_match * seq_lengths[None, :], axis=1)
    row_valid = row_index % seq_len < row_limit
    local_mask = lax.dynamic_slice_in_dim(row_valid, local_start, local_rows).astype(jnp.float32)[
        :, None
    ]
    key_valid = jnp.repeat(row_valid.reshape(seq_count, seq_len), heads_here, axis=0)

    def heads_of(matrix):
        shaped = matrix.reshape(seq_count, seq_len, heads_here, HEAD_DIM).transpose(0, 2, 1, 3)
        return shaped.reshape(seq_count * heads_here, seq_len, HEAD_DIM)

    def rows_of(matrix):
        shaped = matrix.reshape(seq_count, heads_here, seq_len, HEAD_DIM).transpose(0, 2, 1, 3)
        return shaped.reshape(group_rows, head_cols)

    full_query, full_key, full_value, full_out, full_inner, full_outer = (
        lax.all_gather(w_query, "dp", axis=0, tiled=True),
        lax.all_gather(w_key, "dp", axis=0, tiled=True),
        lax.all_gather(w_value, "dp", axis=0, tiled=True),
        lax.all_gather(w_out, "dp", axis=0, tiled=True),
        lax.all_gather(w_inner, "dp", axis=0, tiled=True),
        lax.all_gather(w_outer, "dp", axis=0, tiled=True),
    )
    joint_weight = jnp.concatenate((full_query, full_key, full_value), axis=1)
    query_bias = lax.dynamic_slice_in_dim(b_query, tensor_place * head_cols, head_cols)
    value_bias = lax.dynamic_slice_in_dim(b_value, tensor_place * head_cols, head_cols)
    inner_bias = lax.dynamic_slice_in_dim(b_inner, tensor_place * inner_cols, inner_cols)
    joint_bias = jnp.concatenate((query_bias, jnp.zeros((head_cols,), jnp.float32), value_bias))
    whole_in = lax.all_gather(hidden_in, "tensor", axis=0, tiled=True)
    joint_rows = (
        jnp.dot(whole_in, joint_weight, preferred_element_type=jnp.float32) + joint_bias
    ).astype(jnp.bfloat16)
    query_heads = heads_of(joint_rows[:, :head_cols])
    key_head_tensor = heads_of(joint_rows[:, head_cols : 2 * head_cols])
    value_head_tensor = heads_of(joint_rows[:, 2 * head_cols :])
    mixture_heads, row_max, row_total = attend(
        query_heads, key_head_tensor, value_head_tensor, key_valid, block_rows, score_scale
    )
    mixture = rows_of(mixture_heads)
    summed_out = lax.psum_scatter(
        contract_last(mixture, full_out).astype(jnp.bfloat16),
        "tensor",
        scatter_dimension=0,
        tiled=True,
    ).astype(jnp.float32)
    first_sum = hidden_in.astype(jnp.float32) + (summed_out + b_out)
    first_norm = layer_norm(first_sum, norm1_gain, norm1_bias)
    mid_whole = lax.all_gather(first_norm.astype(jnp.bfloat16), "tensor", axis=0, tiled=True)
    pre_act = jnp.dot(mid_whole, full_inner, preferred_element_type=jnp.float32) + inner_bias
    act_low = exact_gelu(pre_act).astype(jnp.bfloat16)
    second_sum = first_norm + (
        lax.psum_scatter(
            contract_last(act_low, full_outer).astype(jnp.bfloat16),
            "tensor",
            scatter_dimension=0,
            tiled=True,
        ).astype(jnp.float32)
        + b_outer
    )
    normed, norm2_back = jax.vjp(layer_norm, second_sum, norm2_gain, norm2_bias)
    layer_out = (normed * local_mask).astype(jnp.bfloat16)
    out_cot = out_grad.astype(jnp.float32) * local_mask
    dsecond, gain2_part, bias2_part = norm2_back(out_cot)
    dffn_low = dsecond.astype(jnp.bfloat16)
    outer_bias_part = jnp.sum(dffn_low, axis=0, dtype=jnp.float32)
    dffn_whole = lax.all_gather(dffn_low, "tensor", axis=0, tiled=True)
    grad_outer = contract_first(dffn_whole, act_low)
    dact = jnp.dot(dffn_whole, full_outer, preferred_element_type=jnp.float32)
    _, gelu_back = jax.vjp(exact_gelu, pre_act)
    dpre_low = gelu_back(dact)[0].astype(jnp.bfloat16)
    inner_bias_part = jnp.sum(dpre_low, axis=0, dtype=jnp.float32)
    grad_inner = contract_first(mid_whole, dpre_low)
    dfirst_norm = dsecond + lax.psum_scatter(
        contract_last(dpre_low, full_inner).astype(jnp.bfloat16),
        "tensor",
        scatter_dimension=0,
        tiled=True,
    ).astype(jnp.float32)
    _, norm1_back = jax.vjp(layer_norm, first_sum, norm1_gain, norm1_bias)
    dfirst, gain1_part, bias1_part = norm1_back(dfirst_norm)
    dattn_low = dfirst.astype(jnp.bfloat16)
    out_bias_part = jnp.sum(dattn_low, axis=0, dtype=jnp.float32)
    dattn_whole = lax.all_gather(dattn_low, "tensor", axis=0, tiled=True)
    grad_out_w = contract_first(dattn_whole, mixture)
    dmixture = jnp.dot(dattn_whole, full_out, preferred_element_type=jnp.float32).astype(
        jnp.bfloat16
    )
    dquery_heads, dkey_heads, dvalue_heads = attend_back(
        query_heads,
        key_head_tensor,
        value_head_tensor,
        heads_of(dmixture),
        row_max,
        row_total,
        key_valid,
        block_rows,
        score_scale,
    )
    djoint = jnp.concatenate(
        (rows_of(dquery_heads), rows_of(dkey_heads), rows_of(dvalue_heads)), axis=1
    ).astype(jnp.bfloat16)
    joint_bias_part = jnp.sum(djoint, axis=0, dtype=jnp.float32)
    grad_joint = contract_first(whole_in, djoint)
    grad_in = dfirst + lax.psum_scatter(
        contract_last(djoint, joint_weight).astype(jnp.bfloat16),
        "tensor",
        scatter_dimension=0,
        tiled=True,
    ).astype(jnp.float32)
    grad_query = grad_joint[:, :head_cols]
    grad_key = grad_joint[:, head_cols : 2 * head_cols]
    grad_value = grad_joint[:, 2 * head_cols :]
    shard_grads = tuple(
        (
            lax.psum_scatter(grad_query, "dp", scatter_dimension=0, tiled=True),
            lax.psum_scatter(grad_key, "dp", scatter_dimension=0, tiled=True),
            lax.psum_scatter(grad_value, "dp", scatter_dimension=0, tiled=True),
            lax.psum_scatter(grad_out_w, "dp", scatter_dimension=0, tiled=True),
            lax.psum_scatter(grad_inner, "dp", scatter_dimension=0, tiled=True),
            lax.psum_scatter(grad_outer, "dp", scatter_dimension=0, tiled=True),
        )
    )

    def placed(vector, total_len):
        return lax.dynamic_update_slice_in_dim(
            jnp.zeros((total_len,), jnp.float32), vector, tensor_place * vector.shape[0], 0
        )

    query_bias_part = placed(joint_bias_part[:head_cols], feature_width)
    value_bias_part = placed(joint_bias_part[2 * head_cols :], feature_width)
    hidden_bias_part = placed(inner_bias_part, b_inner.shape[0])
    vector_sums = lax.psum(
        (
            query_bias_part,
            value_bias_part,
            out_bias_part,
            gain1_part,
            bias1_part,
            hidden_bias_part,
            outer_bias_part,
            gain2_part,
            bias2_part,
        ),
        ("dp", "tensor"),
    )
    return (
        layer_out,
        grad_in,
        shard_grads[0],
        vector_sums[0],
        shard_grads[1],
        shard_grads[2],
        vector_sums[1],
        shard_grads[3],
        vector_sums[2],
        vector_sums[3],
        vector_sums[4],
        shard_grads[4],
        vector_sums[5],
        shard_grads[5],
        vector_sums[6],
        vector_sums[7],
        vector_sums[8],
    )


Z_SIZE = 4
MESH_IDS = pl.DeviceIdType.MESH


def flip(place, bit):
    return place + bit - 2 * place * bit


class Place:
    def __init__(self):
        self.dp = lax.axis_index("dp")
        self.t = lax.axis_index("tensor")
        self.z = self.dp // 2
        self.x = self.dp % 2
        self.y = self.t // 2
        self.c = self.t % 2

    def chip(self, dz, da, db):
        c = self.c
        z = lax.rem(self.z - dz + Z_SIZE, Z_SIZE)
        x = flip(self.x, da * c + db * (1 - c))
        y = flip(self.y, da * (1 - c) + db * c)
        return z * 2 + x, y

    def device(self, dz=0, da=0, db=0, other=False):
        dp, y = self.chip(dz, da, db)
        core = 1 - self.c if other else self.c
        return {"dp": dp, "tensor": y * 2 + core}


def block_of(ref, m, dp, t, rows):
    return ref.at[m, t, pl.ds(pl.multiple_of(dp * rows, rows), rows), :]


def peers_of(me):
    return [me.device(dz=k) for k in range(1, Z_SIZE)] + [me.device(da=1), me.device(db=1), me.device(other=True)]


def greet(me):
    for peer in peers_of(me):
        pl.semaphore_signal(pltpu.get_barrier_semaphore(), inc=1, device_id=peer, device_id_type=MESH_IDS)


def meet(me):
    pl.semaphore_wait(pltpu.get_barrier_semaphore(), len(peers_of(me)))


def remote(src, dst, send, recv, peer):
    return pltpu.make_async_remote_copy(
        src_ref=src, dst_ref=dst, send_sem=send, recv_sem=recv, device_id=peer, device_id_type=MESH_IDS
    )


def parse(steps):
    for step in steps:
        first, _, stop = step[3:].partition("-")
        for q in range(int(first or 0), int(stop or first or 0) + 1):
            yield step[0], int(step[1]), q


class Routes:
    def __init__(self, me):
        self.me = me
        self.half = me.z // 2
        self.far = 2 - self.half
        self.near = 2 * self.half + (1 - me.z % 2)
        self.mid = (me.z == 1) | (me.z == 2)

    def z_peer(self, z):
        return {"dp": z * 2 + self.me.x, "tensor": self.me.t}

    def dz_of(self, k):
        return lax.rem(k * self.half + (4 - k) * (1 - self.half), Z_SIZE)

    def back(self, z):
        return lax.rem(self.me.z - z + Z_SIZE, Z_SIZE)


class Gather(Routes):
    def __init__(self, me, modes, w, send_sem, recv_sem):
        super().__init__(me)
        self.modes, self.w = modes, w
        self.send_sem, self.recv_sem = send_sem, recv_sem
        self.rows = w.shape[2] // lax.axis_size("dp")

    def sem(self, m, send, recv):
        one = block_of(self.w, m, 0, 0, self.rows)
        return remote(one, one, self.send_sem.at[m, send], self.recv_sem.at[m, recv], self.me.device(db=1))

    def wait(self, m, slot):
        self.sem(m, slot, slot).wait_recv()

    def send(self, m, slot, dz, da, db, peer, leave=None):
        dp, y = self.me.chip(dz, da, db)
        dst = block_of(self.w, m, dp, y * 2 + self.me.c, self.rows)
        leave = slot if leave is None else leave
        remote(dst, dst, self.send_sem.at[m, leave], self.recv_sem.at[m, slot], peer).start()

    def z_slots(self, da):
        return [(4 * lax.rem(z - self.me.z + Z_SIZE, Z_SIZE) + 2 * da, z) for z in (self.far, self.near)]

    def z_send(self, m, da):
        for slot, z in self.z_slots(da):
            self.send(m, slot, 0, da, 0, self.z_peer(z))

    def own(self, m):
        return block_of(self.w, m, self.me.dp, self.me.t, self.rows)

    def place(self, m, q):
        if self.modes[m] == 0:
            return q % 4, q // 4
        return (0, q) if q < 2 else (1 + (q - 2) % 3, (q - 2) // 3)

    def pump(self, m, q):
        me = self.me
        k, da = self.place(m, q)
        dz = self.dz_of(k) if k else 0
        slot = 4 * dz + 2 * da
        self.wait(m, slot)
        if k in (1, 2) and (self.modes[m] == 1 or da == 0):

            @pl.when(self.mid)
            def _():
                there = lax.rem(self.near - me.z + dz + Z_SIZE, Z_SIZE)
                self.send(m, 4 * there + 2 * da, dz, da, 0, self.z_peer(self.near), leave=31 + 2 * da + k)

        if self.modes[m] == 0 and da == 0:
            self.send(m, 4 * dz + 2, dz, 0, 0, me.device(da=1))
        if self.modes[m] == 1 and k == 0:
            self.z_send(m, 1)
        self.send(m, slot + 1, dz, da, 0, me.device(db=1))
        self.send(m, 16 + slot, dz, da, 0, me.device(other=True))

    def last(self, m, q):
        k, da = self.place(m, q)
        dz = self.dz_of(k) if k else 0
        slot = 4 * dz + 2 * da + 1
        self.wait(m, slot)
        self.send(m, 16 + slot, dz, da, 1, self.me.device(other=True))

    def run(self, steps):
        me = self.me
        for op, m, q in parse(steps):
            if op == "A":
                self.send(m, 2, 0, 0, 0, me.device(da=1))
            elif op == "B":
                self.send(m, 1, 0, 0, 0, me.device(db=1))
                self.send(m, 16, 0, 0, 0, me.device(other=True))
            elif op == "y":
                self.z_send(m, 0)
            elif op == "p":
                self.pump(m, q)
            else:
                self.last(m, q)

    def collect(self, m, first=0, stop=4):
        @pl.loop(0, Z_SIZE)
        def _(dz):
            for s in range(first, stop):
                self.wait(m, 16 + 4 * dz + s)

    def drain(self, m):
        left = lambda s: self.sem(m, s, s).wait_send()
        for da in range(1 + self.modes[m]):
            for slot, _ in self.z_slots(da):
                left(slot)

            @pl.when(self.mid)
            def _():
                left(32 + 2 * da)
                left(33 + 2 * da)

        for dz in range(1 if self.modes[m] else Z_SIZE):
            left(4 * dz + 2)

        @pl.loop(0, 8)
        def _(s):
            left(2 * s + 1)

        @pl.loop(16, 32)
        def _(s):
            left(s)


class Scatter(Routes):
    def __init__(self, me, modes, w, w0_grad, out_ref, core_buf, b_buf, t_buf, send_sem, recv_sem):
        super().__init__(me)
        self.out_ref = out_ref
        self.modes, self.w, self.w0_grad = modes, w, w0_grad
        self.core_buf, self.b_buf, self.t_buf = core_buf, b_buf, t_buf
        self.send_sem, self.recv_sem = send_sem, recv_sem
        self.rows = b_buf.shape[2]

    def order(self, i):
        me = self.me
        return flip(me.y, 1 - i // 2) * 2 + flip(1 - me.c, i % 2)

    def part(self, m, dz, da, db, core):
        dp, y = self.me.chip(dz, da, db)
        if m == 0:
            return self.w0_grad.at[y * 2 + core, pl.ds(pl.multiple_of(dp * self.rows, self.rows), self.rows), :]
        return block_of(self.w, m, dp, y * 2 + core, self.rows)

    def sem(self, m, send, recv):
        one = self.b_buf.at[m, 0]
        return remote(one, one, self.send_sem.at[m, send], self.recv_sem.at[m, recv], self.me.device(db=1))

    def wait(self, m, slot):
        self.sem(m, slot, slot).wait_recv()

    def go(self, m, slot, src, dst, peer, leave=None):
        leave = slot if leave is None else leave
        remote(src, dst, self.send_sem.at[m, leave], self.recv_sem.at[m, slot], peer).start()

    def from_core(self, dz, da, db):
        return 4 * dz + 2 * db + da

    def ready(self, m, i):
        me = self.me
        c = me.c
        side = 1 - i // 2

        def where(s):
            other = 1 - s // 4
            return self.dz_of(3 - s % 4), side * (1 - c) + other * c, other * (1 - c) + side * c

        @pl.when(i % 2 == 0)
        def _():
            @pl.loop(0, 8)
            def _(s):
                dz, da, db = where(s)
                slot = 4 * dz + 2 * da + db
                self.go(m, slot, self.part(m, dz, da, db, 1 - c), self.core_buf.at[m, slot], me.device(other=True))

        @pl.when(i % 2 == 1)
        def _():
            @pl.loop(0, 8)
            def _(s):
                dz, da, db = where(s)
                slot = self.from_core(dz, da, db)
                self.wait(m, slot)
                self.core_buf[m, slot] = self.part(m, dz, da, db, c)[...] + self.core_buf[m, slot]

                @pl.when(db == 1)
                def _():
                    place = 2 * dz + da
                    self.go(m, 16 + place, self.core_buf.at[m, slot], self.b_buf.at[m, place], me.device(db=1))

    def way(self, m, da, j):
        return 2 * da + j if self.modes[m] else 4 + j

    def end(self, m, da, far):
        return (4 + 2 * da if self.modes[m] else 6) + far

    def z_out(self, m, dz, da, src):
        owner = lax.rem(self.me.z - dz + Z_SIZE, Z_SIZE)
        is_near = owner == self.near

        @pl.when(is_near)
        def _():
            j = self.end(m, da, 0)
            self.go(m, 24 + j, src, self.t_buf.at[m, j], self.z_peer(self.near))

        @pl.when(jnp.logical_not(is_near | self.mid) & (dz != 0))
        def _():
            j = self.way(m, da, 0) + (owner != self.far).astype(jnp.int32)
            self.go(m, 24 + j, src, self.t_buf.at[m, j], self.z_peer(self.near))

    def source(self, m, dz, da):
        return self.b_buf.at[m, 2 * dz + da] if self.modes[m] else self.t_buf.at[m, dz]

    def b_step(self, m, k, da):
        dz = self.dz_of(k)
        place = 2 * dz + da
        self.wait(m, 16 + place)
        self.b_buf[m, place] = self.b_buf[m, place] + self.core_buf[m, self.from_core(dz, da, 0)]
        if self.modes[m] == 1:
            self.z_out(m, dz, da, self.b_buf.at[m, place])
        elif da == 1:
            self.go(m, 24 + dz, self.b_buf.at[m, place], self.t_buf.at[m, dz], self.me.device(da=1))

    def a_step(self, m, k):
        dz = self.dz_of(k)
        self.wait(m, 24 + dz)
        self.t_buf[m, dz] = self.t_buf[m, dz] + self.b_buf[m, 2 * dz]
        self.z_out(m, dz, 0, self.t_buf.at[m, dz])

    def z_step(self, m, da, j):
        @pl.when(self.mid)
        def _():
            owner = flip(self.far % 2, j) + 2 * (1 - self.half)
            way, end = self.way(m, da, j), self.end(m, da, 1)
            self.wait(m, 24 + way)
            self.t_buf[m, way] = self.t_buf[m, way] + self.source(m, self.back(owner), da)[...]
            self.go(m, 24 + end, self.t_buf.at[m, way], self.t_buf.at[m, end], self.z_peer(owner), leave=24 + way)

    def last_step(self, m):
        near, far = self.end(m, 1, 0), self.end(m, 1, 1)
        self.wait(m, 24 + near)
        self.wait(m, 24 + far)
        self.t_buf[m, near] = self.t_buf[m, near] + self.t_buf[m, far] + self.b_buf[m, 1]
        self.go(m, 32, self.t_buf.at[m, near], self.t_buf.at[m, 8], self.me.device(da=1))

    def run(self, steps):
        for op, m, q in parse(steps):
            if op == "b":
                self.b_step(m, 3 - q // 2, 1 - q % 2)
            elif op == "c":
                self.b_step(m, 3 - q % 4, 1 - q // 4)
            elif op == "a":
                self.a_step(m, 3 - q)
            elif op == "z":
                self.z_step(m, (1 - q // 2) * self.modes[m], 1 - q % 2)
            elif op == "e":
                self.last_step(m)
            else:
                self.finish(m)

    def finish(self, m):
        wide = lambda ref: ref[...].astype(jnp.float32)
        near = self.end(m, 0, 0)
        self.wait(m, 24 + near)
        self.wait(m, 25 + near)
        total = wide(self.source(m, 0, 0)) + wide(self.t_buf.at[m, near]) + wide(self.t_buf.at[m, near + 1])
        if self.modes[m] == 1:
            self.wait(m, 32)
            total = total + wide(self.t_buf.at[m, 8])
        self.out_ref[m] = total

    def drain(self):
        for m in range(3):
            left = lambda s: self.sem(m, s, s).wait_send()

            @pl.loop(0, 24)
            def _(s):
                left(s)

            for da in range(1 + self.modes[m]):
                for j in (self.way(m, da, 0), self.way(m, da, 1), self.end(m, da, 0)):
                    left(24 + j)
            for j in (8,) if self.modes[m] else range(Z_SIZE):
                left(24 + j)


class VectorSum:
    def __init__(self, me, buf, zbuf, send_sem, recv_sem):
        self.me, self.buf, self.zbuf, self.send_sem, self.recv_sem = me, buf, zbuf, send_sem, recv_sem

    def copy(self, step, src, dst, peer):
        return remote(src, dst, self.send_sem.at[step], self.recv_sem.at[step], peer)

    def peer(self, step):
        me = self.me
        if step == 0:
            return me.device(other=True)
        dx, dy = ((1, 0), (0, 1))[step - 1]
        return {"dp": me.z * 2 + flip(me.x, dx), "tensor": 2 * flip(me.y, dy) + me.c}

    def pair(self, step):
        return self.copy(step, self.buf.at[2 * step], self.buf.at[2 * step + 1], self.peer(step))

    def start(self, value):
        self.buf[0] = value
        self.pair(0).start()

    def advance(self, step):
        self.pair(step).wait()
        self.buf[2 * step + 2] = self.buf[2 * step] + self.buf[2 * step + 1]
        if step < 2:
            self.pair(step + 1).start()
        else:
            self.zbuf[self.me.z] = self.buf[6]
            for k in range(1, Z_SIZE):
                self.z_copy(k).start()

    def z_copy(self, k):
        return self.copy(2 + k, self.buf.at[6], self.zbuf.at[self.me.z], self.me.device(dz=k))

    def result(self):
        for k in range(1, Z_SIZE):
            self.z_copy(k).wait()
        return (self.zbuf[0] + self.zbuf[1]) + (self.zbuf[2] + self.zbuf[3])


def dot_nn(a, b):
    return lax.dot_general(a, b, (((1,), (0,)), ((), ())), preferred_element_type=jnp.float32)


def dot_nt(a, b):
    return lax.dot_general(a, b, (((1,), (1,)), ((), ())), preferred_element_type=jnp.float32)


def dot_tn(a, b):
    return lax.dot_general(a, b, (((0,), (0,)), ((), ())), preferred_element_type=jnp.float32)


def low(a):
    return a.astype(jnp.bfloat16)


def row_mean(a):
    return jnp.mean(a, axis=-1, keepdims=True)


def normalise(r):
    centre = r - row_mean(r)
    inverse = lax.rsqrt(row_mean(centre * centre) + NORM_EPS)
    return centre * inverse, inverse


def norm_back(g, z, inverse):
    return (g - row_mean(g) - z * row_mean(g * z)) * inverse


def gelu_pair(u):
    cdf = 0.5 + 0.5 * lax.erf(u * (0.5**0.5))
    density = jnp.exp(-0.5 * u * u) * ((0.5 / jnp.pi) ** 0.5)
    return u * cdf, cdf + u * density


V_BQ, V_BV, V_BO, V_G1, V_B1, V_BF, V_G2, V_B2, V_BI = range(9)
TILE = 64


class Layer:
    def __init__(self, **refs):
        self.__dict__.update(refs)
        self.rows, self.width = self.x.shape
        self.n_t = self.w.shape[1]
        self.cols = self.width // self.n_t
        self.heads = self.cols // HEAD_DIM
        self.ocol = (3 * self.cols) // 128 * 128

    def tiles(self, body):
        @pl.loop(0, self.rows // TILE)
        def _(i):
            body(pl.ds(pl.multiple_of(i * TILE, TILE), TILE))

    def project(self, t):
        lane = lax.broadcasted_iota(jnp.int32, (1, self.width), 1)
        out = dot_nn(self.x[...], self.w[0, t]) + self.qkv_bias[t]
        self.qkv[t] = low(jnp.where(lane < 3 * self.cols, out, 0.0))

    def piece(self, t, which, j):
        first = which * self.cols + j * HEAD_DIM
        return self.qkv.at[t, :, first : first + HEAD_DIM]

    def attend(self, t, valid, between):
        self.att[t, :, : HEAD_DIM] = jnp.zeros((self.rows, HEAD_DIM), jnp.bfloat16)
        for j in range(self.heads):
            q, k, v = (self.piece(t, i, j)[...] for i in range(3))
            s = dot_nt(k, q * jnp.bfloat16(HEAD_DIM**-0.5))
            s = jnp.where(valid, s, NEG_FILL)
            e = jnp.exp(s - jnp.max(s, axis=0, keepdims=True))
            p = low(e * (1.0 / jnp.sum(e, axis=0, keepdims=True)))
            self.p[t * self.heads + j] = p
            mix = dot_tn(v, p)
            first = 3 * self.cols - self.ocol + j * HEAD_DIM
            self.att[t, :, first : first + HEAD_DIM] = low(mix.T)
            between(j)

    def out_project(self, t):
        self.acc[...] += dot_nt(self.att[t], self.w[0, t, :, self.ocol :])

    def start_residual(self):
        self.acc[...] = self.x[...].astype(jnp.float32) + self.vec[2:3, :]

    def first_norm(self):
        def body(r):
            z, inverse = normalise(self.acc[r, :])
            self.z1[r, :] = z
            self.inv1[r, :] = jnp.broadcast_to(inverse, (TILE, 128))
            h1 = z * self.vec[3:4, :] + self.vec[4:5, :]
            self.h1b[r, :] = low(h1)
            self.acc[r, :] = h1 + self.vec[0:1, :]

        self.tiles(body)

    def inner(self, t):
        @pl.loop(0, self.rows // 128)
        def _(i):
            r = pl.ds(pl.multiple_of(i * 128, 128), 128)
            pre = dot_nn(self.h1b[r, :], self.w[1, t]) + self.inner_bias[t]
            act, slope = gelu_pair(pre)
            self.act[t, r, :] = low(act)
            self.slope[t, r, :] = low(slope)

    def outer(self, t):
        self.acc[...] += dot_nt(self.act[t], self.w[2, t])

    def second_norm(self, length):
        self.sums[...] = jnp.zeros_like(self.sums)

        def body(r):
            z, inverse = normalise(self.acc[r, :])
            place = r.start + lax.broadcasted_iota(jnp.int32, (TILE, 1), 0)
            mask = (place < length).astype(jnp.float32)
            gain = self.vec[5:6, :]
            self.y[r, :] = low((z * gain + self.vec[6:7, :]) * mask)
            dy = self.og[r, :].astype(jnp.float32) * mask
            dr2 = norm_back(dy * gain, z, inverse)
            self.acc[r, :] = dr2
            df = low(dr2)
            self.df[r, :] = df
            self.sums[V_G2] += fold(dy * z)
            self.sums[V_B2] += fold(dy)
            self.sums[V_BF] += fold(df.astype(jnp.float32))

        self.tiles(body)

    def outer_back(self, t):
        half = self.rows // 2
        for i in range(2):
            r = slice(i * half, (i + 1) * half)
            d = dot_nn(self.df[r, :], self.w[2, t])
            self.slope[t, r, :] = low(d * self.slope[t, r, :].astype(jnp.float32))
        self.w[2, t] = low(dot_nn(self.df_t[...], self.act[t]))
        self.sums[V_BI + t] = self.column_sums(self.slope[t])

    def column_sums(self, a):
        first = lax.broadcasted_iota(jnp.int32, (16, self.rows), 0) == 0
        return dot_nn(low(first.astype(jnp.float32)), a)[:8]

    def inner_back(self, t):
        self.acc[...] += dot_nt(self.slope[t], self.w[1, t])
        self.w[1, t] = low(dot_nn(self.h1b_t[...], self.slope[t]))

    def first_norm_back(self):
        def body(r):
            z = self.z1[r, :]
            dh1 = self.acc[r, :]
            self.sums[V_G1] += fold(dh1 * z)
            self.sums[V_B1] += fold(dh1)
            dr1 = norm_back(dh1 * self.vec[3:4, :], z, self.inv1[r, :1])
            self.acc[r, :] = dr1
            dob = low(dr1)
            self.df[r, :] = dob
            self.sums[V_BO] += fold(dob.astype(jnp.float32))

        self.tiles(body)

    def attend_back(self, t, between):
        scale = HEAD_DIM**-0.5
        self.datt[...] = low(dot_nn(self.df[...], self.w[0, t, :, self.ocol :]))
        for j in range(self.heads):
            first = 3 * self.cols - self.ocol + j * HEAD_DIM
            d = self.datt[:, first : first + HEAD_DIM]
            q, k, v = (self.piece(t, i, j)[...] for i in range(3))
            p = self.p[t * self.heads + j]
            dp = dot_nt(v, d)
            pf = p.astype(jnp.float32)
            delta = jnp.sum(pf * dp, axis=0, keepdims=True)
            ds = low(pf * (dp - delta))
            self.piece(t, 2, j)[...] = low(dot_nn(p, d))
            self.piece(t, 1, j)[...] = low(dot_nn(ds, q) * scale)
            self.piece(t, 0, j)[...] = low((dot_tn(k, ds) * scale).T)
            between(j)

    def head_sums(self, t):
        self.sums[V_BI + self.n_t + t] = self.column_sums(self.qkv[t])

    def project_grad(self, t):
        self.w0_grad[t] = low(dot_nn(self.x_t[...], self.qkv[t]))
        out = self.w0_grad.at[t, :, self.ocol :]
        out[...] = low(out[...].astype(jnp.float32) + dot_nn(self.df_t[...], self.att[t]))

    def project_back(self, t):
        self.acc[...] += dot_nt(self.qkv[t], self.w[0, t])

    def transpose(self, src, dst):
        dst[...] = src[...].T


def fold(a):
    return jnp.sum(a.reshape(a.shape[0] // 8, 8, a.shape[1]), axis=0)


GATHER_MODES = (0, 1, 1)
SCATTER_MODES = (0, 1, 1)
GATHER_MODES = (0, 1, 1)
SCATTER_MODES = (0, 1, 1)
GATHER = {
    "first": ("y0:0", "A0:0", "A1:0", "p0:4", "B1:0", "y2:0", "B0:0", "l0:4", "p0:1"),
    "start": ("p0:2", "p1:1", "y1:0", "l0:0", "p0:3", "p0:6", "p0:5", "l0:2", "l0:1", "l1:1", "p0:7", "p2:2", "p1:2", "p1:5",
        "l0:5", "B2:0", "l0:6", "A2:0", "l0:3", "l0:7"),
    "attend": (),
    "heads": {4: ("l2:0", "p2:3", "p2:1"), 8: ("p1:4", "p1:7", "l1:0", "l1:5"), 10: ("l2:3",), 11: ("l1:4", "l2:2", "l1:6",
        "p2:4", "l1:3", "l1:2")},
    "out": {0: ("p1:6", "p1:3"), 3: ("p2:5", "l1:7")},
    "norm": (),
    "ffn": ("p2:6",),
    "inner": {1: ("p2:7", "l2:6", "l2:1", "l2:5", "l2:4"), 3: ("l2:7",)},
    "outer": {},
    "late": (),
}
SCATTER = {
    "outer": {3: ("b2:0",)},
    "inner": {0: ("b2:2",), 1: ("z2:0",), 2: ("b2:3", "b2:1", "b2:5")},
    "norm": ("b2:4", "b1:2", "b2:7"),
    "heads": {2: ("z2:1",), 4: ("z2:2-3",), 7: ("z1:1", "b1:6"), 8: ("b1:1", "z1:0")},
    "grad": {0: ("b1:0", "b1:4"), 1: ("b1:3",), 3: ("b1:5", "z1:2", "b0:0")},
    "last": (("z1:3", "b0:2"), ("b0:4", "b0:1"), ("a0:0", "b1:7", "b2:6", "e2:0", "e1:0", "b0:3", "b0:6", "a0:1", "b0:5",
        "z0:0", "b0:7"), ("a0:2", "z0:1", "F1:0", "F2:0", "a0:3", "F0:0")),
}


def step_kernel(
    length_ref, x_in, og_in, wq, wk, wv, wo, w_inner, w_outer, b_outer, b_value, b_out, gain1, bias1, gain2, bias2, b_query, b_inner,
    y_out, acc_out, shards_out, vout_ref,
    x_ref, og_ref, parts, vec_ref, qkv_bias, inner_bias,
    w, sums, qkv, p, att, z1, inv1, h1b, ffn, df, datt, x_t, h1b_t, df_t, y_ref, acc_ref, out_ref,
    core_buf, b_buf, t_buf, vec_buf, vec_z,
    load_sem, store_sem, gather_send, gather_recv, send_sem, recv_sem, vec_send, vec_recv,
):
    me = Place()
    rows, width = x_ref.shape
    act, slope, w0_grad = ffn.at[:, :rows], ffn.at[:, rows:], ffn.at[:, :width]
    gather = Gather(me, GATHER_MODES, w, gather_send, gather_recv)
    scatter = Scatter(me, SCATTER_MODES, w, w0_grad, out_ref, core_buf, b_buf, t_buf, send_sem, recv_sem)
    small = VectorSum(me, vec_buf, vec_z, vec_send, vec_recv)
    a = Layer(
        x=x_ref, og=og_ref, w=w, w0_grad=w0_grad, qkv_bias=qkv_bias, inner_bias=inner_bias, vec=vec_ref, y=y_ref, acc=acc_ref, sums=sums,
        qkv=qkv, p=p, att=att, z1=z1, inv1=inv1, h1b=h1b, act=act, slope=slope, df=df, datt=datt, x_t=x_t, h1b_t=h1b_t, df_t=df_t,
    )
    vectors = (b_outer, b_value, b_out, gain1, bias1, gain2, bias2, b_query)
    pairs = [(ref, parts.at[i]) for i, ref in enumerate((wq, wk, wv, wo))]
    pairs += [(w_inner, gather.own(1)), (w_outer, gather.own(2)), (x_in, x_ref), (b_inner, inner_bias)]
    pairs += [(ref, vec_ref.at[i]) for i, ref in enumerate(vectors)] + [(og_in, og_ref)]
    loads = [pltpu.make_async_copy(src, dst, load_sem.at[i]) for i, (src, dst) in enumerate(pairs)]
    for load in loads:
        load.start()

    def at(run, slots, i):
        for n, steps in slots.items():

            @pl.when(i == n)
            def _():
                run(steps)

    def heads(run, slots, i, j):
        at(run, {n // a.heads: steps for n, steps in slots.items() if n % a.heads == j}, i)

    greet(me)
    for load in loads[:6]:
        load.wait()
    packed = gather.own(0)
    for i in range(4):
        packed[:, i * a.cols : (i + 1) * a.cols] = parts[i]
    meet(me)
    gather.run(GATHER["first"])
    for load in loads[6:]:
        load.wait()
    for t in range(a.n_t):
        here = slice(t * a.cols, (t + 1) * a.cols)
        qkv_bias[t] = jnp.zeros((1, width), jnp.float32)
        qkv_bias[t, :, : a.cols] = vec_ref[7:8, here]
        qkv_bias[t, :, 2 * a.cols : 3 * a.cols] = vec_ref[1:2, here]
    length = length_ref[me.t]
    valid = lax.broadcasted_iota(jnp.int32, (a.rows, 1), 0) < length
    a.transpose(a.x, a.x_t)
    a.start_residual()
    gather.run(GATHER["start"])
    gather.collect(0)
    gather.run(GATHER["attend"])

    @pl.loop(0, a.n_t)
    def _(t):
        a.project(t)
        a.attend(t, valid, lambda j: heads(gather.run, GATHER["heads"], t, j))
        a.out_project(t)
        at(gather.run, GATHER["out"], t)

    a.first_norm()
    a.transpose(a.h1b, a.h1b_t)
    gather.run(GATHER["norm"])
    gather.collect(1)
    gather.run(GATHER["ffn"])

    @pl.loop(0, a.n_t)
    def _(t):
        a.inner(t)
        at(gather.run, GATHER["inner"], t)

    gather.collect(2, 0, 3)
    gather.run(GATHER["late"])

    @pl.loop(0, 2)
    def _(core):
        a.outer(2 * me.y + core)
        at(gather.run, GATHER["outer"], core)

    gather.collect(2, 3, 4)

    @pl.loop(0, 2)
    def _(core):
        a.outer(2 * (1 - me.y) + core)

    a.second_norm(length)
    a.transpose(a.df, a.df_t)
    stores = [(y_ref, y_out), (acc_ref, acc_out), (out_ref, shards_out)]
    stores = [pltpu.make_async_copy(src, dst, store_sem.at[i]) for i, (src, dst) in enumerate(stores)]
    stores[0].start()
    gather.drain(2)

    @pl.loop(0, a.n_t)
    def _(i):
        a.outer_back(scatter.order(i))
        scatter.ready(2, i)
        at(scatter.run, SCATTER["outer"], i)

    gather.drain(1)

    @pl.loop(0, a.n_t)
    def _(i):
        a.inner_back(scatter.order(i))
        scatter.ready(1, i)
        at(scatter.run, SCATTER["inner"], i)

    a.first_norm_back()
    a.transpose(a.df, a.df_t)
    scatter.run(SCATTER["norm"])

    @pl.loop(0, a.n_t)
    def _(i):
        t = scatter.order(i)
        a.attend_back(t, lambda j: heads(scatter.run, SCATTER["heads"], i, j))
        a.head_sums(t)

        @pl.when(i == a.n_t - 1)
        def _():
            small.start(jnp.sum(sums[...], axis=1))

        a.project_grad(t)

        @pl.when(i == a.n_t - 1)
        def _():
            small.advance(0)

        scatter.ready(0, i)
        at(scatter.run, SCATTER["grad"], i)

    for t, steps in enumerate(SCATTER["last"]):
        a.project_back(t)
        if t in (1, 3):
            small.advance((t + 1) // 2)
        scatter.run(steps)
    stores[1].start()
    vout_ref[...] = small.result()
    stores[2].start()
    gather.drain(0)
    scatter.drain()
    for store in stores:
        store.wait()


def step(seq_lengths, x, og, weights, vectors, b_inner, n_t):
    rows, width = x.shape
    cols = width // n_t
    heads = width // HEAD_DIM
    owidth = width - (3 * cols) // 128 * 128
    shard = weights[0].shape[0]
    bf, f32 = jnp.bfloat16, jnp.float32
    vmem, anywhere = pl.BlockSpec(memory_space=pltpu.VMEM), pl.BlockSpec(memory_space=pl.ANY)
    n_v = V_BI + 2 * n_t
    n_w = shard * lax.axis_size("dp")
    buf = lambda n: pltpu.VMEM((3, n, shard, width), bf)
    dma = pltpu.SemaphoreType.DMA
    n_loads = 3 + len(weights) + len(vectors)
    return pl.pallas_call(
        step_kernel,
        out_shape=(
            jax.ShapeDtypeStruct((rows, width), bf),
            jax.ShapeDtypeStruct((rows, width), f32),
            jax.ShapeDtypeStruct((3, shard, width), f32),
            jax.ShapeDtypeStruct((n_v, width), f32),
        ),
        in_specs=[pl.BlockSpec(memory_space=pltpu.SMEM)] + [anywhere] * n_loads,
        out_specs=[anywhere] * 3 + [vmem],
        scratch_shapes=[
            pltpu.VMEM((rows, width), bf),
            pltpu.VMEM((rows, width), bf),
            pltpu.VMEM((4, shard, cols), bf),
            pltpu.VMEM((len(vectors), width), f32),
            pltpu.VMEM((n_t, 1, width), f32),
            pltpu.VMEM((n_t, 1, width), f32),
            pltpu.VMEM((3, n_t, n_w, width), bf),
            pltpu.VMEM((n_v, 8, width), f32),
            pltpu.VMEM((n_t, rows, width), bf),
            pltpu.VMEM((heads, rows, rows), bf),
            pltpu.VMEM((n_t, rows, owidth), bf),
            pltpu.VMEM((rows, width), f32),
            pltpu.VMEM((rows, 128), f32),
            pltpu.VMEM((rows, width), bf),
            pltpu.VMEM((n_t, max(2 * rows, width), width), bf),
            pltpu.VMEM((rows, width), bf),
            pltpu.VMEM((rows, owidth), bf),
            pltpu.VMEM((width, rows), bf),
            pltpu.VMEM((width, rows), bf),
            pltpu.VMEM((width, rows), bf),
            pltpu.VMEM((rows, width), bf),
            pltpu.VMEM((rows, width), f32),
            pltpu.VMEM((3, shard, width), f32),
            buf(16),
            buf(8),
            buf(9),
            pltpu.VMEM((7, n_v, width), f32),
            pltpu.VMEM((Z_SIZE, n_v, width), f32),
            dma((n_loads,)),
            dma((3,)),
            dma((3, 36)),
            dma((3, 36)),
            dma((3, 33)),
            dma((3, 33)),
            dma((6,)),
            dma((6,)),
        ],
        compiler_params=pltpu.CompilerParams(collective_id=0, has_side_effects=True, vmem_limit_bytes=63 * 2**20),
    )(seq_lengths, x, og, *weights, *vectors, b_inner)


def place_kernel(n_t, y_in, gin_in, shards_in, sums_in, *refs):
    y, gin, gq, gk, gv, go, gi, gf, bq, bv, bo, g1, b1, bi, bf, g2, b2, y_buf, gin_buf, shards, sums, parts, heads, sems = refs
    cols = gq.shape[1]
    started = []

    def copy(src, dst):
        started.append(pltpu.make_async_copy(src, dst, sems.at[len(started)]))
        started[-1].start()
        return started[-1]

    pairs = [(sums_in, sums), (shards_in, shards), (gin_in, gin_buf), (y_in, y_buf)]
    loads = [copy(src, dst) for src, dst in pairs]
    loads[0].wait()
    for row, ref in ((V_BO, bo), (V_G1, g1), (V_B1, b1), (V_BF, bf), (V_G2, g2), (V_B2, b2)):
        copy(sums.at[row], ref)
    for t in range(n_t):
        copy(sums.at[V_BI + t], bi.at[t, 0])
        row = sums[V_BI + n_t + t : V_BI + n_t + t + 1, :]
        heads[0:1, t * cols : (t + 1) * cols] = row[:, :cols]
        heads[1:2, t * cols : (t + 1) * cols] = row[:, 2 * cols : 3 * cols]
    loads[1].wait()
    copy(shards.at[1], gi)
    copy(shards.at[2], gf)
    for i in range(4):
        parts[i] = shards[0, :, i * cols : (i + 1) * cols]
    copy(heads.at[0], bq)
    copy(heads.at[1], bv)
    loads[2].wait()
    copy(gin_buf, gin)
    for i, ref in enumerate((gq, gk, gv, go)):
        copy(parts.at[i], ref)
    loads[3].wait()
    copy(y_buf, y)
    for done in started[len(loads) :]:
        done.wait()


def place(y, gin, shards, sums, n_t):
    shard, width = shards.shape[1:]
    cols = width // n_t
    f32 = jnp.float32
    anywhere = pl.BlockSpec(memory_space=pl.ANY)
    row = jax.ShapeDtypeStruct((width,), f32)
    return pl.pallas_call(
        functools.partial(place_kernel, n_t),
        out_shape=(
            [jax.ShapeDtypeStruct(y.shape, y.dtype), jax.ShapeDtypeStruct(gin.shape, f32)]
            + [jax.ShapeDtypeStruct((shard, cols), f32)] * 4
            + [jax.ShapeDtypeStruct((shard, width), f32)] * 2
            + [row] * 5
            + [jax.ShapeDtypeStruct((n_t, 1, width), f32)]
            + [row] * 3
        ),
        in_specs=[anywhere] * 4,
        out_specs=[anywhere] * 17,
        scratch_shapes=[
            pltpu.VMEM(y.shape, y.dtype),
            pltpu.VMEM(gin.shape, f32),
            pltpu.VMEM(shards.shape, f32),
            pltpu.VMEM(sums.shape, f32),
            pltpu.VMEM((4, shard, cols), f32),
            pltpu.VMEM((8, width), f32),
            pltpu.SemaphoreType.DMA((20 + n_t,)),
        ],
    )(y, gin, shards, sums)


def data_parallel(
    hidden_in, seq_lengths, w_query, b_query, w_key, w_value, b_value, w_out, b_out, norm1_gain, norm1_bias,
    w_inner, b_inner, w_outer, b_outer, norm2_gain, norm2_bias, out_grad,
):
    n_t = lax.axis_size("tensor")
    width = hidden_in.shape[1]
    vectors = (b_outer, b_value, b_out, norm1_gain, norm1_bias, norm2_gain, norm2_bias, b_query)
    weights = (w_query, w_key, w_value, w_out, w_inner, w_outer)
    done = step(seq_lengths, hidden_in, out_grad, weights, vectors, b_inner.reshape(n_t, 1, width), n_t)
    y, gin, gq, gk, gv, go, gi, gf, *small = place(*done, n_t)
    bq, bv, bo, g1, b1, bi, bf, g2, b2 = small
    return y, gin, gq, bq, gk, gv, bv, go, bo, g1, b1, gi, bi.reshape(-1), gf, bf, g2, b2


def solution(mesh):
    in_specs = (
        P(("dp", "tensor"), None),
        P("dp"),
        P("dp", "tensor"),
        P(),
        P("dp", "tensor"),
        P("dp", "tensor"),
        P(),
        P("dp", "tensor"),
        P(),
        P(),
        P(),
        P("dp", "tensor"),
        P(),
        P("dp", "tensor"),
        P(),
        P(),
        P(),
        P(("dp", "tensor"), None),
    )
    out_specs = (
        P(("dp", "tensor"), None),
        P(("dp", "tensor"), None),
        P("dp", "tensor"),
        P(),
        P("dp", "tensor"),
        P("dp", "tensor"),
        P(),
        P("dp", "tensor"),
        P(),
        P(),
        P(),
        P("dp", "tensor"),
        P(),
        P("dp", "tensor"),
        P(),
        P(),
        P(),
    )
    small = mesh.shape["dp"] == 2 * Z_SIZE and mesh.shape["tensor"] == 4
    return jax.shard_map(
        data_parallel if small else per_device, mesh=mesh, in_specs=in_specs, out_specs=out_specs, check_vma=False
    )
```

```python
import functools

import jax
import jax.numpy as jnp
from jax import lax
from jax.experimental import pallas as pl
from jax.experimental.pallas import tpu as pltpu
from jax.sharding import PartitionSpec as P

HEAD_DIM = 64


NEG_FILL = -1000000000.0
NORM_EPS = 1e-12


def layer_norm(residual, norm_gain, norm_bias):
    centre = residual - jnp.mean(residual, axis=-1, keepdims=True)
    spread = jnp.mean(centre * centre, axis=-1, keepdims=True)
    return centre * lax.rsqrt(spread + NORM_EPS) * norm_gain + norm_bias


def exact_gelu(values):
    return jax.nn.gelu(values, approximate=False)


def contract_last(first_op, second_op):
    return lax.dot_general(
        first_op, second_op, (((1,), (1,)), ((), ())), preferred_element_type=jnp.float32
    )


def contract_first(first_op, second_op):
    return lax.dot_general(
        first_op, second_op, (((0,), (0,)), ((), ())), preferred_element_type=jnp.float32
    )


def split_blocks(heads_arr, block_rows):
    batches, length, head_size = heads_arr.shape
    return heads_arr.reshape(batches, length // block_rows, block_rows, head_size).transpose(
        1, 0, 2, 3
    )


def join_blocks(block_array):
    block_count, batches, block_rows, head_size = block_array.shape
    return block_array.transpose(1, 0, 2, 3).reshape(batches, block_count * block_rows, head_size)


def block_scores(query_portion, key_head_tensor, key_valid, score_scale):
    scores = (
        jnp.einsum(
            "eix,evx->eiv", query_portion, key_head_tensor, preferred_element_type=jnp.float32
        )
        * score_scale
    )
    return jnp.where(key_valid[:, None, :], scores, NEG_FILL)


def attend(query_heads, key_head_tensor, value_head_tensor, key_valid, block_rows, score_scale):

    def one_block(query_portion):
        scores = block_scores(query_portion, key_head_tensor, key_valid, score_scale)
        row_max = jnp.max(scores, axis=-1, keepdims=True)
        exponent = jnp.exp(scores - row_max)
        row_total = jnp.sum(exponent, axis=-1, keepdims=True)
        softmax_reduced = (exponent / row_total).astype(jnp.bfloat16)
        mixture = jnp.einsum(
            "fwj,fjt->fwt", softmax_reduced, value_head_tensor, preferred_element_type=jnp.float32
        )
        return (mixture.astype(jnp.bfloat16), row_max, row_total)

    mixture, row_max, row_total = lax.map(one_block, split_blocks(query_heads, block_rows))
    return (join_blocks(mixture), row_max, row_total)


def attend_back(
    query_heads,
    key_head_tensor,
    value_head_tensor,
    grad_heads,
    row_max,
    row_total,
    key_valid,
    block_rows,
    score_scale,
):

    def one_block(running, block_in):
        key_grad, value_grad = running
        query_portion, gradient_portion, max_part, total_part = block_in
        scores = block_scores(query_portion, key_head_tensor, key_valid, score_scale)
        softmax = jnp.exp(scores - max_part) / total_part
        softmax_reduced = softmax.astype(jnp.bfloat16)
        soft_grad = jnp.einsum(
            "eix,evx->eiv", gradient_portion, value_head_tensor, preferred_element_type=jnp.float32
        )
        centre = jnp.sum(softmax * soft_grad, axis=-1, keepdims=True)
        score_gradient = (softmax * (soft_grad - centre)).astype(jnp.bfloat16)
        query_grad = (
            jnp.einsum(
                "fwj,fjt->fwt", score_gradient, key_head_tensor, preferred_element_type=jnp.float32
            )
            * score_scale
        )
        key_grad = (
            key_grad
            + jnp.einsum(
                "oxl,oxn->oln", score_gradient, query_portion, preferred_element_type=jnp.float32
            )
            * score_scale
        )
        value_grad = value_grad + jnp.einsum(
            "oxl,oxn->oln", softmax_reduced, gradient_portion, preferred_element_type=jnp.float32
        )
        return ((key_grad, value_grad), query_grad)

    zero_grads = jnp.zeros(key_head_tensor.shape, jnp.float32)
    block_inputs = (
        split_blocks(query_heads, block_rows),
        split_blocks(grad_heads, block_rows),
        row_max,
        row_total,
    )
    (key_grad, value_grad), query_grad = lax.scan(one_block, (zero_grads, zero_grads), block_inputs)
    return (join_blocks(query_grad), key_grad, value_grad)


def per_device(
    hidden_in,
    seq_lengths,
    w_query,
    b_query,
    w_key,
    w_value,
    b_value,
    w_out,
    b_out,
    norm1_gain,
    norm1_bias,
    w_inner,
    b_inner,
    w_outer,
    b_outer,
    norm2_gain,
    norm2_bias,
    out_grad,
):
    tensor_size = lax.axis_size("tensor")
    tensor_place = lax.axis_index("tensor")
    local_rows, feature_width = hidden_in.shape
    group_rows = local_rows * tensor_size
    seq_count = seq_lengths.shape[0]
    seq_len = group_rows // seq_count
    head_cols = w_query.shape[1]
    inner_cols = w_inner.shape[1]
    heads_here = head_cols // HEAD_DIM
    block_rows = min(512, seq_len)
    score_scale = HEAD_DIM ** (-0.5)
    local_start = tensor_place * local_rows
    row_index = lax.iota(jnp.int32, group_rows)
    seq_match = (row_index[:, None] // seq_len == lax.iota(jnp.int32, seq_count)[None, :]).astype(
        jnp.int32
    )
    row_limit = jnp.sum(seq_match * seq_lengths[None, :], axis=1)
    row_valid = row_index % seq_len < row_limit
    local_mask = lax.dynamic_slice_in_dim(row_valid, local_start, local_rows).astype(jnp.float32)[
        :, None
    ]
    key_valid = jnp.repeat(row_valid.reshape(seq_count, seq_len), heads_here, axis=0)

    def heads_of(matrix):
        shaped = matrix.reshape(seq_count, seq_len, heads_here, HEAD_DIM).transpose(0, 2, 1, 3)
        return shaped.reshape(seq_count * heads_here, seq_len, HEAD_DIM)

    def rows_of(matrix):
        shaped = matrix.reshape(seq_count, heads_here, seq_len, HEAD_DIM).transpose(0, 2, 1, 3)
        return shaped.reshape(group_rows, head_cols)

    full_query, full_key, full_value, full_out, full_inner, full_outer = (
        lax.all_gather(w_query, "dp", axis=0, tiled=True),
        lax.all_gather(w_key, "dp", axis=0, tiled=True),
        lax.all_gather(w_value, "dp", axis=0, tiled=True),
        lax.all_gather(w_out, "dp", axis=0, tiled=True),
        lax.all_gather(w_inner, "dp", axis=0, tiled=True),
        lax.all_gather(w_outer, "dp", axis=0, tiled=True),
    )
    joint_weight = jnp.concatenate((full_query, full_key, full_value), axis=1)
    query_bias = lax.dynamic_slice_in_dim(b_query, tensor_place * head_cols, head_cols)
    value_bias = lax.dynamic_slice_in_dim(b_value, tensor_place * head_cols, head_cols)
    inner_bias = lax.dynamic_slice_in_dim(b_inner, tensor_place * inner_cols, inner_cols)
    joint_bias = jnp.concatenate((query_bias, jnp.zeros((head_cols,), jnp.float32), value_bias))
    whole_in = lax.all_gather(hidden_in, "tensor", axis=0, tiled=True)
    joint_rows = (
        jnp.dot(whole_in, joint_weight, preferred_element_type=jnp.float32) + joint_bias
    ).astype(jnp.bfloat16)
    query_heads = heads_of(joint_rows[:, :head_cols])
    key_head_tensor = heads_of(joint_rows[:, head_cols : 2 * head_cols])
    value_head_tensor = heads_of(joint_rows[:, 2 * head_cols :])
    mixture_heads, row_max, row_total = attend(
        query_heads, key_head_tensor, value_head_tensor, key_valid, block_rows, score_scale
    )
    mixture = rows_of(mixture_heads)
    summed_out = lax.psum_scatter(
        contract_last(mixture, full_out).astype(jnp.bfloat16),
        "tensor",
        scatter_dimension=0,
        tiled=True,
    ).astype(jnp.float32)
    first_sum = hidden_in.astype(jnp.float32) + (summed_out + b_out)
    first_norm = layer_norm(first_sum, norm1_gain, norm1_bias)
    mid_whole = lax.all_gather(first_norm.astype(jnp.bfloat16), "tensor", axis=0, tiled=True)
    pre_act = jnp.dot(mid_whole, full_inner, preferred_element_type=jnp.float32) + inner_bias
    act_low = exact_gelu(pre_act).astype(jnp.bfloat16)
    second_sum = first_norm + (
        lax.psum_scatter(
            contract_last(act_low, full_outer).astype(jnp.bfloat16),
            "tensor",
            scatter_dimension=0,
            tiled=True,
        ).astype(jnp.float32)
        + b_outer
    )
    normed, norm2_back = jax.vjp(layer_norm, second_sum, norm2_gain, norm2_bias)
    layer_out = (normed * local_mask).astype(jnp.bfloat16)
    out_cot = out_grad.astype(jnp.float32) * local_mask
    dsecond, gain2_part, bias2_part = norm2_back(out_cot)
    dffn_low = dsecond.astype(jnp.bfloat16)
    outer_bias_part = jnp.sum(dffn_low, axis=0, dtype=jnp.float32)
    dffn_whole = lax.all_gather(dffn_low, "tensor", axis=0, tiled=True)
    grad_outer = contract_first(dffn_whole, act_low)
    dact = jnp.dot(dffn_whole, full_outer, preferred_element_type=jnp.float32)
    _, gelu_back = jax.vjp(exact_gelu, pre_act)
    dpre_low = gelu_back(dact)[0].astype(jnp.bfloat16)
    inner_bias_part = jnp.sum(dpre_low, axis=0, dtype=jnp.float32)
    grad_inner = contract_first(mid_whole, dpre_low)
    dfirst_norm = dsecond + lax.psum_scatter(
        contract_last(dpre_low, full_inner).astype(jnp.bfloat16),
        "tensor",
        scatter_dimension=0,
        tiled=True,
    ).astype(jnp.float32)
    _, norm1_back = jax.vjp(layer_norm, first_sum, norm1_gain, norm1_bias)
    dfirst, gain1_part, bias1_part = norm1_back(dfirst_norm)
    dattn_low = dfirst.astype(jnp.bfloat16)
    out_bias_part = jnp.sum(dattn_low, axis=0, dtype=jnp.float32)
    dattn_whole = lax.all_gather(dattn_low, "tensor", axis=0, tiled=True)
    grad_out_w = contract_first(dattn_whole, mixture)
    dmixture = jnp.dot(dattn_whole, full_out, preferred_element_type=jnp.float32).astype(
        jnp.bfloat16
    )
    dquery_heads, dkey_heads, dvalue_heads = attend_back(
        query_heads,
        key_head_tensor,
        value_head_tensor,
        heads_of(dmixture),
        row_max,
        row_total,
        key_valid,
        block_rows,
        score_scale,
    )
    djoint = jnp.concatenate(
        (rows_of(dquery_heads), rows_of(dkey_heads), rows_of(dvalue_heads)), axis=1
    ).astype(jnp.bfloat16)
    joint_bias_part = jnp.sum(djoint, axis=0, dtype=jnp.float32)
    grad_joint = contract_first(whole_in, djoint)
    grad_in = dfirst + lax.psum_scatter(
        contract_last(djoint, joint_weight).astype(jnp.bfloat16),
        "tensor",
        scatter_dimension=0,
        tiled=True,
    ).astype(jnp.float32)
    grad_query = grad_joint[:, :head_cols]
    grad_key = grad_joint[:, head_cols : 2 * head_cols]
    grad_value = grad_joint[:, 2 * head_cols :]
    shard_grads = tuple(
        (
            lax.psum_scatter(grad_query, "dp", scatter_dimension=0, tiled=True),
            lax.psum_scatter(grad_key, "dp", scatter_dimension=0, tiled=True),
            lax.psum_scatter(grad_value, "dp", scatter_dimension=0, tiled=True),
            lax.psum_scatter(grad_out_w, "dp", scatter_dimension=0, tiled=True),
            lax.psum_scatter(grad_inner, "dp", scatter_dimension=0, tiled=True),
            lax.psum_scatter(grad_outer, "dp", scatter_dimension=0, tiled=True),
        )
    )

    def placed(vector, total_len):
        return lax.dynamic_update_slice_in_dim(
            jnp.zeros((total_len,), jnp.float32), vector, tensor_place * vector.shape[0], 0
        )

    query_bias_part = placed(joint_bias_part[:head_cols], feature_width)
    value_bias_part = placed(joint_bias_part[2 * head_cols :], feature_width)
    hidden_bias_part = placed(inner_bias_part, b_inner.shape[0])
    vector_sums = lax.psum(
        (
            query_bias_part,
            value_bias_part,
            out_bias_part,
            gain1_part,
            bias1_part,
            hidden_bias_part,
            outer_bias_part,
            gain2_part,
            bias2_part,
        ),
        ("dp", "tensor"),
    )
    return (
        layer_out,
        grad_in,
        shard_grads[0],
        vector_sums[0],
        shard_grads[1],
        shard_grads[2],
        vector_sums[1],
        shard_grads[3],
        vector_sums[2],
        vector_sums[3],
        vector_sums[4],
        shard_grads[4],
        vector_sums[5],
        shard_grads[5],
        vector_sums[6],
        vector_sums[7],
        vector_sums[8],
    )


Z_SIZE = 4
MESH_IDS = pl.DeviceIdType.MESH


def flip(place, bit):
    return place + bit - 2 * place * bit


class Place:
    def __init__(self):
        self.dp = lax.axis_index("dp")
        self.t = lax.axis_index("tensor")
        self.z = self.dp // 2
        self.x = self.dp % 2
        self.y = self.t // 2
        self.c = self.t % 2

    def chip(self, dz, da, db):
        c = self.c
        z = lax.rem(self.z - dz + Z_SIZE, Z_SIZE)
        x = flip(self.x, da * c + db * (1 - c))
        y = flip(self.y, da * (1 - c) + db * c)
        return z * 2 + x, y

    def device(self, dz=0, da=0, db=0, other=False):
        dp, y = self.chip(dz, da, db)
        core = 1 - self.c if other else self.c
        return {"dp": dp, "tensor": y * 2 + core}


def block_of(ref, m, dp, t, rows):
    return ref.at[m, t, pl.ds(pl.multiple_of(dp * rows, rows), rows), :]


def peers_of(me):
    return [me.device(dz=k) for k in range(1, Z_SIZE)] + [me.device(da=1), me.device(db=1), me.device(other=True)]


def greet(me):
    for peer in peers_of(me):
        pl.semaphore_signal(pltpu.get_barrier_semaphore(), inc=1, device_id=peer, device_id_type=MESH_IDS)


def meet(me):
    pl.semaphore_wait(pltpu.get_barrier_semaphore(), len(peers_of(me)))


def remote(src, dst, send, recv, peer):
    return pltpu.make_async_remote_copy(
        src_ref=src, dst_ref=dst, send_sem=send, recv_sem=recv, device_id=peer, device_id_type=MESH_IDS
    )


def parse(steps):
    for step in steps:
        first, _, stop = step[3:].partition("-")
        for q in range(int(first or 0), int(stop or first or 0) + 1):
            yield step[0], int(step[1]), q


class Routes:
    def __init__(self, me):
        self.me = me
        self.half = me.z // 2
        self.far = 2 - self.half
        self.near = 2 * self.half + (1 - me.z % 2)
        self.mid = (me.z == 1) | (me.z == 2)

    def z_peer(self, z):
        return {"dp": z * 2 + self.me.x, "tensor": self.me.t}

    def dz_of(self, k):
        return lax.rem(k * self.half + (4 - k) * (1 - self.half), Z_SIZE)

    def back(self, z):
        return lax.rem(self.me.z - z + Z_SIZE, Z_SIZE)


class Gather(Routes):
    def __init__(self, me, modes, w, send_sem, recv_sem):
        super().__init__(me)
        self.modes, self.w = modes, w
        self.send_sem, self.recv_sem = send_sem, recv_sem
        self.rows = w.shape[2] // lax.axis_size("dp")

    def sem(self, m, send, recv):
        one = block_of(self.w, m, 0, 0, self.rows)
        return remote(one, one, self.send_sem.at[m, send], self.recv_sem.at[m, recv], self.me.device(db=1))

    def wait(self, m, slot):
        self.sem(m, slot, slot).wait_recv()

    def send(self, m, slot, dz, da, db, peer, leave=None):
        dp, y = self.me.chip(dz, da, db)
        dst = block_of(self.w, m, dp, y * 2 + self.me.c, self.rows)
        leave = slot if leave is None else leave
        remote(dst, dst, self.send_sem.at[m, leave], self.recv_sem.at[m, slot], peer).start()

    def z_slots(self, da):
        return [(4 * lax.rem(z - self.me.z + Z_SIZE, Z_SIZE) + 2 * da, z) for z in (self.far, self.near)]

    def z_send(self, m, da):
        for slot, z in self.z_slots(da):
            self.send(m, slot, 0, da, 0, self.z_peer(z))

    def own(self, m):
        return block_of(self.w, m, self.me.dp, self.me.t, self.rows)

    def place(self, m, q):
        if self.modes[m] == 0:
            return q % 4, q // 4
        return (0, q) if q < 2 else (1 + (q - 2) % 3, (q - 2) // 3)

    def pump(self, m, q):
        me = self.me
        k, da = self.place(m, q)
        dz = self.dz_of(k) if k else 0
        slot = 4 * dz + 2 * da
        self.wait(m, slot)
        if k in (1, 2) and (self.modes[m] == 1 or da == 0):

            @pl.when(self.mid)
            def _():
                there = lax.rem(self.near - me.z + dz + Z_SIZE, Z_SIZE)
                self.send(m, 4 * there + 2 * da, dz, da, 0, self.z_peer(self.near), leave=31 + 2 * da + k)

        if self.modes[m] == 0 and da == 0:
            self.send(m, 4 * dz + 2, dz, 0, 0, me.device(da=1))
        if self.modes[m] == 1 and k == 0:
            self.z_send(m, 1)
        self.send(m, slot + 1, dz, da, 0, me.device(db=1))
        self.send(m, 16 + slot, dz, da, 0, me.device(other=True))

    def last(self, m, q):
        k, da = self.place(m, q)
        dz = self.dz_of(k) if k else 0
        slot = 4 * dz + 2 * da + 1
        self.wait(m, slot)
        self.send(m, 16 + slot, dz, da, 1, self.me.device(other=True))

    def run(self, steps):
        me = self.me
        for op, m, q in parse(steps):
            if op == "A":
                self.send(m, 2, 0, 0, 0, me.device(da=1))
            elif op == "B":
                self.send(m, 1, 0, 0, 0, me.device(db=1))
                self.send(m, 16, 0, 0, 0, me.device(other=True))
            elif op == "y":
                self.z_send(m, 0)
            elif op == "p":
                self.pump(m, q)
            else:
                self.last(m, q)

    def collect(self, m, first=0, stop=4):
        @pl.loop(0, Z_SIZE)
        def _(dz):
            for s in range(first, stop):
                self.wait(m, 16 + 4 * dz + s)

    def drain(self, m):
        left = lambda s: self.sem(m, s, s).wait_send()
        for da in range(1 + self.modes[m]):
            for slot, _ in self.z_slots(da):
                left(slot)

            @pl.when(self.mid)
            def _():
                left(32 + 2 * da)
                left(33 + 2 * da)

        for dz in range(1 if self.modes[m] else Z_SIZE):
            left(4 * dz + 2)

        @pl.loop(0, 8)
        def _(s):
            left(2 * s + 1)

        @pl.loop(16, 32)
        def _(s):
            left(s)


class Scatter(Routes):
    def __init__(self, me, modes, w, w0_grad, out_ref, core_buf, b_buf, t_buf, send_sem, recv_sem):
        super().__init__(me)
        self.out_ref = out_ref
        self.modes, self.w, self.w0_grad = modes, w, w0_grad
        self.core_buf, self.b_buf, self.t_buf = core_buf, b_buf, t_buf
        self.send_sem, self.recv_sem = send_sem, recv_sem
        self.rows = b_buf.shape[2]

    def order(self, i):
        me = self.me
        return flip(me.y, 1 - i // 2) * 2 + flip(1 - me.c, i % 2)

    def part(self, m, dz, da, db, core):
        dp, y = self.me.chip(dz, da, db)
        if m == 0:
            return self.w0_grad.at[y * 2 + core, pl.ds(pl.multiple_of(dp * self.rows, self.rows), self.rows), :]
        return block_of(self.w, m, dp, y * 2 + core, self.rows)

    def sem(self, m, send, recv):
        one = self.b_buf.at[m, 0]
        return remote(one, one, self.send_sem.at[m, send], self.recv_sem.at[m, recv], self.me.device(db=1))

    def wait(self, m, slot):
        self.sem(m, slot, slot).wait_recv()

    def go(self, m, slot, src, dst, peer, leave=None):
        leave = slot if leave is None else leave
        remote(src, dst, self.send_sem.at[m, leave], self.recv_sem.at[m, slot], peer).start()

    def from_core(self, dz, da, db):
        return 4 * dz + 2 * db + da

    def ready(self, m, i):
        me = self.me
        c = me.c
        side = 1 - i // 2

        def where(s):
            other = 1 - s // 4
            return self.dz_of(3 - s % 4), side * (1 - c) + other * c, other * (1 - c) + side * c

        @pl.when(i % 2 == 0)
        def _():
            @pl.loop(0, 8)
            def _(s):
                dz, da, db = where(s)
                slot = 4 * dz + 2 * da + db
                self.go(m, slot, self.part(m, dz, da, db, 1 - c), self.core_buf.at[m, slot], me.device(other=True))

        @pl.when(i % 2 == 1)
        def _():
            @pl.loop(0, 8)
            def _(s):
                dz, da, db = where(s)
                slot = self.from_core(dz, da, db)
                self.wait(m, slot)
                self.core_buf[m, slot] = self.part(m, dz, da, db, c)[...] + self.core_buf[m, slot]

                @pl.when(db == 1)
                def _():
                    place = 2 * dz + da
                    self.go(m, 16 + place, self.core_buf.at[m, slot], self.b_buf.at[m, place], me.device(db=1))

    def way(self, m, da, j):
        return 2 * da + j if self.modes[m] else 4 + j

    def end(self, m, da, far):
        return (4 + 2 * da if self.modes[m] else 6) + far

    def z_out(self, m, dz, da, src):
        owner = lax.rem(self.me.z - dz + Z_SIZE, Z_SIZE)
        is_near = owner == self.near

        @pl.when(is_near)
        def _():
            j = self.end(m, da, 0)
            self.go(m, 24 + j, src, self.t_buf.at[m, j], self.z_peer(self.near))

        @pl.when(jnp.logical_not(is_near | self.mid) & (dz != 0))
        def _():
            j = self.way(m, da, 0) + (owner != self.far).astype(jnp.int32)
            self.go(m, 24 + j, src, self.t_buf.at[m, j], self.z_peer(self.near))

    def source(self, m, dz, da):
        return self.b_buf.at[m, 2 * dz + da] if self.modes[m] else self.t_buf.at[m, dz]

    def b_step(self, m, k, da):
        dz = self.dz_of(k)
        place = 2 * dz + da
        self.wait(m, 16 + place)
        self.b_buf[m, place] = self.b_buf[m, place] + self.core_buf[m, self.from_core(dz, da, 0)]
        if self.modes[m] == 1:
            self.z_out(m, dz, da, self.b_buf.at[m, place])
        elif da == 1:
            self.go(m, 24 + dz, self.b_buf.at[m, place], self.t_buf.at[m, dz], self.me.device(da=1))

    def a_step(self, m, k):
        dz = self.dz_of(k)
        self.wait(m, 24 + dz)
        self.t_buf[m, dz] = self.t_buf[m, dz] + self.b_buf[m, 2 * dz]
        self.z_out(m, dz, 0, self.t_buf.at[m, dz])

    def z_step(self, m, da, j):
        @pl.when(self.mid)
        def _():
            owner = flip(self.far % 2, j) + 2 * (1 - self.half)
            way, end = self.way(m, da, j), self.end(m, da, 1)
            self.wait(m, 24 + way)
            self.t_buf[m, way] = self.t_buf[m, way] + self.source(m, self.back(owner), da)[...]
            self.go(m, 24 + end, self.t_buf.at[m, way], self.t_buf.at[m, end], self.z_peer(owner), leave=24 + way)

    def last_step(self, m):
        near, far = self.end(m, 1, 0), self.end(m, 1, 1)
        self.wait(m, 24 + near)
        self.wait(m, 24 + far)
        self.t_buf[m, near] = self.t_buf[m, near] + self.t_buf[m, far] + self.b_buf[m, 1]
        self.go(m, 32, self.t_buf.at[m, near], self.t_buf.at[m, 8], self.me.device(da=1))

    def run(self, steps):
        for op, m, q in parse(steps):
            if op == "b":
                self.b_step(m, 3 - q // 2, 1 - q % 2)
            elif op == "c":
                self.b_step(m, 3 - q % 4, 1 - q // 4)
            elif op == "a":
                self.a_step(m, 3 - q)
            elif op == "z":
                self.z_step(m, (1 - q // 2) * self.modes[m], 1 - q % 2)
            elif op == "e":
                self.last_step(m)
            else:
                self.finish(m)

    def finish(self, m):
        wide = lambda ref: ref[...].astype(jnp.float32)
        near = self.end(m, 0, 0)
        self.wait(m, 24 + near)
        self.wait(m, 25 + near)
        total = wide(self.source(m, 0, 0)) + wide(self.t_buf.at[m, near]) + wide(self.t_buf.at[m, near + 1])
        if self.modes[m] == 1:
            self.wait(m, 32)
            total = total + wide(self.t_buf.at[m, 8])
        self.out_ref[m] = total

    def drain(self):
        for m in range(3):
            left = lambda s: self.sem(m, s, s).wait_send()

            @pl.loop(0, 24)
            def _(s):
                left(s)

            for da in range(1 + self.modes[m]):
                for j in (self.way(m, da, 0), self.way(m, da, 1), self.end(m, da, 0)):
                    left(24 + j)
            for j in (8,) if self.modes[m] else range(Z_SIZE):
                left(24 + j)


class VectorSum:
    def __init__(self, me, buf, zbuf, send_sem, recv_sem):
        self.me, self.buf, self.zbuf, self.send_sem, self.recv_sem = me, buf, zbuf, send_sem, recv_sem

    def copy(self, step, src, dst, peer):
        return remote(src, dst, self.send_sem.at[step], self.recv_sem.at[step], peer)

    def peer(self, step):
        me = self.me
        if step == 0:
            return me.device(other=True)
        dx, dy = ((1, 0), (0, 1))[step - 1]
        return {"dp": me.z * 2 + flip(me.x, dx), "tensor": 2 * flip(me.y, dy) + me.c}

    def pair(self, step):
        return self.copy(step, self.buf.at[2 * step], self.buf.at[2 * step + 1], self.peer(step))

    def start(self, value):
        self.buf[0] = value
        self.pair(0).start()

    def advance(self, step):
        self.pair(step).wait()
        self.buf[2 * step + 2] = self.buf[2 * step] + self.buf[2 * step + 1]
        if step < 2:
            self.pair(step + 1).start()
        else:
            self.zbuf[self.me.z] = self.buf[6]
            for k in range(1, Z_SIZE):
                self.z_copy(k).start()

    def z_copy(self, k):
        return self.copy(2 + k, self.buf.at[6], self.zbuf.at[self.me.z], self.me.device(dz=k))

    def result(self):
        for k in range(1, Z_SIZE):
            self.z_copy(k).wait()
        return (self.zbuf[0] + self.zbuf[1]) + (self.zbuf[2] + self.zbuf[3])


def dot_nn(a, b):
    return lax.dot_general(a, b, (((1,), (0,)), ((), ())), preferred_element_type=jnp.float32)


def dot_nt(a, b):
    return lax.dot_general(a, b, (((1,), (1,)), ((), ())), preferred_element_type=jnp.float32)


def dot_tn(a, b):
    return lax.dot_general(a, b, (((0,), (0,)), ((), ())), preferred_element_type=jnp.float32)


def low(a):
    return a.astype(jnp.bfloat16)


def row_mean(a):
    return jnp.mean(a, axis=-1, keepdims=True)


def normalise(r):
    centre = r - row_mean(r)
    inverse = lax.rsqrt(row_mean(centre * centre) + NORM_EPS)
    return centre * inverse, inverse


def norm_back(g, z, inverse):
    return (g - row_mean(g) - z * row_mean(g * z)) * inverse


def gelu_pair(u):
    cdf = 0.5 + 0.5 * lax.erf(u * (0.5**0.5))
    density = jnp.exp(-0.5 * u * u) * ((0.5 / jnp.pi) ** 0.5)
    return u * cdf, cdf + u * density


V_BQ, V_BV, V_BO, V_G1, V_B1, V_BF, V_G2, V_B2, V_BI = range(9)
TILE = 64


class Layer:
    def __init__(self, **refs):
        self.__dict__.update(refs)
        self.rows, self.width = self.x.shape
        self.n_t = self.w.shape[1]
        self.cols = self.width // self.n_t
        self.heads = self.cols // HEAD_DIM
        self.ocol = (3 * self.cols) // 128 * 128

    def tiles(self, body):
        @pl.loop(0, self.rows // TILE)
        def _(i):
            body(pl.ds(pl.multiple_of(i * TILE, TILE), TILE))

    def project(self, t):
        lane = lax.broadcasted_iota(jnp.int32, (1, self.width), 1)
        out = dot_nn(self.x[...], self.w[0, t]) + self.qkv_bias[t]
        self.qkv[t] = low(jnp.where(lane < 3 * self.cols, out, 0.0))

    def piece(self, t, which, j):
        first = which * self.cols + j * HEAD_DIM
        return self.qkv.at[t, :, first : first + HEAD_DIM]

    def attend(self, t, valid, between):
        self.att[t, :, : HEAD_DIM] = jnp.zeros((self.rows, HEAD_DIM), jnp.bfloat16)
        for j in range(self.heads):
            q, k, v = (self.piece(t, i, j)[...] for i in range(3))
            s = dot_nt(k, q * jnp.bfloat16(HEAD_DIM**-0.5))
            s = jnp.where(valid, s, NEG_FILL)
            e = jnp.exp(s - jnp.max(s, axis=0, keepdims=True))
            p = low(e * (1.0 / jnp.sum(e, axis=0, keepdims=True)))
            self.p[t * self.heads + j] = p
            mix = dot_tn(v, p)
            first = 3 * self.cols - self.ocol + j * HEAD_DIM
            self.att[t, :, first : first + HEAD_DIM] = low(mix.T)
            between(j)

    def out_project(self, t):
        self.acc[...] += dot_nt(self.att[t], self.w[0, t, :, self.ocol :])

    def start_residual(self):
        self.acc[...] = self.x[...].astype(jnp.float32) + self.vec[2:3, :]

    def first_norm(self):
        def body(r):
            z, inverse = normalise(self.acc[r, :])
            self.z1[r, :] = z
            self.inv1[r, :] = jnp.broadcast_to(inverse, (TILE, 128))
            h1 = z * self.vec[3:4, :] + self.vec[4:5, :]
            self.h1b[r, :] = low(h1)
            self.acc[r, :] = h1 + self.vec[0:1, :]

        self.tiles(body)

    def inner(self, t):
        @pl.loop(0, self.rows // 128)
        def _(i):
            r = pl.ds(pl.multiple_of(i * 128, 128), 128)
            pre = dot_nn(self.h1b[r, :], self.w[1, t]) + self.inner_bias[t]
            act, slope = gelu_pair(pre)
            self.act[t, r, :] = low(act)
            self.slope[t, r, :] = low(slope)

    def outer(self, t):
        self.acc[...] += dot_nt(self.act[t], self.w[2, t])

    def second_norm(self, length):
        self.sums[...] = jnp.zeros_like(self.sums)

        def body(r):
            z, inverse = normalise(self.acc[r, :])
            place = r.start + lax.broadcasted_iota(jnp.int32, (TILE, 1), 0)
            mask = (place < length).astype(jnp.float32)
            gain = self.vec[5:6, :]
            self.y[r, :] = low((z * gain + self.vec[6:7, :]) * mask)
            dy = self.og[r, :].astype(jnp.float32) * mask
            dr2 = norm_back(dy * gain, z, inverse)
            self.acc[r, :] = dr2
            df = low(dr2)
            self.df[r, :] = df
            self.sums[V_G2] += fold(dy * z)
            self.sums[V_B2] += fold(dy)
            self.sums[V_BF] += fold(df.astype(jnp.float32))

        self.tiles(body)

    def outer_back(self, t):
        half = self.rows // 2
        for i in range(2):
            r = slice(i * half, (i + 1) * half)
            d = dot_nn(self.df[r, :], self.w[2, t])
            self.slope[t, r, :] = low(d * self.slope[t, r, :].astype(jnp.float32))
        self.w[2, t] = low(dot_nn(self.df_t[...], self.act[t]))
        self.sums[V_BI + t] = self.column_sums(self.slope[t])

    def column_sums(self, a):
        first = lax.broadcasted_iota(jnp.int32, (16, self.rows), 0) == 0
        return dot_nn(low(first.astype(jnp.float32)), a)[:8]

    def inner_back(self, t):
        self.acc[...] += dot_nt(self.slope[t], self.w[1, t])
        self.w[1, t] = low(dot_nn(self.h1b_t[...], self.slope[t]))

    def first_norm_back(self):
        def body(r):
            z = self.z1[r, :]
            dh1 = self.acc[r, :]
            self.sums[V_G1] += fold(dh1 * z)
            self.sums[V_B1] += fold(dh1)
            dr1 = norm_back(dh1 * self.vec[3:4, :], z, self.inv1[r, :1])
            self.acc[r, :] = dr1
            dob = low(dr1)
            self.df[r, :] = dob
            self.sums[V_BO] += fold(dob.astype(jnp.float32))

        self.tiles(body)

    def attend_back(self, t, between):
        scale = HEAD_DIM**-0.5
        self.datt[...] = low(dot_nn(self.df[...], self.w[0, t, :, self.ocol :]))
        for j in range(self.heads):
            first = 3 * self.cols - self.ocol + j * HEAD_DIM
            d = self.datt[:, first : first + HEAD_DIM]
            q, k, v = (self.piece(t, i, j)[...] for i in range(3))
            p = self.p[t * self.heads + j]
            dp = dot_nt(v, d)
            pf = p.astype(jnp.float32)
            delta = jnp.sum(pf * dp, axis=0, keepdims=True)
            ds = low(pf * (dp - delta))
            self.piece(t, 2, j)[...] = low(dot_nn(p, d))
            self.piece(t, 1, j)[...] = low(dot_nn(ds, q) * scale)
            self.piece(t, 0, j)[...] = low((dot_tn(k, ds) * scale).T)
            between(j)

    def head_sums(self, t):
        self.sums[V_BI + self.n_t + t] = self.column_sums(self.qkv[t])

    def project_grad(self, t):
        self.w0_grad[t] = low(dot_nn(self.x_t[...], self.qkv[t]))
        out = self.w0_grad.at[t, :, self.ocol :]
        out[...] = low(out[...].astype(jnp.float32) + dot_nn(self.df_t[...], self.att[t]))

    def project_back(self, t):
        self.acc[...] += dot_nt(self.qkv[t], self.w[0, t])

    def transpose(self, src, dst):
        dst[...] = src[...].T


def fold(a):
    return jnp.sum(a.reshape(a.shape[0] // 8, 8, a.shape[1]), axis=0)


GATHER_MODES = (0, 1, 1)
SCATTER_MODES = (0, 1, 1)
GATHER_MODES = (0, 1, 1)
SCATTER_MODES = (0, 1, 1)
GATHER = {
    "first": ("y0:0", "A0:0", "A1:0", "p0:4", "B1:0", "y2:0", "B0:0", "l0:4", "p0:1"),
    "start": ("p0:2", "p1:1", "y1:0", "l0:0", "p0:3", "p0:6", "p0:5", "l0:2", "l0:1", "l1:1", "p0:7", "p2:2", "p1:2", "p1:5",
        "l0:5", "B2:0", "l0:6", "A2:0", "l0:3", "l0:7"),
    "attend": (),
    "heads": {4: ("l2:0", "p2:3", "p2:1"), 8: ("p1:4", "p1:7", "l1:0", "l1:5"), 10: ("l2:3",), 11: ("l1:4", "l2:2", "l1:6",
        "p2:4", "l1:3", "l1:2")},
    "out": {0: ("p1:6", "p1:3"), 3: ("p2:5", "l1:7")},
    "norm": (),
    "ffn": ("p2:6",),
    "inner": {1: ("p2:7", "l2:6", "l2:1", "l2:5", "l2:4"), 3: ("l2:7",)},
    "outer": {},
    "late": (),
}
SCATTER = {
    "outer": {3: ("b2:0",)},
    "inner": {0: ("b2:2",), 1: ("z2:0",), 2: ("b2:3", "b2:1", "b2:5")},
    "norm": ("b2:4", "b1:2", "b2:7"),
    "heads": {2: ("z2:1",), 4: ("z2:2-3",), 7: ("z1:1", "b1:6"), 8: ("b1:1", "z1:0")},
    "grad": {0: ("b1:0", "b1:4"), 1: ("b1:3",), 3: ("b1:5", "z1:2", "b0:0")},
    "last": (("z1:3", "b0:2"), ("b0:4", "b0:1"), ("a0:0", "b1:7", "b2:6", "e2:0", "e1:0", "b0:3", "b0:6", "a0:1", "b0:5",
        "z0:0", "b0:7"), ("a0:2", "z0:1", "F1:0", "F2:0", "a0:3", "F0:0")),
}


def step_kernel(
    length_ref, x_in, og_in, wq, wk, wv, wo, w_inner, w_outer, b_outer, b_value, b_out, gain1, bias1, gain2, bias2, b_query, b_inner,
    y_out, acc_out, shards_out, vout_ref,
    x_ref, og_ref, parts, vec_ref, qkv_bias, inner_bias,
    w, sums, qkv, p, att, z1, inv1, h1b, ffn, df, datt, x_t, h1b_t, df_t, y_ref, acc_ref, out_ref,
    core_buf, b_buf, t_buf, vec_buf, vec_z,
    load_sem, store_sem, gather_send, gather_recv, send_sem, recv_sem, vec_send, vec_recv,
):
    me = Place()
    rows, width = x_ref.shape
    act, slope, w0_grad = ffn.at[:, :rows], ffn.at[:, rows:], ffn.at[:, :width]
    gather = Gather(me, GATHER_MODES, w, gather_send, gather_recv)
    scatter = Scatter(me, SCATTER_MODES, w, w0_grad, out_ref, core_buf, b_buf, t_buf, send_sem, recv_sem)
    small = VectorSum(me, vec_buf, vec_z, vec_send, vec_recv)
    a = Layer(
        x=x_ref, og=og_ref, w=w, w0_grad=w0_grad, qkv_bias=qkv_bias, inner_bias=inner_bias, vec=vec_ref, y=y_ref, acc=acc_ref, sums=sums,
        qkv=qkv, p=p, att=att, z1=z1, inv1=inv1, h1b=h1b, act=act, slope=slope, df=df, datt=datt, x_t=x_t, h1b_t=h1b_t, df_t=df_t,
    )
    vectors = (b_outer, b_value, b_out, gain1, bias1, gain2, bias2, b_query)
    pairs = [(ref, parts.at[i]) for i, ref in enumerate((wq, wk, wv, wo))]
    pairs += [(w_inner, gather.own(1)), (w_outer, gather.own(2)), (x_in, x_ref), (b_inner, inner_bias)]
    pairs += [(ref, vec_ref.at[i]) for i, ref in enumerate(vectors)] + [(og_in, og_ref)]
    loads = [pltpu.make_async_copy(src, dst, load_sem.at[i]) for i, (src, dst) in enumerate(pairs)]
    for load in loads:
        load.start()

    def at(run, slots, i):
        for n, steps in slots.items():

            @pl.when(i == n)
            def _():
                run(steps)

    def heads(run, slots, i, j):
        at(run, {n // a.heads: steps for n, steps in slots.items() if n % a.heads == j}, i)

    greet(me)
    for load in loads[:6]:
        load.wait()
    packed = gather.own(0)
    for i in range(4):
        packed[:, i * a.cols : (i + 1) * a.cols] = parts[i]
    meet(me)
    gather.run(GATHER["first"])
    for load in loads[6:]:
        load.wait()
    for t in range(a.n_t):
        here = slice(t * a.cols, (t + 1) * a.cols)
        qkv_bias[t] = jnp.zeros((1, width), jnp.float32)
        qkv_bias[t, :, : a.cols] = vec_ref[7:8, here]
        qkv_bias[t, :, 2 * a.cols : 3 * a.cols] = vec_ref[1:2, here]
    length = length_ref[me.t]
    valid = lax.broadcasted_iota(jnp.int32, (a.rows, 1), 0) < length
    a.transpose(a.x, a.x_t)
    a.start_residual()
    gather.run(GATHER["start"])
    gather.collect(0)
    gather.run(GATHER["attend"])

    @pl.loop(0, a.n_t)
    def _(t):
        a.project(t)
        a.attend(t, valid, lambda j: heads(gather.run, GATHER["heads"], t, j))
        a.out_project(t)
        at(gather.run, GATHER["out"], t)

    a.first_norm()
    a.transpose(a.h1b, a.h1b_t)
    gather.run(GATHER["norm"])
    gather.collect(1)
    gather.run(GATHER["ffn"])

    @pl.loop(0, a.n_t)
    def _(t):
        a.inner(t)
        at(gather.run, GATHER["inner"], t)

    gather.collect(2, 0, 3)
    gather.run(GATHER["late"])

    @pl.loop(0, 2)
    def _(core):
        a.outer(2 * me.y + core)
        at(gather.run, GATHER["outer"], core)

    gather.collect(2, 3, 4)

    @pl.loop(0, 2)
    def _(core):
        a.outer(2 * (1 - me.y) + core)

    a.second_norm(length)
    a.transpose(a.df, a.df_t)
    stores = [(y_ref, y_out), (acc_ref, acc_out), (out_ref, shards_out)]
    stores = [pltpu.make_async_copy(src, dst, store_sem.at[i]) for i, (src, dst) in enumerate(stores)]
    stores[0].start()
    gather.drain(2)

    @pl.loop(0, a.n_t)
    def _(i):
        a.outer_back(scatter.order(i))
        scatter.ready(2, i)
        at(scatter.run, SCATTER["outer"], i)

    gather.drain(1)

    @pl.loop(0, a.n_t)
    def _(i):
        a.inner_back(scatter.order(i))
        scatter.ready(1, i)
        at(scatter.run, SCATTER["inner"], i)

    a.first_norm_back()
    a.transpose(a.df, a.df_t)
    scatter.run(SCATTER["norm"])

    @pl.loop(0, a.n_t)
    def _(i):
        t = scatter.order(i)
        a.attend_back(t, lambda j: heads(scatter.run, SCATTER["heads"], i, j))
        a.head_sums(t)

        @pl.when(i == a.n_t - 1)
        def _():
            small.start(jnp.sum(sums[...], axis=1))

        a.project_grad(t)

        @pl.when(i == a.n_t - 1)
        def _():
            small.advance(0)

        scatter.ready(0, i)
        at(scatter.run, SCATTER["grad"], i)

    for t, steps in enumerate(SCATTER["last"]):
        a.project_back(t)
        if t == 1:
            small.advance(1)
        if t == 2:
            scatter.run(steps[:3])
            small.advance(2)
            steps = steps[3:]
        scatter.run(steps)
    stores[1].start()
    vout_ref[...] = small.result()
    stores[2].start()
    gather.drain(0)
    scatter.drain()
    for store in stores:
        store.wait()


def step(seq_lengths, x, og, weights, vectors, b_inner, n_t):
    rows, width = x.shape
    cols = width // n_t
    heads = width // HEAD_DIM
    owidth = width - (3 * cols) // 128 * 128
    shard = weights[0].shape[0]
    bf, f32 = jnp.bfloat16, jnp.float32
    vmem, anywhere = pl.BlockSpec(memory_space=pltpu.VMEM), pl.BlockSpec(memory_space=pl.ANY)
    n_v = V_BI + 2 * n_t
    n_w = shard * lax.axis_size("dp")
    buf = lambda n: pltpu.VMEM((3, n, shard, width), bf)
    dma = pltpu.SemaphoreType.DMA
    n_loads = 3 + len(weights) + len(vectors)
    return pl.pallas_call(
        step_kernel,
        out_shape=(
            jax.ShapeDtypeStruct((rows, width), bf),
            jax.ShapeDtypeStruct((rows, width), f32),
            jax.ShapeDtypeStruct((3, shard, width), f32),
            jax.ShapeDtypeStruct((n_v, width), f32),
        ),
        in_specs=[pl.BlockSpec(memory_space=pltpu.SMEM)] + [anywhere] * n_loads,
        out_specs=[anywhere] * 3 + [vmem],
        scratch_shapes=[
            pltpu.VMEM((rows, width), bf),
            pltpu.VMEM((rows, width), bf),
            pltpu.VMEM((4, shard, cols), bf),
            pltpu.VMEM((len(vectors), width), f32),
            pltpu.VMEM((n_t, 1, width), f32),
            pltpu.VMEM((n_t, 1, width), f32),
            pltpu.VMEM((3, n_t, n_w, width), bf),
            pltpu.VMEM((n_v, 8, width), f32),
            pltpu.VMEM((n_t, rows, width), bf),
            pltpu.VMEM((heads, rows, rows), bf),
            pltpu.VMEM((n_t, rows, owidth), bf),
            pltpu.VMEM((rows, width), f32),
            pltpu.VMEM((rows, 128), f32),
            pltpu.VMEM((rows, width), bf),
            pltpu.VMEM((n_t, max(2 * rows, width), width), bf),
            pltpu.VMEM((rows, width), bf),
            pltpu.VMEM((rows, owidth), bf),
            pltpu.VMEM((width, rows), bf),
            pltpu.VMEM((width, rows), bf),
            pltpu.VMEM((width, rows), bf),
            pltpu.VMEM((rows, width), bf),
            pltpu.VMEM((rows, width), f32),
            pltpu.VMEM((3, shard, width), f32),
            buf(16),
            buf(8),
            buf(9),
            pltpu.VMEM((7, n_v, width), f32),
            pltpu.VMEM((Z_SIZE, n_v, width), f32),
            dma((n_loads,)),
            dma((3,)),
            dma((3, 36)),
            dma((3, 36)),
            dma((3, 33)),
            dma((3, 33)),
            dma((6,)),
            dma((6,)),
        ],
        compiler_params=pltpu.CompilerParams(collective_id=0, has_side_effects=True, vmem_limit_bytes=63 * 2**20),
    )(seq_lengths, x, og, *weights, *vectors, b_inner)


def place_kernel(n_t, y_in, gin_in, shards_in, sums_in, *refs):
    y, gin, gq, gk, gv, go, gi, gf, bq, bv, bo, g1, b1, bi, bf, g2, b2, y_buf, gin_buf, shards, sums, parts, heads, sems = refs
    cols = gq.shape[1]
    started = []

    def copy(src, dst):
        started.append(pltpu.make_async_copy(src, dst, sems.at[len(started)]))
        started[-1].start()
        return started[-1]

    pairs = [(sums_in, sums), (shards_in, shards), (gin_in, gin_buf), (y_in, y_buf)]
    loads = [copy(src, dst) for src, dst in pairs]
    loads[0].wait()
    for row, ref in ((V_BO, bo), (V_G1, g1), (V_B1, b1), (V_BF, bf), (V_G2, g2), (V_B2, b2)):
        copy(sums.at[row], ref)
    for t in range(n_t):
        copy(sums.at[V_BI + t], bi.at[t, 0])
        row = sums[V_BI + n_t + t : V_BI + n_t + t + 1, :]
        heads[0:1, t * cols : (t + 1) * cols] = row[:, :cols]
        heads[1:2, t * cols : (t + 1) * cols] = row[:, 2 * cols : 3 * cols]
    loads[1].wait()
    copy(shards.at[1], gi)
    copy(shards.at[2], gf)
    for i in range(4):
        parts[i] = shards[0, :, i * cols : (i + 1) * cols]
    copy(heads.at[0], bq)
    copy(heads.at[1], bv)
    loads[2].wait()
    copy(gin_buf, gin)
    for i, ref in enumerate((gq, gk, gv, go)):
        copy(parts.at[i], ref)
    loads[3].wait()
    copy(y_buf, y)
    for done in started[len(loads) :]:
        done.wait()


def place(y, gin, shards, sums, n_t):
    shard, width = shards.shape[1:]
    cols = width // n_t
    f32 = jnp.float32
    anywhere = pl.BlockSpec(memory_space=pl.ANY)
    row = jax.ShapeDtypeStruct((width,), f32)
    return pl.pallas_call(
        functools.partial(place_kernel, n_t),
        out_shape=(
            [jax.ShapeDtypeStruct(y.shape, y.dtype), jax.ShapeDtypeStruct(gin.shape, f32)]
            + [jax.ShapeDtypeStruct((shard, cols), f32)] * 4
            + [jax.ShapeDtypeStruct((shard, width), f32)] * 2
            + [row] * 5
            + [jax.ShapeDtypeStruct((n_t, 1, width), f32)]
            + [row] * 3
        ),
        in_specs=[anywhere] * 4,
        out_specs=[anywhere] * 17,
        scratch_shapes=[
            pltpu.VMEM(y.shape, y.dtype),
            pltpu.VMEM(gin.shape, f32),
            pltpu.VMEM(shards.shape, f32),
            pltpu.VMEM(sums.shape, f32),
            pltpu.VMEM((4, shard, cols), f32),
            pltpu.VMEM((8, width), f32),
            pltpu.SemaphoreType.DMA((20 + n_t,)),
        ],
    )(y, gin, shards, sums)


def data_parallel(
    hidden_in, seq_lengths, w_query, b_query, w_key, w_value, b_value, w_out, b_out, norm1_gain, norm1_bias,
    w_inner, b_inner, w_outer, b_outer, norm2_gain, norm2_bias, out_grad,
):
    n_t = lax.axis_size("tensor")
    width = hidden_in.shape[1]
    vectors = (b_outer, b_value, b_out, norm1_gain, norm1_bias, norm2_gain, norm2_bias, b_query)
    weights = (w_query, w_key, w_value, w_out, w_inner, w_outer)
    done = step(seq_lengths, hidden_in, out_grad, weights, vectors, b_inner.reshape(n_t, 1, width), n_t)
    y, gin, gq, gk, gv, go, gi, gf, *small = place(*done, n_t)
    bq, bv, bo, g1, b1, bi, bf, g2, b2 = small
    return y, gin, gq, bq, gk, gv, bv, go, bo, g1, b1, gi, bi.reshape(-1), gf, bf, g2, b2


def solution(mesh):
    in_specs = (
        P(("dp", "tensor"), None),
        P("dp"),
        P("dp", "tensor"),
        P(),
        P("dp", "tensor"),
        P("dp", "tensor"),
        P(),
        P("dp", "tensor"),
        P(),
        P(),
        P(),
        P("dp", "tensor"),
        P(),
        P("dp", "tensor"),
        P(),
        P(),
        P(),
        P(("dp", "tensor"), None),
    )
    out_specs = (
        P(("dp", "tensor"), None),
        P(("dp", "tensor"), None),
        P("dp", "tensor"),
        P(),
        P("dp", "tensor"),
        P("dp", "tensor"),
        P(),
        P("dp", "tensor"),
        P(),
        P(),
        P(),
        P("dp", "tensor"),
        P(),
        P("dp", "tensor"),
        P(),
        P(),
        P(),
    )
    small = mesh.shape["dp"] == 2 * Z_SIZE and mesh.shape["tensor"] == 4
    return jax.shard_map(
        data_parallel if small else per_device, mesh=mesh, in_specs=in_specs, out_specs=out_specs, check_vma=False
    )
```

```python
import functools

import jax
import jax.numpy as jnp
from jax import lax
from jax.experimental import pallas as pl
from jax.experimental.pallas import tpu as pltpu
from jax.sharding import PartitionSpec as P

HEAD_DIM = 64


NEG_FILL = -1000000000.0
NORM_EPS = 1e-12


def layer_norm(residual, norm_gain, norm_bias):
    centre = residual - jnp.mean(residual, axis=-1, keepdims=True)
    spread = jnp.mean(centre * centre, axis=-1, keepdims=True)
    return centre * lax.rsqrt(spread + NORM_EPS) * norm_gain + norm_bias


def exact_gelu(values):
    return jax.nn.gelu(values, approximate=False)


def contract_last(first_op, second_op):
    return lax.dot_general(
        first_op, second_op, (((1,), (1,)), ((), ())), preferred_element_type=jnp.float32
    )


def contract_first(first_op, second_op):
    return lax.dot_general(
        first_op, second_op, (((0,), (0,)), ((), ())), preferred_element_type=jnp.float32
    )


def split_blocks(heads_arr, block_rows):
    batches, length, head_size = heads_arr.shape
    return heads_arr.reshape(batches, length // block_rows, block_rows, head_size).transpose(
        1, 0, 2, 3
    )


def join_blocks(block_array):
    block_count, batches, block_rows, head_size = block_array.shape
    return block_array.transpose(1, 0, 2, 3).reshape(batches, block_count * block_rows, head_size)


def block_scores(query_portion, key_head_tensor, key_valid, score_scale):
    scores = (
        jnp.einsum(
            "eix,evx->eiv", query_portion, key_head_tensor, preferred_element_type=jnp.float32
        )
        * score_scale
    )
    return jnp.where(key_valid[:, None, :], scores, NEG_FILL)


def attend(query_heads, key_head_tensor, value_head_tensor, key_valid, block_rows, score_scale):

    def one_block(query_portion):
        scores = block_scores(query_portion, key_head_tensor, key_valid, score_scale)
        row_max = jnp.max(scores, axis=-1, keepdims=True)
        exponent = jnp.exp(scores - row_max)
        row_total = jnp.sum(exponent, axis=-1, keepdims=True)
        softmax_reduced = (exponent / row_total).astype(jnp.bfloat16)
        mixture = jnp.einsum(
            "fwj,fjt->fwt", softmax_reduced, value_head_tensor, preferred_element_type=jnp.float32
        )
        return (mixture.astype(jnp.bfloat16), row_max, row_total)

    mixture, row_max, row_total = lax.map(one_block, split_blocks(query_heads, block_rows))
    return (join_blocks(mixture), row_max, row_total)


def attend_back(
    query_heads,
    key_head_tensor,
    value_head_tensor,
    grad_heads,
    row_max,
    row_total,
    key_valid,
    block_rows,
    score_scale,
):

    def one_block(running, block_in):
        key_grad, value_grad = running
        query_portion, gradient_portion, max_part, total_part = block_in
        scores = block_scores(query_portion, key_head_tensor, key_valid, score_scale)
        softmax = jnp.exp(scores - max_part) / total_part
        softmax_reduced = softmax.astype(jnp.bfloat16)
        soft_grad = jnp.einsum(
            "eix,evx->eiv", gradient_portion, value_head_tensor, preferred_element_type=jnp.float32
        )
        centre = jnp.sum(softmax * soft_grad, axis=-1, keepdims=True)
        score_gradient = (softmax * (soft_grad - centre)).astype(jnp.bfloat16)
        query_grad = (
            jnp.einsum(
                "fwj,fjt->fwt", score_gradient, key_head_tensor, preferred_element_type=jnp.float32
            )
            * score_scale
        )
        key_grad = (
            key_grad
            + jnp.einsum(
                "oxl,oxn->oln", score_gradient, query_portion, preferred_element_type=jnp.float32
            )
            * score_scale
        )
        value_grad = value_grad + jnp.einsum(
            "oxl,oxn->oln", softmax_reduced, gradient_portion, preferred_element_type=jnp.float32
        )
        return ((key_grad, value_grad), query_grad)

    zero_grads = jnp.zeros(key_head_tensor.shape, jnp.float32)
    block_inputs = (
        split_blocks(query_heads, block_rows),
        split_blocks(grad_heads, block_rows),
        row_max,
        row_total,
    )
    (key_grad, value_grad), query_grad = lax.scan(one_block, (zero_grads, zero_grads), block_inputs)
    return (join_blocks(query_grad), key_grad, value_grad)


def per_device(
    hidden_in,
    seq_lengths,
    w_query,
    b_query,
    w_key,
    w_value,
    b_value,
    w_out,
    b_out,
    norm1_gain,
    norm1_bias,
    w_inner,
    b_inner,
    w_outer,
    b_outer,
    norm2_gain,
    norm2_bias,
    out_grad,
):
    tensor_size = lax.axis_size("tensor")
    tensor_place = lax.axis_index("tensor")
    local_rows, feature_width = hidden_in.shape
    group_rows = local_rows * tensor_size
    seq_count = seq_lengths.shape[0]
    seq_len = group_rows // seq_count
    head_cols = w_query.shape[1]
    inner_cols = w_inner.shape[1]
    heads_here = head_cols // HEAD_DIM
    block_rows = min(512, seq_len)
    score_scale = HEAD_DIM ** (-0.5)
    local_start = tensor_place * local_rows
    row_index = lax.iota(jnp.int32, group_rows)
    seq_match = (row_index[:, None] // seq_len == lax.iota(jnp.int32, seq_count)[None, :]).astype(
        jnp.int32
    )
    row_limit = jnp.sum(seq_match * seq_lengths[None, :], axis=1)
    row_valid = row_index % seq_len < row_limit
    local_mask = lax.dynamic_slice_in_dim(row_valid, local_start, local_rows).astype(jnp.float32)[
        :, None
    ]
    key_valid = jnp.repeat(row_valid.reshape(seq_count, seq_len), heads_here, axis=0)

    def heads_of(matrix):
        shaped = matrix.reshape(seq_count, seq_len, heads_here, HEAD_DIM).transpose(0, 2, 1, 3)
        return shaped.reshape(seq_count * heads_here, seq_len, HEAD_DIM)

    def rows_of(matrix):
        shaped = matrix.reshape(seq_count, heads_here, seq_len, HEAD_DIM).transpose(0, 2, 1, 3)
        return shaped.reshape(group_rows, head_cols)

    full_query, full_key, full_value, full_out, full_inner, full_outer = (
        lax.all_gather(w_query, "dp", axis=0, tiled=True),
        lax.all_gather(w_key, "dp", axis=0, tiled=True),
        lax.all_gather(w_value, "dp", axis=0, tiled=True),
        lax.all_gather(w_out, "dp", axis=0, tiled=True),
        lax.all_gather(w_inner, "dp", axis=0, tiled=True),
        lax.all_gather(w_outer, "dp", axis=0, tiled=True),
    )
    joint_weight = jnp.concatenate((full_query, full_key, full_value), axis=1)
    query_bias = lax.dynamic_slice_in_dim(b_query, tensor_place * head_cols, head_cols)
    value_bias = lax.dynamic_slice_in_dim(b_value, tensor_place * head_cols, head_cols)
    inner_bias = lax.dynamic_slice_in_dim(b_inner, tensor_place * inner_cols, inner_cols)
    joint_bias = jnp.concatenate((query_bias, jnp.zeros((head_cols,), jnp.float32), value_bias))
    whole_in = lax.all_gather(hidden_in, "tensor", axis=0, tiled=True)
    joint_rows = (
        jnp.dot(whole_in, joint_weight, preferred_element_type=jnp.float32) + joint_bias
    ).astype(jnp.bfloat16)
    query_heads = heads_of(joint_rows[:, :head_cols])
    key_head_tensor = heads_of(joint_rows[:, head_cols : 2 * head_cols])
    value_head_tensor = heads_of(joint_rows[:, 2 * head_cols :])
    mixture_heads, row_max, row_total = attend(
        query_heads, key_head_tensor, value_head_tensor, key_valid, block_rows, score_scale
    )
    mixture = rows_of(mixture_heads)
    summed_out = lax.psum_scatter(
        contract_last(mixture, full_out).astype(jnp.bfloat16),
        "tensor",
        scatter_dimension=0,
        tiled=True,
    ).astype(jnp.float32)
    first_sum = hidden_in.astype(jnp.float32) + (summed_out + b_out)
    first_norm = layer_norm(first_sum, norm1_gain, norm1_bias)
    mid_whole = lax.all_gather(first_norm.astype(jnp.bfloat16), "tensor", axis=0, tiled=True)
    pre_act = jnp.dot(mid_whole, full_inner, preferred_element_type=jnp.float32) + inner_bias
    act_low = exact_gelu(pre_act).astype(jnp.bfloat16)
    second_sum = first_norm + (
        lax.psum_scatter(
            contract_last(act_low, full_outer).astype(jnp.bfloat16),
            "tensor",
            scatter_dimension=0,
            tiled=True,
        ).astype(jnp.float32)
        + b_outer
    )
    normed, norm2_back = jax.vjp(layer_norm, second_sum, norm2_gain, norm2_bias)
    layer_out = (normed * local_mask).astype(jnp.bfloat16)
    out_cot = out_grad.astype(jnp.float32) * local_mask
    dsecond, gain2_part, bias2_part = norm2_back(out_cot)
    dffn_low = dsecond.astype(jnp.bfloat16)
    outer_bias_part = jnp.sum(dffn_low, axis=0, dtype=jnp.float32)
    dffn_whole = lax.all_gather(dffn_low, "tensor", axis=0, tiled=True)
    grad_outer = contract_first(dffn_whole, act_low)
    dact = jnp.dot(dffn_whole, full_outer, preferred_element_type=jnp.float32)
    _, gelu_back = jax.vjp(exact_gelu, pre_act)
    dpre_low = gelu_back(dact)[0].astype(jnp.bfloat16)
    inner_bias_part = jnp.sum(dpre_low, axis=0, dtype=jnp.float32)
    grad_inner = contract_first(mid_whole, dpre_low)
    dfirst_norm = dsecond + lax.psum_scatter(
        contract_last(dpre_low, full_inner).astype(jnp.bfloat16),
        "tensor",
        scatter_dimension=0,
        tiled=True,
    ).astype(jnp.float32)
    _, norm1_back = jax.vjp(layer_norm, first_sum, norm1_gain, norm1_bias)
    dfirst, gain1_part, bias1_part = norm1_back(dfirst_norm)
    dattn_low = dfirst.astype(jnp.bfloat16)
    out_bias_part = jnp.sum(dattn_low, axis=0, dtype=jnp.float32)
    dattn_whole = lax.all_gather(dattn_low, "tensor", axis=0, tiled=True)
    grad_out_w = contract_first(dattn_whole, mixture)
    dmixture = jnp.dot(dattn_whole, full_out, preferred_element_type=jnp.float32).astype(
        jnp.bfloat16
    )
    dquery_heads, dkey_heads, dvalue_heads = attend_back(
        query_heads,
        key_head_tensor,
        value_head_tensor,
        heads_of(dmixture),
        row_max,
        row_total,
        key_valid,
        block_rows,
        score_scale,
    )
    djoint = jnp.concatenate(
        (rows_of(dquery_heads), rows_of(dkey_heads), rows_of(dvalue_heads)), axis=1
    ).astype(jnp.bfloat16)
    joint_bias_part = jnp.sum(djoint, axis=0, dtype=jnp.float32)
    grad_joint = contract_first(whole_in, djoint)
    grad_in = dfirst + lax.psum_scatter(
        contract_last(djoint, joint_weight).astype(jnp.bfloat16),
        "tensor",
        scatter_dimension=0,
        tiled=True,
    ).astype(jnp.float32)
    grad_query = grad_joint[:, :head_cols]
    grad_key = grad_joint[:, head_cols : 2 * head_cols]
    grad_value = grad_joint[:, 2 * head_cols :]
    shard_grads = tuple(
        (
            lax.psum_scatter(grad_query, "dp", scatter_dimension=0, tiled=True),
            lax.psum_scatter(grad_key, "dp", scatter_dimension=0, tiled=True),
            lax.psum_scatter(grad_value, "dp", scatter_dimension=0, tiled=True),
            lax.psum_scatter(grad_out_w, "dp", scatter_dimension=0, tiled=True),
            lax.psum_scatter(grad_inner, "dp", scatter_dimension=0, tiled=True),
            lax.psum_scatter(grad_outer, "dp", scatter_dimension=0, tiled=True),
        )
    )

    def placed(vector, total_len):
        return lax.dynamic_update_slice_in_dim(
            jnp.zeros((total_len,), jnp.float32), vector, tensor_place * vector.shape[0], 0
        )

    query_bias_part = placed(joint_bias_part[:head_cols], feature_width)
    value_bias_part = placed(joint_bias_part[2 * head_cols :], feature_width)
    hidden_bias_part = placed(inner_bias_part, b_inner.shape[0])
    vector_sums = lax.psum(
        (
            query_bias_part,
            value_bias_part,
            out_bias_part,
            gain1_part,
            bias1_part,
            hidden_bias_part,
            outer_bias_part,
            gain2_part,
            bias2_part,
        ),
        ("dp", "tensor"),
    )
    return (
        layer_out,
        grad_in,
        shard_grads[0],
        vector_sums[0],
        shard_grads[1],
        shard_grads[2],
        vector_sums[1],
        shard_grads[3],
        vector_sums[2],
        vector_sums[3],
        vector_sums[4],
        shard_grads[4],
        vector_sums[5],
        shard_grads[5],
        vector_sums[6],
        vector_sums[7],
        vector_sums[8],
    )


Z_SIZE = 4
MESH_IDS = pl.DeviceIdType.MESH


def flip(place, bit):
    return place + bit - 2 * place * bit


class Place:
    def __init__(self):
        self.dp = lax.axis_index("dp")
        self.t = lax.axis_index("tensor")
        self.z = self.dp // 2
        self.x = self.dp % 2
        self.y = self.t // 2
        self.c = self.t % 2

    def chip(self, dz, da, db):
        c = self.c
        z = lax.rem(self.z - dz + Z_SIZE, Z_SIZE)
        x = flip(self.x, da * c + db * (1 - c))
        y = flip(self.y, da * (1 - c) + db * c)
        return z * 2 + x, y

    def device(self, dz=0, da=0, db=0, other=False):
        dp, y = self.chip(dz, da, db)
        core = 1 - self.c if other else self.c
        return {"dp": dp, "tensor": y * 2 + core}


def block_of(ref, m, dp, t, rows):
    return ref.at[m, t, pl.ds(pl.multiple_of(dp * rows, rows), rows), :]


def peers_of(me):
    return [me.device(dz=k) for k in range(1, Z_SIZE)] + [me.device(da=1), me.device(db=1), me.device(other=True)]


def greet(me):
    for peer in peers_of(me):
        pl.semaphore_signal(pltpu.get_barrier_semaphore(), inc=1, device_id=peer, device_id_type=MESH_IDS)


def meet(me):
    pl.semaphore_wait(pltpu.get_barrier_semaphore(), len(peers_of(me)))


def remote(src, dst, send, recv, peer):
    return pltpu.make_async_remote_copy(
        src_ref=src, dst_ref=dst, send_sem=send, recv_sem=recv, device_id=peer, device_id_type=MESH_IDS
    )


def parse(steps):
    for step in steps:
        first, _, stop = step[3:].partition("-")
        for q in range(int(first or 0), int(stop or first or 0) + 1):
            yield step[0], int(step[1]), q


class Routes:
    def __init__(self, me):
        self.me = me
        self.half = me.z // 2
        self.far = 2 - self.half
        self.near = 2 * self.half + (1 - me.z % 2)
        self.mid = (me.z == 1) | (me.z == 2)

    def z_peer(self, z):
        return {"dp": z * 2 + self.me.x, "tensor": self.me.t}

    def dz_of(self, k):
        return lax.rem(k * self.half + (4 - k) * (1 - self.half), Z_SIZE)

    def back(self, z):
        return lax.rem(self.me.z - z + Z_SIZE, Z_SIZE)


class Gather(Routes):
    def __init__(self, me, modes, w, send_sem, recv_sem):
        super().__init__(me)
        self.modes, self.w = modes, w
        self.send_sem, self.recv_sem = send_sem, recv_sem
        self.rows = w.shape[2] // lax.axis_size("dp")

    def sem(self, m, send, recv):
        one = block_of(self.w, m, 0, 0, self.rows)
        return remote(one, one, self.send_sem.at[m, send], self.recv_sem.at[m, recv], self.me.device(db=1))

    def wait(self, m, slot):
        self.sem(m, slot, slot).wait_recv()

    def send(self, m, slot, dz, da, db, peer, leave=None):
        dp, y = self.me.chip(dz, da, db)
        dst = block_of(self.w, m, dp, y * 2 + self.me.c, self.rows)
        leave = slot if leave is None else leave
        remote(dst, dst, self.send_sem.at[m, leave], self.recv_sem.at[m, slot], peer).start()

    def z_slots(self, da):
        return [(4 * lax.rem(z - self.me.z + Z_SIZE, Z_SIZE) + 2 * da, z) for z in (self.far, self.near)]

    def z_send(self, m, da):
        for slot, z in self.z_slots(da):
            self.send(m, slot, 0, da, 0, self.z_peer(z))

    def own(self, m):
        return block_of(self.w, m, self.me.dp, self.me.t, self.rows)

    def place(self, m, q):
        if self.modes[m] == 0:
            return q % 4, q // 4
        return (0, q) if q < 2 else (1 + (q - 2) % 3, (q - 2) // 3)

    def pump(self, m, q):
        me = self.me
        k, da = self.place(m, q)
        dz = self.dz_of(k) if k else 0
        slot = 4 * dz + 2 * da
        self.wait(m, slot)
        if k in (1, 2) and (self.modes[m] == 1 or da == 0):

            @pl.when(self.mid)
            def _():
                there = lax.rem(self.near - me.z + dz + Z_SIZE, Z_SIZE)
                self.send(m, 4 * there + 2 * da, dz, da, 0, self.z_peer(self.near), leave=31 + 2 * da + k)

        if self.modes[m] == 0 and da == 0:
            self.send(m, 4 * dz + 2, dz, 0, 0, me.device(da=1))
        if self.modes[m] == 1 and k == 0:
            self.z_send(m, 1)
        self.send(m, slot + 1, dz, da, 0, me.device(db=1))
        self.send(m, 16 + slot, dz, da, 0, me.device(other=True))

    def last(self, m, q):
        k, da = self.place(m, q)
        dz = self.dz_of(k) if k else 0
        slot = 4 * dz + 2 * da + 1
        self.wait(m, slot)
        self.send(m, 16 + slot, dz, da, 1, self.me.device(other=True))

    def run(self, steps):
        me = self.me
        for op, m, q in parse(steps):
            if op == "A":
                self.send(m, 2, 0, 0, 0, me.device(da=1))
            elif op == "B":
                self.send(m, 1, 0, 0, 0, me.device(db=1))
                self.send(m, 16, 0, 0, 0, me.device(other=True))
            elif op == "y":
                self.z_send(m, 0)
            elif op == "p":
                self.pump(m, q)
            else:
                self.last(m, q)

    def collect(self, m, first=0, stop=4):
        @pl.loop(0, Z_SIZE)
        def _(dz):
            for s in range(first, stop):
                self.wait(m, 16 + 4 * dz + s)

    def drain(self, m):
        left = lambda s: self.sem(m, s, s).wait_send()
        for da in range(1 + self.modes[m]):
            for slot, _ in self.z_slots(da):
                left(slot)

            @pl.when(self.mid)
            def _():
                left(32 + 2 * da)
                left(33 + 2 * da)

        for dz in range(1 if self.modes[m] else Z_SIZE):
            left(4 * dz + 2)

        @pl.loop(0, 8)
        def _(s):
            left(2 * s + 1)

        @pl.loop(16, 32)
        def _(s):
            left(s)


class Scatter(Routes):
    def __init__(self, me, modes, w, w0_grad, out_ref, core_buf, b_buf, t_buf, send_sem, recv_sem):
        super().__init__(me)
        self.out_ref = out_ref
        self.modes, self.w, self.w0_grad = modes, w, w0_grad
        self.core_buf, self.b_buf, self.t_buf = core_buf, b_buf, t_buf
        self.send_sem, self.recv_sem = send_sem, recv_sem
        self.rows = b_buf.shape[2]

    def order(self, i):
        me = self.me
        return flip(me.y, 1 - i // 2) * 2 + flip(1 - me.c, i % 2)

    def part(self, m, dz, da, db, core):
        dp, y = self.me.chip(dz, da, db)
        if m == 0:
            return self.w0_grad.at[y * 2 + core, pl.ds(pl.multiple_of(dp * self.rows, self.rows), self.rows), :]
        return block_of(self.w, m, dp, y * 2 + core, self.rows)

    def sem(self, m, send, recv):
        one = self.b_buf.at[m, 0]
        return remote(one, one, self.send_sem.at[m, send], self.recv_sem.at[m, recv], self.me.device(db=1))

    def wait(self, m, slot):
        self.sem(m, slot, slot).wait_recv()

    def go(self, m, slot, src, dst, peer, leave=None):
        leave = slot if leave is None else leave
        remote(src, dst, self.send_sem.at[m, leave], self.recv_sem.at[m, slot], peer).start()

    def from_core(self, dz, da, db):
        return 4 * dz + 2 * db + da

    def ready(self, m, i):
        me = self.me
        c = me.c
        side = 1 - i // 2

        def where(s):
            other = 1 - s // 4
            return self.dz_of(3 - s % 4), side * (1 - c) + other * c, other * (1 - c) + side * c

        @pl.when(i % 2 == 0)
        def _():
            @pl.loop(0, 8)
            def _(s):
                dz, da, db = where(s)
                slot = 4 * dz + 2 * da + db
                self.go(m, slot, self.part(m, dz, da, db, 1 - c), self.core_buf.at[m, slot], me.device(other=True))

        @pl.when(i % 2 == 1)
        def _():
            @pl.loop(0, 8)
            def _(s):
                dz, da, db = where(s)
                slot = self.from_core(dz, da, db)
                self.wait(m, slot)
                self.core_buf[m, slot] = self.part(m, dz, da, db, c)[...] + self.core_buf[m, slot]

                @pl.when(db == 1)
                def _():
                    place = 2 * dz + da
                    self.go(m, 16 + place, self.core_buf.at[m, slot], self.b_buf.at[m, place], me.device(db=1))

    def way(self, m, da, j):
        return 2 * da + j if self.modes[m] else 4 + j

    def end(self, m, da, far):
        return (4 + 2 * da if self.modes[m] else 6) + far

    def z_out(self, m, dz, da, src):
        owner = lax.rem(self.me.z - dz + Z_SIZE, Z_SIZE)
        is_near = owner == self.near

        @pl.when(is_near)
        def _():
            j = self.end(m, da, 0)
            self.go(m, 24 + j, src, self.t_buf.at[m, j], self.z_peer(self.near))

        @pl.when(jnp.logical_not(is_near | self.mid) & (dz != 0))
        def _():
            j = self.way(m, da, 0) + (owner != self.far).astype(jnp.int32)
            self.go(m, 24 + j, src, self.t_buf.at[m, j], self.z_peer(self.near))

    def source(self, m, dz, da):
        return self.b_buf.at[m, 2 * dz + da] if self.modes[m] else self.t_buf.at[m, dz]

    def b_step(self, m, k, da):
        dz = self.dz_of(k)
        place = 2 * dz + da
        self.wait(m, 16 + place)
        self.b_buf[m, place] = self.b_buf[m, place] + self.core_buf[m, self.from_core(dz, da, 0)]
        if self.modes[m] == 1:
            self.z_out(m, dz, da, self.b_buf.at[m, place])
        elif da == 1:
            self.go(m, 24 + dz, self.b_buf.at[m, place], self.t_buf.at[m, dz], self.me.device(da=1))

    def a_step(self, m, k):
        dz = self.dz_of(k)
        self.wait(m, 24 + dz)
        self.t_buf[m, dz] = self.t_buf[m, dz] + self.b_buf[m, 2 * dz]
        self.z_out(m, dz, 0, self.t_buf.at[m, dz])

    def z_step(self, m, da, j):
        @pl.when(self.mid)
        def _():
            owner = flip(self.far % 2, j) + 2 * (1 - self.half)
            way, end = self.way(m, da, j), self.end(m, da, 1)
            self.wait(m, 24 + way)
            self.t_buf[m, way] = self.t_buf[m, way] + self.source(m, self.back(owner), da)[...]
            self.go(m, 24 + end, self.t_buf.at[m, way], self.t_buf.at[m, end], self.z_peer(owner), leave=24 + way)

    def last_step(self, m):
        near, far = self.end(m, 1, 0), self.end(m, 1, 1)
        self.wait(m, 24 + near)
        self.wait(m, 24 + far)
        self.t_buf[m, near] = self.t_buf[m, near] + self.t_buf[m, far] + self.b_buf[m, 1]
        self.go(m, 32, self.t_buf.at[m, near], self.t_buf.at[m, 8], self.me.device(da=1))

    def run(self, steps):
        for op, m, q in parse(steps):
            if op == "b":
                self.b_step(m, 3 - q // 2, 1 - q % 2)
            elif op == "c":
                self.b_step(m, 3 - q % 4, 1 - q // 4)
            elif op == "a":
                self.a_step(m, 3 - q)
            elif op == "z":
                self.z_step(m, (1 - q // 2) * self.modes[m], 1 - q % 2)
            elif op == "e":
                self.last_step(m)
            else:
                self.finish(m)

    def finish(self, m):
        wide = lambda ref: ref[...].astype(jnp.float32)
        near = self.end(m, 0, 0)
        self.wait(m, 24 + near)
        self.wait(m, 25 + near)
        total = wide(self.source(m, 0, 0)) + wide(self.t_buf.at[m, near]) + wide(self.t_buf.at[m, near + 1])
        if self.modes[m] == 1:
            self.wait(m, 32)
            total = total + wide(self.t_buf.at[m, 8])
        self.out_ref[m] = total

    def drain(self):
        for m in range(3):
            left = lambda s: self.sem(m, s, s).wait_send()

            @pl.loop(0, 24)
            def _(s):
                left(s)

            for da in range(1 + self.modes[m]):
                for j in (self.way(m, da, 0), self.way(m, da, 1), self.end(m, da, 0)):
                    left(24 + j)
            for j in (8,) if self.modes[m] else range(Z_SIZE):
                left(24 + j)


class VectorSum:
    def __init__(self, me, buf, zbuf, send_sem, recv_sem):
        self.me, self.buf, self.zbuf, self.send_sem, self.recv_sem = me, buf, zbuf, send_sem, recv_sem

    def copy(self, step, src, dst, peer):
        return remote(src, dst, self.send_sem.at[step], self.recv_sem.at[step], peer)

    def peer(self, step):
        me = self.me
        if step == 0:
            return me.device(other=True)
        dx, dy = ((1, 0), (0, 1))[step - 1]
        return {"dp": me.z * 2 + flip(me.x, dx), "tensor": 2 * flip(me.y, dy) + me.c}

    def pair(self, step):
        return self.copy(step, self.buf.at[2 * step], self.buf.at[2 * step + 1], self.peer(step))

    def start(self, value):
        self.buf[0] = value
        self.pair(0).start()

    def advance(self, step):
        self.pair(step).wait()
        self.buf[2 * step + 2] = self.buf[2 * step] + self.buf[2 * step + 1]
        if step < 2:
            self.pair(step + 1).start()
        else:
            self.zbuf[self.me.z] = self.buf[6]
            for k in range(1, Z_SIZE):
                self.z_copy(k).start()

    def z_copy(self, k):
        return self.copy(2 + k, self.buf.at[6], self.zbuf.at[self.me.z], self.me.device(dz=k))

    def result(self):
        for k in range(1, Z_SIZE):
            self.z_copy(k).wait()
        return (self.zbuf[0] + self.zbuf[1]) + (self.zbuf[2] + self.zbuf[3])


def dot_nn(a, b):
    return lax.dot_general(a, b, (((1,), (0,)), ((), ())), preferred_element_type=jnp.float32)


def dot_nt(a, b):
    return lax.dot_general(a, b, (((1,), (1,)), ((), ())), preferred_element_type=jnp.float32)


def dot_tn(a, b):
    return lax.dot_general(a, b, (((0,), (0,)), ((), ())), preferred_element_type=jnp.float32)


def low(a):
    return a.astype(jnp.bfloat16)


def row_mean(a):
    return jnp.mean(a, axis=-1, keepdims=True)


def normalise(r):
    centre = r - row_mean(r)
    inverse = lax.rsqrt(row_mean(centre * centre) + NORM_EPS)
    return centre * inverse, inverse


def norm_back(g, z, inverse):
    return (g - row_mean(g) - z * row_mean(g * z)) * inverse


def gelu_pair(u):
    cdf = 0.5 + 0.5 * lax.erf(u * (0.5**0.5))
    density = jnp.exp(-0.5 * u * u) * ((0.5 / jnp.pi) ** 0.5)
    return u * cdf, cdf + u * density


V_BQ, V_BV, V_BO, V_G1, V_B1, V_BF, V_G2, V_B2, V_BI = range(9)
TILE = 64


class Layer:
    def __init__(self, **refs):
        self.__dict__.update(refs)
        self.rows, self.width = self.x.shape
        self.n_t = self.w.shape[1]
        self.cols = self.width // self.n_t
        self.heads = self.cols // HEAD_DIM
        self.ocol = (3 * self.cols) // 128 * 128

    def tiles(self, body):
        @pl.loop(0, self.rows // TILE)
        def _(i):
            body(pl.ds(pl.multiple_of(i * TILE, TILE), TILE))

    def project(self, t):
        lane = lax.broadcasted_iota(jnp.int32, (1, self.width), 1)
        out = dot_nn(self.x[...], self.w[0, t]) + self.qkv_bias[t]
        self.qkv[t] = low(jnp.where(lane < 3 * self.cols, out, 0.0))

    def piece(self, t, which, j):
        first = which * self.cols + j * HEAD_DIM
        return self.qkv.at[t, :, first : first + HEAD_DIM]

    def attend(self, t, valid, between):
        self.att[t, :, : HEAD_DIM] = jnp.zeros((self.rows, HEAD_DIM), jnp.bfloat16)
        for j in range(self.heads):
            q, k, v = (self.piece(t, i, j)[...] for i in range(3))
            s = dot_nt(k, q * jnp.bfloat16(HEAD_DIM**-0.5))
            s = jnp.where(valid, s, NEG_FILL)
            e = jnp.exp(s - jnp.max(s, axis=0, keepdims=True))
            p = low(e * (1.0 / jnp.sum(e, axis=0, keepdims=True)))
            self.p[t * self.heads + j] = p
            mix = dot_tn(v, p)
            first = 3 * self.cols - self.ocol + j * HEAD_DIM
            self.att[t, :, first : first + HEAD_DIM] = low(mix.T)
            between(j)

    def out_project(self, t):
        self.acc[...] += dot_nt(self.att[t], self.w[0, t, :, self.ocol :])

    def start_residual(self):
        self.acc[...] = self.x[...].astype(jnp.float32) + self.vec[2:3, :]

    def first_norm(self):
        def body(r):
            z, inverse = normalise(self.acc[r, :])
            self.z1[r, :] = z
            self.inv1[r, :] = jnp.broadcast_to(inverse, (TILE, 128))
            h1 = z * self.vec[3:4, :] + self.vec[4:5, :]
            self.h1b[r, :] = low(h1)
            self.acc[r, :] = h1 + self.vec[0:1, :]

        self.tiles(body)

    def inner(self, t):
        @pl.loop(0, self.rows // 128)
        def _(i):
            r = pl.ds(pl.multiple_of(i * 128, 128), 128)
            pre = dot_nn(self.h1b[r, :], self.w[1, t]) + self.inner_bias[t]
            act, slope = gelu_pair(pre)
            self.act[t, r, :] = low(act)
            self.slope[t, r, :] = low(slope)

    def outer(self, t):
        self.acc[...] += dot_nt(self.act[t], self.w[2, t])

    def second_norm(self, length):
        self.sums[...] = jnp.zeros_like(self.sums)

        def body(r):
            z, inverse = normalise(self.acc[r, :])
            place = r.start + lax.broadcasted_iota(jnp.int32, (TILE, 1), 0)
            mask = (place < length).astype(jnp.float32)
            gain = self.vec[5:6, :]
            self.y[r, :] = low((z * gain + self.vec[6:7, :]) * mask)
            dy = self.og[r, :].astype(jnp.float32) * mask
            dr2 = norm_back(dy * gain, z, inverse)
            self.acc[r, :] = dr2
            df = low(dr2)
            self.df[r, :] = df
            self.sums[V_G2] += fold(dy * z)
            self.sums[V_B2] += fold(dy)
            self.sums[V_BF] += fold(df.astype(jnp.float32))

        self.tiles(body)

    def outer_back(self, t):
        half = self.rows // 2
        for i in range(2):
            r = slice(i * half, (i + 1) * half)
            d = dot_nn(self.df[r, :], self.w[2, t])
            self.slope[t, r, :] = low(d * self.slope[t, r, :].astype(jnp.float32))
        self.w[2, t] = low(dot_nn(self.df_t[...], self.act[t]))
        self.sums[V_BI + t] = self.column_sums(self.slope[t])

    def column_sums(self, a):
        first = lax.broadcasted_iota(jnp.int32, (16, self.rows), 0) == 0
        return dot_nn(low(first.astype(jnp.float32)), a)[:8]

    def inner_back(self, t):
        self.acc[...] += dot_nt(self.slope[t], self.w[1, t])
        self.w[1, t] = low(dot_nn(self.h1b_t[...], self.slope[t]))

    def first_norm_back(self):
        def body(r):
            z = self.z1[r, :]
            dh1 = self.acc[r, :]
            self.sums[V_G1] += fold(dh1 * z)
            self.sums[V_B1] += fold(dh1)
            dr1 = norm_back(dh1 * self.vec[3:4, :], z, self.inv1[r, :1])
            self.acc[r, :] = dr1
            dob = low(dr1)
            self.df[r, :] = dob
            self.sums[V_BO] += fold(dob.astype(jnp.float32))

        self.tiles(body)

    def attend_back(self, t, between):
        scale = HEAD_DIM**-0.5
        self.datt[...] = low(dot_nn(self.df[...], self.w[0, t, :, self.ocol :]))
        for j in range(self.heads):
            first = 3 * self.cols - self.ocol + j * HEAD_DIM
            d = self.datt[:, first : first + HEAD_DIM]
            q, k, v = (self.piece(t, i, j)[...] for i in range(3))
            p = self.p[t * self.heads + j]
            dp = dot_nt(v, d)
            pf = p.astype(jnp.float32)
            delta = jnp.sum(pf * dp, axis=0, keepdims=True)
            ds = low(pf * (dp - delta))
            self.piece(t, 2, j)[...] = low(dot_nn(p, d))
            self.piece(t, 1, j)[...] = low(dot_nn(ds, q) * scale)
            self.piece(t, 0, j)[...] = low((dot_tn(k, ds) * scale).T)
            between(j)

    def head_sums(self, t):
        self.sums[V_BI + self.n_t + t] = self.column_sums(self.qkv[t])

    def project_grad(self, t):
        self.w0_grad[t] = low(dot_nn(self.x_t[...], self.qkv[t]))
        out = self.w0_grad.at[t, :, self.ocol :]
        out[...] = low(out[...].astype(jnp.float32) + dot_nn(self.df_t[...], self.att[t]))

    def project_back(self, t):
        self.acc[...] += dot_nt(self.qkv[t], self.w[0, t])

    def transpose(self, src, dst):
        dst[...] = src[...].T


def fold(a):
    return jnp.sum(a.reshape(a.shape[0] // 8, 8, a.shape[1]), axis=0)


GATHER_MODES = (0, 1, 1)
SCATTER_MODES = (0, 1, 1)
GATHER_MODES = (0, 1, 1)
SCATTER_MODES = (0, 1, 1)
GATHER = {
    "first": ("y0:0", "A0:0", "A1:0", "p0:4", "B1:0", "y2:0", "B0:0", "l0:4", "p0:1"),
    "start": ("p0:2", "p1:1", "y1:0", "l0:0", "p0:3", "p0:6", "p0:5", "l0:2", "l0:1", "l1:1", "p0:7", "p2:2", "p1:2", "p1:5",
        "l0:5", "B2:0", "l0:6", "A2:0", "l0:3", "l0:7"),
    "attend": (),
    "heads": {4: ("l2:0", "p2:3", "p2:1"), 8: ("p1:4", "p1:7", "l1:0", "l1:5"), 10: ("l2:3",), 11: ("l1:4", "l2:2", "l1:6",
        "p2:4", "l1:3", "l1:2")},
    "out": {0: ("p1:6", "p1:3"), 3: ("p2:5", "l1:7")},
    "norm": (),
    "ffn": ("p2:6",),
    "inner": {1: ("p2:7", "l2:6", "l2:1", "l2:5", "l2:4"), 3: ("l2:7",)},
    "outer": {},
    "late": (),
}
SCATTER = {
    "outer": {3: ("b2:0",)},
    "inner": {0: ("b2:2",), 1: ("z2:0",), 2: ("b2:3", "b2:1", "b2:5")},
    "norm": ("b2:4", "b1:2", "b2:7"),
    "heads": {2: ("z2:1",), 4: ("z2:2-3",), 7: ("z1:1", "b1:6"), 8: ("b1:1", "z1:0")},
    "grad": {0: ("b1:0", "b1:4"), 1: ("b1:3",), 3: ("b1:5", "z1:2", "b0:0")},
    "last": (("z1:3", "b0:2"), ("b0:4", "b0:1"), ("a0:0", "b1:7", "b2:6", "e2:0", "e1:0", "b0:3", "b0:6", "a0:1", "b0:5",
        "z0:0", "b0:7"), ("a0:2", "z0:1", "F1:0", "F2:0", "a0:3", "F0:0")),
}


def step_kernel(
    length_ref, x_in, og_in, wq, wk, wv, wo, w_inner, w_outer, b_outer, b_value, b_out, gain1, bias1, gain2, bias2, b_query, b_inner,
    y_out, acc_out, shards_out, vout_ref,
    x_ref, og_ref, parts, vec_ref, qkv_bias, inner_bias,
    w, sums, qkv, p, att, z1, inv1, h1b, ffn, df, datt, x_t, h1b_t, df_t, y_ref, acc_ref, out_ref,
    core_buf, b_buf, t_buf, vec_buf, vec_z,
    load_sem, store_sem, gather_send, gather_recv, send_sem, recv_sem, vec_send, vec_recv,
):
    me = Place()
    rows, width = x_ref.shape
    act, slope, w0_grad = ffn.at[:, :rows], ffn.at[:, rows:], ffn.at[:, :width]
    gather = Gather(me, GATHER_MODES, w, gather_send, gather_recv)
    scatter = Scatter(me, SCATTER_MODES, w, w0_grad, out_ref, core_buf, b_buf, t_buf, send_sem, recv_sem)
    small = VectorSum(me, vec_buf, vec_z, vec_send, vec_recv)
    a = Layer(
        x=x_ref, og=og_ref, w=w, w0_grad=w0_grad, qkv_bias=qkv_bias, inner_bias=inner_bias, vec=vec_ref, y=y_ref, acc=acc_ref, sums=sums,
        qkv=qkv, p=p, att=att, z1=z1, inv1=inv1, h1b=h1b, act=act, slope=slope, df=df, datt=datt, x_t=x_t, h1b_t=h1b_t, df_t=df_t,
    )
    vectors = (b_outer, b_value, b_out, gain1, bias1, gain2, bias2, b_query)
    pairs = [(ref, parts.at[i]) for i, ref in enumerate((wq, wk, wv, wo))]
    pairs += [(w_inner, gather.own(1)), (w_outer, gather.own(2)), (x_in, x_ref), (b_inner, inner_bias)]
    pairs += [(ref, vec_ref.at[i]) for i, ref in enumerate(vectors)] + [(og_in, og_ref)]
    loads = [pltpu.make_async_copy(src, dst, load_sem.at[i]) for i, (src, dst) in enumerate(pairs)]
    for load in loads:
        load.start()

    def at(run, slots, i):
        for n, steps in slots.items():

            @pl.when(i == n)
            def _():
                run(steps)

    def heads(run, slots, i, j):
        at(run, {n // a.heads: steps for n, steps in slots.items() if n % a.heads == j}, i)

    greet(me)
    for load in loads[:6]:
        load.wait()
    packed = gather.own(0)
    for i in range(4):
        packed[:, i * a.cols : (i + 1) * a.cols] = parts[i]
    meet(me)
    gather.run(GATHER["first"])
    for load in loads[6:]:
        load.wait()
    for t in range(a.n_t):
        here = slice(t * a.cols, (t + 1) * a.cols)
        qkv_bias[t] = jnp.zeros((1, width), jnp.float32)
        qkv_bias[t, :, : a.cols] = vec_ref[7:8, here]
        qkv_bias[t, :, 2 * a.cols : 3 * a.cols] = vec_ref[1:2, here]
    length = length_ref[me.t]
    valid = lax.broadcasted_iota(jnp.int32, (a.rows, 1), 0) < length
    a.transpose(a.x, a.x_t)
    a.start_residual()
    gather.run(GATHER["start"])
    gather.collect(0)
    gather.run(GATHER["attend"])

    @pl.loop(0, a.n_t)
    def _(t):
        a.project(t)
        a.attend(t, valid, lambda j: heads(gather.run, GATHER["heads"], t, j))
        a.out_project(t)
        at(gather.run, GATHER["out"], t)

    a.first_norm()
    a.transpose(a.h1b, a.h1b_t)
    gather.run(GATHER["norm"])
    gather.collect(1)
    gather.run(GATHER["ffn"])

    @pl.loop(0, a.n_t)
    def _(t):
        a.inner(t)
        at(gather.run, GATHER["inner"], t)

    gather.collect(2, 0, 3)
    gather.run(GATHER["late"])

    @pl.loop(0, 2)
    def _(core):
        a.outer(2 * me.y + core)
        at(gather.run, GATHER["outer"], core)

    gather.collect(2, 3, 4)

    @pl.loop(0, 2)
    def _(core):
        a.outer(2 * (1 - me.y) + core)

    a.second_norm(length)
    a.transpose(a.df, a.df_t)
    stores = [(y_ref, y_out), (acc_ref, acc_out)] + [(out_ref.at[m], shards_out.at[m]) for m in range(3)]
    stores = [pltpu.make_async_copy(src, dst, store_sem.at[i]) for i, (src, dst) in enumerate(stores)]
    stores[0].start()
    gather.drain(2)

    @pl.loop(0, a.n_t)
    def _(i):
        a.outer_back(scatter.order(i))
        scatter.ready(2, i)
        at(scatter.run, SCATTER["outer"], i)

    gather.drain(1)

    @pl.loop(0, a.n_t)
    def _(i):
        a.inner_back(scatter.order(i))
        scatter.ready(1, i)
        at(scatter.run, SCATTER["inner"], i)

    a.first_norm_back()
    a.transpose(a.df, a.df_t)
    scatter.run(SCATTER["norm"])

    @pl.loop(0, a.n_t)
    def _(i):
        t = scatter.order(i)
        a.attend_back(t, lambda j: heads(scatter.run, SCATTER["heads"], i, j))
        a.head_sums(t)

        @pl.when(i == a.n_t - 1)
        def _():
            small.start(jnp.sum(sums[...], axis=1))

        a.project_grad(t)

        @pl.when(i == a.n_t - 1)
        def _():
            small.advance(0)

        scatter.ready(0, i)
        at(scatter.run, SCATTER["grad"], i)

    for t, steps in enumerate(SCATTER["last"]):
        a.project_back(t)
        if t == 1:
            small.advance(1)
        if t == 2:
            scatter.run(steps[:3])
            small.advance(2)
            steps = steps[3:]
        if t == a.n_t - 1:
            scatter.run(steps[:-1])
            for store in (stores[1], stores[3], stores[4]):
                store.start()
            steps = steps[-1:]
        scatter.run(steps)
    vout_ref[...] = small.result()
    stores[2].start()
    gather.drain(0)
    scatter.drain()
    for store in stores:
        store.wait()


def step(seq_lengths, x, og, weights, vectors, b_inner, n_t):
    rows, width = x.shape
    cols = width // n_t
    heads = width // HEAD_DIM
    owidth = width - (3 * cols) // 128 * 128
    shard = weights[0].shape[0]
    bf, f32 = jnp.bfloat16, jnp.float32
    vmem, anywhere = pl.BlockSpec(memory_space=pltpu.VMEM), pl.BlockSpec(memory_space=pl.ANY)
    n_v = V_BI + 2 * n_t
    n_w = shard * lax.axis_size("dp")
    buf = lambda n: pltpu.VMEM((3, n, shard, width), bf)
    dma = pltpu.SemaphoreType.DMA
    n_loads = 3 + len(weights) + len(vectors)
    return pl.pallas_call(
        step_kernel,
        out_shape=(
            jax.ShapeDtypeStruct((rows, width), bf),
            jax.ShapeDtypeStruct((rows, width), f32),
            jax.ShapeDtypeStruct((3, shard, width), f32),
            jax.ShapeDtypeStruct((n_v, width), f32),
        ),
        in_specs=[pl.BlockSpec(memory_space=pltpu.SMEM)] + [anywhere] * n_loads,
        out_specs=[anywhere] * 3 + [vmem],
        scratch_shapes=[
            pltpu.VMEM((rows, width), bf),
            pltpu.VMEM((rows, width), bf),
            pltpu.VMEM((4, shard, cols), bf),
            pltpu.VMEM((len(vectors), width), f32),
            pltpu.VMEM((n_t, 1, width), f32),
            pltpu.VMEM((n_t, 1, width), f32),
            pltpu.VMEM((3, n_t, n_w, width), bf),
            pltpu.VMEM((n_v, 8, width), f32),
            pltpu.VMEM((n_t, rows, width), bf),
            pltpu.VMEM((heads, rows, rows), bf),
            pltpu.VMEM((n_t, rows, owidth), bf),
            pltpu.VMEM((rows, width), f32),
            pltpu.VMEM((rows, 128), f32),
            pltpu.VMEM((rows, width), bf),
            pltpu.VMEM((n_t, max(2 * rows, width), width), bf),
            pltpu.VMEM((rows, width), bf),
            pltpu.VMEM((rows, owidth), bf),
            pltpu.VMEM((width, rows), bf),
            pltpu.VMEM((width, rows), bf),
            pltpu.VMEM((width, rows), bf),
            pltpu.VMEM((rows, width), bf),
            pltpu.VMEM((rows, width), f32),
            pltpu.VMEM((3, shard, width), f32),
            buf(16),
            buf(8),
            buf(9),
            pltpu.VMEM((7, n_v, width), f32),
            pltpu.VMEM((Z_SIZE, n_v, width), f32),
            dma((n_loads,)),
            dma((5,)),
            dma((3, 36)),
            dma((3, 36)),
            dma((3, 33)),
            dma((3, 33)),
            dma((6,)),
            dma((6,)),
        ],
        compiler_params=pltpu.CompilerParams(collective_id=0, has_side_effects=True, vmem_limit_bytes=63 * 2**20),
    )(seq_lengths, x, og, *weights, *vectors, b_inner)


def place_kernel(n_t, y_in, gin_in, shards_in, sums_in, *refs):
    y, gin, gq, gk, gv, go, gi, gf, bq, bv, bo, g1, b1, bi, bf, g2, b2, y_buf, gin_buf, shards, sums, parts, heads, sems = refs
    cols = gq.shape[1]
    started = []

    def copy(src, dst):
        started.append(pltpu.make_async_copy(src, dst, sems.at[len(started)]))
        started[-1].start()
        return started[-1]

    pairs = [(sums_in, sums), (shards_in, shards), (gin_in, gin_buf), (y_in, y_buf)]
    loads = [copy(src, dst) for src, dst in pairs]
    loads[0].wait()
    for row, ref in ((V_BO, bo), (V_G1, g1), (V_B1, b1), (V_BF, bf), (V_G2, g2), (V_B2, b2)):
        copy(sums.at[row], ref)
    for t in range(n_t):
        copy(sums.at[V_BI + t], bi.at[t, 0])
        row = sums[V_BI + n_t + t : V_BI + n_t + t + 1, :]
        heads[0:1, t * cols : (t + 1) * cols] = row[:, :cols]
        heads[1:2, t * cols : (t + 1) * cols] = row[:, 2 * cols : 3 * cols]
    loads[1].wait()
    copy(shards.at[1], gi)
    copy(shards.at[2], gf)
    for i in range(4):
        parts[i] = shards[0, :, i * cols : (i + 1) * cols]
    copy(heads.at[0], bq)
    copy(heads.at[1], bv)
    loads[2].wait()
    copy(gin_buf, gin)
    for i, ref in enumerate((gq, gk, gv, go)):
        copy(parts.at[i], ref)
    loads[3].wait()
    copy(y_buf, y)
    for done in started[len(loads) :]:
        done.wait()


def place(y, gin, shards, sums, n_t):
    shard, width = shards.shape[1:]
    cols = width // n_t
    f32 = jnp.float32
    anywhere = pl.BlockSpec(memory_space=pl.ANY)
    row = jax.ShapeDtypeStruct((width,), f32)
    return pl.pallas_call(
        functools.partial(place_kernel, n_t),
        out_shape=(
            [jax.ShapeDtypeStruct(y.shape, y.dtype), jax.ShapeDtypeStruct(gin.shape, f32)]
            + [jax.ShapeDtypeStruct((shard, cols), f32)] * 4
            + [jax.ShapeDtypeStruct((shard, width), f32)] * 2
            + [row] * 5
            + [jax.ShapeDtypeStruct((n_t, 1, width), f32)]
            + [row] * 3
        ),
        in_specs=[anywhere] * 4,
        out_specs=[anywhere] * 17,
        scratch_shapes=[
            pltpu.VMEM(y.shape, y.dtype),
            pltpu.VMEM(gin.shape, f32),
            pltpu.VMEM(shards.shape, f32),
            pltpu.VMEM(sums.shape, f32),
            pltpu.VMEM((4, shard, cols), f32),
            pltpu.VMEM((8, width), f32),
            pltpu.SemaphoreType.DMA((20 + n_t,)),
        ],
    )(y, gin, shards, sums)


def data_parallel(
    hidden_in, seq_lengths, w_query, b_query, w_key, w_value, b_value, w_out, b_out, norm1_gain, norm1_bias,
    w_inner, b_inner, w_outer, b_outer, norm2_gain, norm2_bias, out_grad,
):
    n_t = lax.axis_size("tensor")
    width = hidden_in.shape[1]
    vectors = (b_outer, b_value, b_out, norm1_gain, norm1_bias, norm2_gain, norm2_bias, b_query)
    weights = (w_query, w_key, w_value, w_out, w_inner, w_outer)
    done = step(seq_lengths, hidden_in, out_grad, weights, vectors, b_inner.reshape(n_t, 1, width), n_t)
    y, gin, gq, gk, gv, go, gi, gf, *small = place(*done, n_t)
    bq, bv, bo, g1, b1, bi, bf, g2, b2 = small
    return y, gin, gq, bq, gk, gv, bv, go, bo, g1, b1, gi, bi.reshape(-1), gf, bf, g2, b2


def solution(mesh):
    in_specs = (
        P(("dp", "tensor"), None),
        P("dp"),
        P("dp", "tensor"),
        P(),
        P("dp", "tensor"),
        P("dp", "tensor"),
        P(),
        P("dp", "tensor"),
        P(),
        P(),
        P(),
        P("dp", "tensor"),
        P(),
        P("dp", "tensor"),
        P(),
        P(),
        P(),
        P(("dp", "tensor"), None),
    )
    out_specs = (
        P(("dp", "tensor"), None),
        P(("dp", "tensor"), None),
        P("dp", "tensor"),
        P(),
        P("dp", "tensor"),
        P("dp", "tensor"),
        P(),
        P("dp", "tensor"),
        P(),
        P(),
        P(),
        P("dp", "tensor"),
        P(),
        P("dp", "tensor"),
        P(),
        P(),
        P(),
    )
    small = mesh.shape["dp"] == 2 * Z_SIZE and mesh.shape["tensor"] == 4
    return jax.shard_map(
        data_parallel if small else per_device, mesh=mesh, in_specs=in_specs, out_specs=out_specs, check_vma=False
    )
```
